32 devices in a mesh: dp: 4 (over y, core), blk: 8 (over z, x).
Axes of the slice: x: 2, y: 2, z: 4, core: 2. Of those that a mesh axis runs over, the one named last changes fastest.
Arguments:
- tokens: bfloat16 [4096, 768], P(('dp', 'blk')), may hold values from -6 to 6
- w_qkv: bfloat16 [768, 2304], P(('dp', 'blk')), may hold values from -0.108974863 to 0.108974863
- qv_bias: bfloat16 [2, 768], P(None, ('dp', 'blk')), may hold values from -3 to 3
- w_out: bfloat16 [768, 768], P(('dp', 'blk')), may hold values from -6 to 6
- out_bias: bfloat16 [768], P(('dp', 'blk')), may hold values from -3 to 3
- norm_gain: bfloat16 [2, 768], P(None, ('dp', 'blk')), may hold values from 0.5 to 1.5
- norm_bias: bfloat16 [2, 768], P(None, ('dp', 'blk')), may hold values from -3 to 3
- w_up: bfloat16 [768, 3072], P(('dp', 'blk')), may hold values from -0.21875 to 0.21875
- up_bias: bfloat16 [3072], P(('dp', 'blk')), may hold values from -3 to 3
- w_down: bfloat16 [3072, 768], P(('dp', 'blk')), may hold values from -0.109375 to 0.109375
- down_bias: bfloat16 [768], P(('dp', 'blk')), may hold values from -3 to 3
- cotangent: bfloat16 [4096, 768], P(('dp', 'blk')), may hold values from -6 to 6
Outputs:
- output: bfloat16 [4096, 768], P(('dp', 'blk'))
- d_tokens: float32 [4096, 768], P(('dp', 'blk'))
- d_w_qkv: float32 [768, 2304], P(('dp', 'blk'))
- d_qv_bias: float32 [2, 768], P(None, ('dp', 'blk'))
- d_w_out: float32 [768, 768], P(('dp', 'blk'))
- d_out_bias: float32 [768], P(('dp', 'blk'))
- d_norm_gain: float32 [2, 768], P(None, ('dp', 'blk'))
- d_norm_bias: float32 [2, 768], P(None, ('dp', 'blk'))
- d_w_up: float32 [768, 3072], P(('dp', 'blk'))
- d_up_bias: float32 [3072], P(('dp', 'blk'))
- d_w_down: float32 [3072, 768], P(('dp', 'blk'))
- d_down_bias: float32 [768], P(('dp', 'blk'))
The draws below stay inside these ranges and needn't reach their ends.
All inputs are finite; a program needn't handle non-finite values.
Results may differ from the reference program's by a relative error of at most 0.014.
Values may be sent and summed in bfloat16 or wider, within the bound.
A program may use at most 192 MiB of HBM per device.

```python
import math
import jax
import jax.numpy as jnp
from jax import lax

D = 768
FF = 3072
HEAD = 64
HEADS = 12
SEQ_LEN = 1024
TOKENS = 4096
N_DP = 4


def draw_w_qkv(key, part):
    order_key = jax.random.fold_in(key, 11)
    value_key = jax.random.fold_in(key, 23)
    heads = D // HEAD
    ranks = jax.random.permutation(order_key, heads).astype(jnp.float32)
    spread = ranks / float(max(heads - 1, 1))
    strength = 0.3 * jnp.exp(spread * math.log(2.0))
    columns = jnp.arange(3 * D)
    head_of = columns % D // HEAD
    factor = jnp.where(columns < 2 * D, strength[head_of], 1.0)
    base = jnp.clip(jax.random.normal(value_key, (D, 3 * D), jnp.float32), -3.0, 3.0)
    return (base * factor[None, :] * (1.0 / math.sqrt(D))).astype(jnp.bfloat16)


def steps_of(rng, shape, cuts, least, top_value):
    factor_of, own = 1.0, jax.random.fold_in(rng, 6)
    for position, blocks in cuts:
        heights = jnp.exp(jax.random.uniform(jax.random.fold_in(own, position), (blocks,), jnp.float32, least / len(cuts), top_value / len(cuts)))
        factor_of = factor_of * jnp.repeat(heights, shape[position] // blocks).reshape([-1 if axis == position else 1 for axis in range(len(shape))])
    return factor_of


def centred(key, extent, deviation, limit, cuts=(), dtype=jnp.bfloat16):
    level = steps_of(key, extent, cuts, -0.22, 0.18) if cuts else 1.0
    drawn = jax.random.normal(key, extent, jnp.float32) * deviation * level
    return jnp.minimum(jnp.maximum(drawn, -limit), limit).astype(dtype)


def setup_inputs(seed: int = 0) -> dict:
    streams_of = jax.random.split(jax.random.key(seed), 13)
    return {
        "tokens": centred(streams_of[0], (TOKENS, D), 1.0, 6.0, ((0, 32),)),
        "w_qkv": draw_w_qkv(jax.random.fold_in(streams_of[12], 71), 0),
        "qv_bias": centred(streams_of[2], (2, D), 0.5, 3.0, ((1, 32),)),
        "w_out": centred(streams_of[3], (D, D), 1.0, 6.0, ((0, 32),)),
        "out_bias": centred(streams_of[4], (D,), 0.5, 3.0, ((0, 32),)),
        "norm_gain": jnp.clip(1.0 + 0.1 * jax.random.normal(streams_of[5], (2, D), jnp.float32), 0.5, 1.5).astype(jnp.bfloat16),
        "norm_bias": centred(streams_of[6], (2, D), 0.5, 3.0, ((1, 32),)),
        "w_up": centred(streams_of[7], (D, FF), D ** -0.5, 0.21875, ((0, 32),)),
        "up_bias": centred(streams_of[8], (FF,), 0.5, 3.0, ((0, 32),)),
        "w_down": centred(streams_of[9], (FF, D), FF ** -0.5, 0.109375, ((0, 32),)),
        "down_bias": centred(streams_of[10], (D,), 0.5, 3.0, ((0, 32),)),
        "cotangent": centred(streams_of[11], (TOKENS, D), 1.0, 6.0, ((0, 32),)),
    }


EPS = 1e-05
SCALE = 0.125

def layernorm_forward(h, norm_gain_vector, norm_offset):
    row_average = lax.optimization_barrier(jnp.mean(h, axis=-1, keepdims=True))
    centered_input = h - row_average
    var = lax.optimization_barrier(jnp.mean(centered_input * centered_input, axis=-1, keepdims=True))
    inverse_deviation = lax.rsqrt(var + EPS)
    normalized_input = centered_input * inverse_deviation
    return (normalized_input * norm_gain_vector + norm_offset, normalized_input, inverse_deviation)

def layernorm_backward(incoming_gradient, normalized_input, inverse_deviation, norm_gain_vector):
    scaled_values = incoming_gradient * norm_gain_vector
    return inverse_deviation * (scaled_values - lax.optimization_barrier(jnp.mean(scaled_values, axis=-1, keepdims=True)) - normalized_input * lax.optimization_barrier(jnp.mean(scaled_values * normalized_input, axis=-1, keepdims=True)))

def gelu_grad(up):
    cdf = 0.5 * (1.0 + jax.scipy.special.erf(up * 0.7071067811865476))
    return cdf + up * jnp.exp(-0.5 * up * up) * 0.3989422804014327

def heads_of(block):
    return block.reshape(N_DP, SEQ_LEN, HEADS, HEAD).transpose(0, 2, 1, 3).reshape(N_DP * HEADS, SEQ_LEN, HEAD)

def rows_of(block):
    return block.reshape(N_DP, HEADS, SEQ_LEN, HEAD).transpose(0, 2, 1, 3).reshape(TOKENS, D)

def head_forward(args):
    query, key, value = args
    scores = jnp.dot(query, key.T, preferred_element_type=jnp.float32) * SCALE
    peak = lax.optimization_barrier(jnp.max(scores, axis=1))
    weights = jnp.exp(scores - peak[:, None])
    total = lax.optimization_barrier(jnp.sum(weights, axis=1))
    attn = jnp.dot(weights.astype(jnp.bfloat16), value, preferred_element_type=jnp.float32) / total[:, None]
    return (attn.astype(jnp.bfloat16), peak + jnp.log(total))

def head_backward(args):
    query, key, value, d_attn, lse, delta = args
    scores = jnp.dot(query, key.T, preferred_element_type=jnp.float32) * SCALE
    probs = jnp.exp(scores - lse[:, None])
    dprobs = jnp.dot(d_attn, value.T, preferred_element_type=jnp.float32)
    dscores = (probs * (dprobs - delta[:, None])).astype(jnp.bfloat16)
    d_query = SCALE * jnp.dot(dscores, key, preferred_element_type=jnp.float32)
    d_key = SCALE * jnp.dot(dscores.T, query, preferred_element_type=jnp.float32)
    d_value = jnp.dot(probs.astype(jnp.bfloat16).T, d_attn, preferred_element_type=jnp.float32)
    return (d_query, d_key, d_value)

def reference(tokens, w_qkv, qv_bias, w_out, out_bias, norm_gain, norm_bias, w_up, up_bias, w_down, down_bias, cotangent):
    f32 = jnp.float32
    bf16 = jnp.bfloat16
    norm_gain_pair = norm_gain.astype(f32)
    norm_offset_pair = norm_bias.astype(f32)
    qvb = qv_bias.astype(f32)
    bias_row = jnp.concatenate([qvb[0], jnp.zeros((D,), f32), qvb[1]])
    qkv = (jnp.dot(tokens, w_qkv, preferred_element_type=f32) + bias_row).astype(bf16)
    query = heads_of(qkv[:, :D])
    key = heads_of(qkv[:, D:2 * D])
    value = heads_of(qkv[:, 2 * D:])
    attn_heads, lse = lax.map(head_forward, (query, key, value))
    attn = rows_of(attn_heads)
    first_hidden = tokens.astype(f32) + jnp.dot(attn, w_out, preferred_element_type=f32) + out_bias.astype(f32)
    first_norm_output, first_normalized, first_inverse_deviation = layernorm_forward(first_hidden, norm_gain_pair[0], norm_offset_pair[0])
    y1_low = first_norm_output.astype(bf16)
    up = jnp.dot(y1_low, w_up, preferred_element_type=f32) + up_bias.astype(f32)
    act = jax.nn.gelu(up, approximate=False).astype(bf16)
    second_hidden = first_norm_output + jnp.dot(act, w_down, preferred_element_type=f32) + down_bias.astype(f32)
    output_float, second_normalized, second_inverse_deviation = layernorm_forward(second_hidden, norm_gain_pair[1], norm_offset_pair[1])
    output = output_float.astype(bf16)
    incoming_gradient = cotangent.astype(f32)
    second_gain_gradient = lax.optimization_barrier(jnp.sum(incoming_gradient * second_normalized, axis=0))
    d_shift2 = lax.optimization_barrier(jnp.sum(incoming_gradient, axis=0))
    second_hidden_gradient = layernorm_backward(incoming_gradient, second_normalized, second_inverse_deviation, norm_gain_pair[1])
    dh2_low = second_hidden_gradient.astype(bf16)
    d_w_down = jnp.dot(act.T, dh2_low, preferred_element_type=f32)
    d_down_bias = lax.optimization_barrier(jnp.sum(second_hidden_gradient, axis=0))
    d_up_f = jnp.dot(dh2_low, w_down.T, preferred_element_type=f32) * gelu_grad(up)
    d_up_bias = lax.optimization_barrier(jnp.sum(d_up_f, axis=0))
    d_up = d_up_f.astype(bf16)
    d_w_up = jnp.dot(y1_low.T, d_up, preferred_element_type=f32)
    first_output_gradient = second_hidden_gradient + jnp.dot(d_up, w_up.T, preferred_element_type=f32)
    first_gain_gradient = lax.optimization_barrier(jnp.sum(first_output_gradient * first_normalized, axis=0))
    d_shift1 = lax.optimization_barrier(jnp.sum(first_output_gradient, axis=0))
    first_hidden_gradient = layernorm_backward(first_output_gradient, first_normalized, first_inverse_deviation, norm_gain_pair[0])
    dh1_low = first_hidden_gradient.astype(bf16)
    d_w_out = jnp.dot(attn.T, dh1_low, preferred_element_type=f32)
    d_out_bias = lax.optimization_barrier(jnp.sum(first_hidden_gradient, axis=0))
    d_attn = jnp.dot(dh1_low, w_out.T, preferred_element_type=f32).astype(bf16)
    delta = heads_of((d_attn.astype(f32) * attn.astype(f32)).astype(f32))
    delta = lax.optimization_barrier(jnp.sum(delta, axis=-1))
    d_query, d_key, d_value = lax.map(head_backward, (query, key, value, heads_of(d_attn), lse, delta))
    d_query = rows_of(d_query)
    d_key = rows_of(d_key)
    d_value = rows_of(d_value)
    d_qv_bias = jnp.stack([lax.optimization_barrier(jnp.sum(d_query, axis=0)), lax.optimization_barrier(jnp.sum(d_value, axis=0))])
    d_qkv = jnp.concatenate([d_query, d_key, d_value], axis=1).astype(bf16)
    d_w_qkv = jnp.dot(tokens.T, d_qkv, preferred_element_type=f32)
    d_tokens = first_hidden_gradient + jnp.dot(d_qkv, w_qkv.T, preferred_element_type=f32)
    d_norm_gain = jnp.stack([first_gain_gradient, second_gain_gradient])
    d_norm_bias = jnp.stack([d_shift1, d_shift2])
    return (output, d_tokens, d_w_qkv, d_qv_bias, d_w_out, d_out_bias, d_norm_gain, d_norm_bias, d_w_up, d_up_bias, d_w_down, d_down_bias)
```

```python
import functools
import itertools

import jax
import jax.numpy as jnp
from jax import lax
from jax.experimental import pallas as pl
from jax.experimental.pallas import tpu as pltpu
from jax.sharding import PartitionSpec as P

HEAD = 64


EPS = 1e-05
SCALE = 0.125


def layernorm_forward(h, norm_gain_vector, norm_offset):
    row_average = jnp.mean(h, axis=-1, keepdims=True)
    centered_input = h - row_average
    var = jnp.mean(centered_input * centered_input, axis=-1, keepdims=True)
    inverse_deviation = lax.rsqrt(var + EPS)
    normalized_input = centered_input * inverse_deviation
    return (normalized_input * norm_gain_vector + norm_offset, normalized_input, inverse_deviation)


def layernorm_backward(incoming_gradient, normalized_input, inverse_deviation, norm_gain_vector):
    scaled_values = incoming_gradient * norm_gain_vector
    return inverse_deviation * (
        scaled_values
        - jnp.mean(scaled_values, axis=-1, keepdims=True)
        - normalized_input * jnp.mean(scaled_values * normalized_input, axis=-1, keepdims=True)
    )


def gelu_grad(up):
    cdf = 0.5 * (1.0 + jax.scipy.special.erf(up * 0.7071067811865476))
    return cdf + up * jnp.exp(-0.5 * up * up) * 0.3989422804014327


def contract_rows(left, right):
    return lax.dot_general(
        left, right, (((0,), (0,)), ((), ())), preferred_element_type=jnp.float32
    )


def contract_cols(left, right):
    return lax.dot_general(
        left, right, (((1,), (1,)), ((), ())), preferred_element_type=jnp.float32
    )


PAIR = 2 * HEAD


def attend_kernel(width, q_ref, kv_ref, attn_ref, lse_ref):
    def pair(i, carry):
        at = pl.ds(pl.multiple_of(i * PAIR, PAIR), PAIR)
        q2 = q_ref[:, at]
        k2 = kv_ref[:, at]
        v2 = kv_ref[:, pl.ds(pl.multiple_of(width + i * PAIR, PAIR), PAIR)]
        outs, logs = [], []
        for j in range(2):
            own = slice(j * HEAD, (j + 1) * HEAD)
            scores = contract_cols(q2[:, own], k2[:, own]) * SCALE
            peak = jnp.max(scores, axis=1, keepdims=True)
            weights = jnp.exp(scores - peak)
            total = jnp.sum(weights, axis=1, keepdims=True)
            part = jnp.dot(
                weights.astype(jnp.bfloat16), v2[:, own], preferred_element_type=jnp.float32
            )
            outs.append((part / total).astype(jnp.bfloat16))
            logs.append(peak + jnp.log(total))
        attn_ref[:, at] = jnp.concatenate(outs, axis=1)
        lse_ref[i] = jnp.concatenate(logs, axis=1)
        return carry

    lax.fori_loop(0, width // PAIR, pair, 0)


def attend(query, kv):
    rows, width = query.shape
    vmem = pl.BlockSpec(memory_space=pltpu.VMEM)
    return pl.pallas_call(
        functools.partial(attend_kernel, width),
        out_shape=(
            jax.ShapeDtypeStruct((rows, width), jnp.bfloat16),
            jax.ShapeDtypeStruct((width // PAIR, rows, 2), jnp.float32),
        ),
        in_specs=[vmem] * 2,
        out_specs=(vmem, vmem),
        compiler_params=pltpu.CompilerParams(vmem_limit_bytes=60 << 20),
    )(query, kv)


def attend_back_kernel(width, q_ref, kv_ref, do_ref, lse_ref, delta_ref, dq_ref, dkv_ref):
    def pair(i, carry):
        at = pl.ds(pl.multiple_of(i * PAIR, PAIR), PAIR)
        val = pl.ds(pl.multiple_of(width + i * PAIR, PAIR), PAIR)
        q2 = q_ref[:, at]
        do2 = do_ref[:, at]
        k2 = kv_ref[:, at]
        v2 = kv_ref[:, val]
        lse2 = lse_ref[i]
        delta2 = delta_ref[i]
        dqs, dks, dvs = [], [], []
        for j in range(2):
            own = slice(j * HEAD, (j + 1) * HEAD)
            q_h, do_h, k_h, v_h = q2[:, own], do2[:, own], k2[:, own], v2[:, own]
            scores = contract_cols(k_h, q_h) * SCALE
            probs = jnp.exp(scores - lse2[j : j + 1])
            dprobs = contract_cols(v_h, do_h)
            dscores = (probs * (dprobs - delta2[j : j + 1])).astype(jnp.bfloat16)
            dqs.append(SCALE * contract_rows(dscores, k_h))
            dks.append(SCALE * jnp.dot(dscores, q_h, preferred_element_type=jnp.float32))
            dvs.append(
                jnp.dot(probs.astype(jnp.bfloat16), do_h, preferred_element_type=jnp.float32)
            )
        dq_ref[:, at] = jnp.concatenate(dqs, axis=1)
        dkv_ref[:, at] = jnp.concatenate(dks, axis=1).astype(jnp.bfloat16)
        dkv_ref[:, val] = jnp.concatenate(dvs, axis=1).astype(jnp.bfloat16)
        return carry

    lax.fori_loop(0, width // PAIR, pair, 0)


def attend_back(query, kv, d_attn, lse, delta):
    rows, width = query.shape
    vmem = pl.BlockSpec(memory_space=pltpu.VMEM)
    return pl.pallas_call(
        functools.partial(attend_back_kernel, width),
        out_shape=(
            jax.ShapeDtypeStruct((rows, width), jnp.float32),
            jax.ShapeDtypeStruct(kv.shape, jnp.bfloat16),
        ),
        in_specs=[vmem] * 5,
        out_specs=(vmem, vmem),
        compiler_params=pltpu.CompilerParams(vmem_limit_bytes=60 << 20),
    )(query, kv, d_attn, lse, delta)


MESH = pl.DeviceIdType.MESH
CORES = 2


def tree_events(order, depth):
    spans = {"x": [0, 1], "y": [0, 1], "z": [0] + [s * k for k in range(1, depth) for s in (1, -1)]}
    sides = {"x": [("x", 1)], "y": [("y", 1)], "z": [("z", 1), ("z", -1)]}
    found = []
    for offsets in itertools.product(*(spans[d] for d in order)):
        moved = [i for i, o in enumerate(offsets) if o]
        last = moved[-1] if moved else -1
        parent, children = None, []
        if moved:
            toward = 1 if offsets[last] > 0 else -1
            parent = (order[last], toward)
            if order[last] == "z":
                children.append(("z", -toward))
        for d in order[last + 1 :]:
            children += sides[d]
        found.append((sum(abs(o) for o in offsets), dict(zip(order, offsets)), parent, children))
    return found


def here(depth):
    dp, blk = lax.axis_index("dp"), lax.axis_index("blk")
    return {"y": dp // CORES, "c": lax.rem(dp, CORES), "z": blk // 2, "x": lax.rem(blk, 2)}


def device_of(pos):
    return (pos["y"] * CORES + pos["c"], pos["z"] * 2 + pos["x"])


def beside(pos, side):
    d, step = side
    moved = dict(pos)
    moved[d] = pos[d] + step if d == "z" else 1 - pos[d]
    return moved


def exists(pos, side, depth):
    if side[0] != "z":
        return None
    return pos["z"] + 1 < depth if side[1] > 0 else pos["z"] >= 1


def source_of(pos, offsets):
    moved = dict(pos)
    for d, o in offsets.items():
        if o:
            moved[d] = pos[d] + o if d == "z" else 1 - pos[d]
    return moved


def in_line(pos, offsets, depth):
    o = offsets.get("z", 0)
    if o == 0:
        return None
    return pos["z"] + o < depth if o > 0 else pos["z"] >= -o


def when(cond, body):
    if cond is None:
        body()
    else:
        pl.when(cond)(body)


def greet(pos, sides, depth):
    barrier = pltpu.get_barrier_semaphore()
    for side in sides:
        when(
            exists(pos, side, depth),
            lambda side=side: pl.semaphore_signal(
                barrier, inc=1, device_id=device_of(beside(pos, side)), device_id_type=MESH
            ),
        )
    peers = sum(1 for d, _ in sides if d != "z")
    if any(d == "z" for d, _ in sides):
        up = jnp.where(pos["z"] + 1 < depth, 1, 0)
        peers = peers + up + jnp.where(pos["z"] >= 1, 1, 0)
    pl.semaphore_wait(barrier, peers)


def schedule(flows, depth):
    events = []
    for f, flow in enumerate(flows):
        for hops, offsets, parent, children in tree_events(flow["order"], depth):
            events.append((hops, f, offsets, parent, children))
    events.sort(key=lambda e: (e[0], e[1]))
    return events


def group_of(offsets):
    return tuple(sorted((d, o) for d, o in offsets.items() if d != "z"))


def flat_sides(flows):
    axes = sorted({d for flow in flows for d in flow["order"]})
    sides = [s for d in axes for s in ([("z", 1), ("z", -1)] if d == "z" else [(d, 1)])]
    return sides + ([("c", 1)] if any(flow["cores"] for flow in flows) else [])


def block(ref, flow, src):
    lead = (src["y"], src["c"], src["z"], src["x"]) if flow["cores"] else (src["z"], src["x"])
    low, wide = flow["columns"]
    return ref.at[lead + (slice(None), pl.ds(low, wide))]


def column(ref, flow, src):
    lead = (src["y"], src["c"], slice(None), src["x"]) if flow["cores"] else (slice(None), src["x"])
    low, wide = flow["columns"]
    return ref.at[lead + (slice(None), pl.ds(low, wide))]


def gather_kernel(flows, depth, n_in, n_out, *refs):
    ins, outs = refs[:n_in], refs[n_in : n_in + n_out]
    recv, sent, core_recv, core_sent, local = refs[n_in + n_out :]
    pos = here(depth)
    greet(pos, flat_sides(flows), depth)
    events = schedule(flows, depth)
    copies = []
    for f, flow in enumerate(flows):
        low, wide = flow["in_columns"]
        own = ins[flow["in"]].at[:, pl.ds(low, wide)]
        copy = pltpu.make_async_copy(own, block(outs[flow["out"]], flow, pos), local.at[f])
        copy.start()
        copies.append(copy)
    waits, sites, met = [], 0, {}
    last = {}
    for i, e in enumerate(events):
        last[(e[1], group_of(e[2]))] = i
    for i, (hops, f, offsets, parent, children) in enumerate(events):
        flow = flows[f]
        src = source_of(pos, offsets)
        out = outs[flow["out"]]
        low, wide = flow["in_columns"]
        target = block(out, flow, src)
        origin = ins[flow["in"]].at[:, pl.ds(low, wide)] if parent is None else target
        mark = recv.at[f, src["y"] if "y" in flow["order"] else 0, src["z"], src["x"]]
        sends = []
        for side in children:
            sends.append(
                (
                    side,
                    functools.partial(
                        pltpu.make_async_remote_copy,
                        origin,
                        target,
                        sent.at[sites],
                        mark,
                        device_id=device_of(beside(pos, side)),
                        device_id_type=MESH,
                    ),
                )
            )
            sites += 1

        def arrive():
            if parent is not None:
                pltpu.make_async_copy(target, target, mark).wait()
            for side, send in sends:
                when(exists(pos, side, depth), lambda: send().start())

        def finish(sends=sends):
            for side, send in sends:
                when(exists(pos, side, depth), lambda: send().wait_send())

        cond = in_line(pos, offsets, depth)
        when(cond, arrive)
        if sends:
            waits.append((cond, finish))
        if flow["cores"] and last[(f, group_of(offsets))] == i:
            if not any(o for d, o in offsets.items() if d != "z"):
                copies[f].wait()
            other = beside(src, ("c", 1))
            whole = column(out, flow, src)
            core = pltpu.make_async_remote_copy(
                whole,
                whole,
                core_sent.at[f, src["y"], src["x"]],
                core_recv.at[f, src["y"], src["x"]],
                device_id=device_of(beside(pos, ("c", 1))),
                device_id_type=MESH,
            )
            core.start()
            landed = column(out, flow, other)
            arrival = pltpu.make_async_copy(landed, landed, core_recv.at[f, src["y"], src["x"]])
            waits.append((None, lambda core=core, arrival=arrival: (core.wait_send(), arrival.wait())))
    for f, flow in enumerate(flows):
        if not flow["cores"]:
            copies[f].wait()
    for cond, finish in waits:
        when(cond, finish)


def count_sites(flows, depth):
    return sum(len(e[4]) for e in schedule(flows, depth))


def gather(flows, depth, inputs, out_shapes, collective_id):
    hbm = pl.BlockSpec(memory_space=pl.ANY)
    n = len(flows)
    return pl.pallas_call(
        functools.partial(gather_kernel, flows, depth, len(inputs), len(out_shapes)),
        out_shape=tuple(out_shapes),
        in_specs=[hbm] * len(inputs),
        out_specs=tuple([hbm] * len(out_shapes)),
        scratch_shapes=[
            pltpu.SemaphoreType.DMA((n, 2, depth, 2)),
            pltpu.SemaphoreType.DMA((count_sites(flows, depth),)),
            pltpu.SemaphoreType.DMA((n, 2, 2)),
            pltpu.SemaphoreType.DMA((n, 2, 2)),
            pltpu.SemaphoreType.DMA((n,)),
        ],
        compiler_params=pltpu.CompilerParams(collective_id=collective_id, has_side_effects=True),
    )(*inputs)


def slots_of(flow, d, depth):
    sizes = {"x": 2, "y": 2, "z": depth}
    before = flow["order"][: flow["order"].index(d)]
    return ([2] if d == "z" else []) + [sizes[k] for k in before] + ([depth] if d == "z" else [])


def slot(flow, d, src, side):
    before = flow["order"][: flow["order"].index(d)]
    return (
        ([0 if side > 0 else 1] if d == "z" else [])
        + [src[k] for k in before]
        + ([src["z"]] if d == "z" else [])
    )


def chunk_of(rows, columns):
    wide = 128
    while columns % (2 * wide) == 0 and rows * 2 * wide <= 12 * 1024:
        wide *= 2
    return wide


def scatter_kernel(flows, depth, n_in, n_out, *refs):
    ins, outs = refs[:n_in], refs[n_in : n_in + n_out]
    at = n_in + n_out
    mine, theirs, slots, marks = [], [], [], []
    for flow in flows:
        mine.append(refs[at])
        at += 1
        theirs.append(refs[at] if flow["cores"] else None)
        at += 1 if flow["cores"] else 0
        slots.append({})
        marks.append({})
        for d in flow["order"]:
            slots[-1][d], marks[-1][d] = refs[at], refs[at + 1]
            at += 2
    sent, core_recv, core_sent, local = refs[at:]
    pos = here(depth)
    greet(pos, flat_sides(flows), depth)
    events = schedule(flows, depth)[::-1]

    def lead(flow, src):
        return (src["y"], src["z"], src["x"]) if flow["cores"] else (src["z"], src["x"])

    def col(flow, src):
        return (src["y"], slice(None), src["x"]) if flow["cores"] else (slice(None), src["x"])

    ready, waits, sites = {}, [], 0
    for hops, f, offsets, parent, children in events:
        key = (f, group_of(offsets))
        if key in ready:
            continue
        flow = flows[f]
        src = source_of(pos, {d: o for d, o in offsets.items() if d != "z"})
        y = src["y"] if flow["cores"] else 0
        loads = []
        if flow["cores"]:
            core = pltpu.make_async_remote_copy(
                column(ins[flow["in"]], flow, beside(src, ("c", 1))),
                theirs[f].at[col(flow, src)],
                core_sent.at[f, y, src["x"]],
                core_recv.at[f, y, src["x"]],
                device_id=device_of(beside(pos, ("c", 1))),
                device_id_type=MESH,
            )
            core.start()
            loads.append(core.wait_recv)
            waits.append((None, core.wait_send))
        copy = pltpu.make_async_copy(
            column(ins[flow["in"]], flow, src), mine[f].at[col(flow, src)], local.at[f, y, src["x"]]
        )
        copy.start()
        loads.append(copy.wait)
        ready[key] = loads
    for hops, f, offsets, parent, children in events:
        flow = flows[f]
        for load in ready.pop((f, group_of(offsets)), []):
            load()
        src = source_of(pos, offsets)
        own = lead(flow, src)
        send = None
        if parent is not None:
            d, toward = parent
            place = tuple(slot(flow, d, src, -toward))
            send = pltpu.make_async_remote_copy(
                mine[f].at[own],
                slots[f][d].at[place] if place else slots[f][d],
                sent.at[sites],
                marks[f][d].at[place if place else (0,)],
                device_id=device_of(beside(pos, parent)),
                device_id_type=MESH,
            )
            sites += 1

        def step():
            rows, columns = mine[f].shape[-2:]
            wide = chunk_of(rows, columns)
            terms = []
            for side in children:
                d = side[0]
                place = tuple(slot(flow, d, src, side[1]))
                buf = slots[f][d].at[place] if place else slots[f][d]
                there = exists(pos, side, depth)
                when(
                    there,
                    lambda: pltpu.make_async_copy(
                        buf, buf, marks[f][d].at[place if place else (0,)]
                    ).wait(),
                )
                terms.append((place, d, there))

            def total(cols):
                value = mine[f][own + (slice(None), cols)].astype(jnp.float32)
                if flow["cores"]:
                    value += theirs[f][own + (slice(None), cols)].astype(jnp.float32)
                return value

            def put(cols, value):
                if send is None:
                    low = flow["out_low"]
                    outs[flow["out"]][:, pl.ds(pl.multiple_of(low + cols.start, 128), wide)] = value
                else:
                    mine[f][own + (slice(None), cols)] = value.astype(mine[f].dtype)

            def with_terms(chosen):
                def go():
                    def body(k, carry):
                        cols = pl.ds(pl.multiple_of(k * wide, wide), wide)
                        value = total(cols)
                        for place, d in chosen:
                            value += slots[f][d][place + (slice(None), cols)].astype(jnp.float32)
                        put(cols, value)
                        return carry

                    lax.fori_loop(0, columns // wide, body, 0)

                return go

            always = [(p, d) for p, d, there in terms if there is None]
            maybe = [(p, d, there) for p, d, there in terms if there is not None]
            if flow["cores"] or always or maybe:
                for picks in itertools.product((True, False), repeat=len(maybe)):
                    cond = None
                    for (p, d, there), pick in zip(maybe, picks):
                        test = there if pick else jnp.logical_not(there)
                        cond = test if cond is None else jnp.logical_and(cond, test)
                    chosen = always + [(p, d) for (p, d, _), pick in zip(maybe, picks) if pick]
                    if not chosen and not flow["cores"] and send is not None:
                        continue
                    when(cond, with_terms(chosen))
            if send is not None:
                send.start()

        cond = in_line(pos, offsets, depth)
        when(cond, step)
        if send is not None:
            waits.append((cond, send.wait_send))
    for cond, finish in waits:
        when(cond, finish)


def scatter(flows, depth, inputs, out_shapes, collective_id):
    hbm = pl.BlockSpec(memory_space=pl.ANY)
    vmem = pl.BlockSpec(memory_space=pltpu.VMEM)
    n = len(flows)
    scratch = []
    for flow in flows:
        rows = inputs[flow["in"]].shape[-2]
        unit = (rows, flow["columns"][1])
        kind = inputs[flow["in"]].dtype
        whole = ((2, depth, 2) if flow["cores"] else (depth, 2)) + unit
        scratch.append(pltpu.VMEM(whole, kind))
        if flow["cores"]:
            scratch.append(pltpu.VMEM(whole, kind))
        for d in flow["order"]:
            places = tuple(slots_of(flow, d, depth))
            scratch.append(pltpu.VMEM(places + unit, kind))
            scratch.append(pltpu.SemaphoreType.DMA(places if places else (1,)))
    events = schedule(flows, depth)
    scratch += [
        pltpu.SemaphoreType.DMA((len(events),)),
        pltpu.SemaphoreType.DMA((n, 2, 2)),
        pltpu.SemaphoreType.DMA((n, 2, 2)),
        pltpu.SemaphoreType.DMA((n, 2, 2)),
    ]
    return pl.pallas_call(
        functools.partial(scatter_kernel, flows, depth, len(inputs), len(out_shapes)),
        out_shape=tuple(out_shapes),
        in_specs=[hbm] * len(inputs),
        out_specs=tuple([vmem] * len(out_shapes)),
        scratch_shapes=scratch,
        compiler_params=pltpu.CompilerParams(
            collective_id=collective_id, has_side_effects=True, vmem_limit_bytes=60 << 20
        ),
    )(*inputs)


ORDERS = (("z", "x", "y"), ("z", "y", "x"), ("x", "z", "y"), ("y", "z", "x"), ("z", "y", "x"))


def weight_flows(columns):
    return [
        dict(order=order, cores=True, columns=(0, wide), in_columns=(0, wide), out_low=0, **{"in": i, "out": i})
        for i, (order, wide) in enumerate(zip(ORDERS, columns))
    ]


def kv_flows(width, low):
    half = width // 2
    parts = [(("z", "x"), 0, width), (("z", "x"), width, half), (("x", "z"), width + half, half)]
    return [
        dict(order=order, cores=False, columns=(at, wide), in_columns=(low + at, wide), out_low=at, **{"in": 0, "out": 0})
        for order, at, wide in parts
    ]


def layout_of(large):
    dp, blk = lax.axis_size("dp"), lax.axis_size("blk")
    rows = [v.shape[0] for v in large]
    if dp == 2 * CORES and blk % 2 == 0 and 2 <= blk // 2 <= 4 and all(r % 8 == 0 for r in rows):
        return blk // 2
    return None


def gather_weights(large, depth):
    if depth is None:
        wholes = [lax.all_gather(v, ("dp", "blk"), axis=0, tiled=True) for v in large]
        return wholes
    shapes = [jax.ShapeDtypeStruct((2, CORES, depth, 2) + v.shape, v.dtype) for v in large]
    flows = weight_flows([v.shape[1] for v in large])
    wholes = gather(flows, depth, large, shapes, 1)
    return [w.reshape(-1, w.shape[-1]) for w in wholes]


def gather_kv(qkv, width, depth):
    if depth is None:
        return lax.all_gather(qkv[:, width:], "blk", axis=0, tiled=True)
    rows = qkv.shape[0]
    shape = jax.ShapeDtypeStruct((depth, 2, rows, 2 * width), qkv.dtype)
    (kv,) = gather(kv_flows(width, width), depth, [qkv], [shape], 2)
    return kv.reshape(-1, 2 * width)


def scatter_kv(d_kv, rows, depth):
    if depth is None:
        return lax.psum_scatter(d_kv, "blk", scatter_dimension=0, tiled=True).astype(jnp.float32)
    columns = d_kv.shape[1]
    shape = jax.ShapeDtypeStruct((rows, columns), jnp.float32)
    (out,) = scatter(
        kv_flows(columns // 2, 0), depth, [d_kv.reshape(depth, 2, rows, columns)], [shape], 3
    )
    return out


def scatter_weights(grads, large, depth):
    n = lax.axis_size("dp") * lax.axis_size("blk")
    if depth is None:
        return [
            lax.psum_scatter(g, ("dp", "blk"), scatter_dimension=0, tiled=True).astype(jnp.float32)
            for g in grads
        ]
    blocks = [g.reshape((2, CORES, depth, 2) + v.shape) for g, v in zip(grads, large)]
    shapes = [jax.ShapeDtypeStruct(v.shape, jnp.float32) for v in large]
    return scatter(weight_flows([v.shape[1] for v in large]), depth, blocks, shapes, 4)


def on_device(
    tokens,
    w_qkv,
    qv_bias,
    w_out,
    out_bias,
    norm_gain,
    norm_bias,
    w_up,
    up_bias,
    w_down,
    down_bias,
    cotangent,
):
    f32 = jnp.float32
    bf16 = jnp.bfloat16
    rows, width = tokens.shape
    heads = width // HEAD
    n = lax.axis_size("dp") * lax.axis_size("blk")
    large = [w_qkv, w_out, w_up, w_down]
    depth = layout_of(large)
    own = out_bias.shape[0]
    narrow = jnp.concatenate([qv_bias, out_bias[None], norm_gain, norm_bias, down_bias[None]])
    flat = jnp.concatenate([narrow.reshape(-1), up_bias])
    split = 8 * own + up_bias.size
    high = -(-split // 2048) * 16
    flat = jnp.pad(flat, (0, high * 128 - split)).reshape(high, 128)
    wq_full, wo_full, wu_full, wd_full, gathered = gather_weights(large + [flat], depth)
    gathered = gathered.astype(f32).reshape(n, -1)
    narrow_full = gathered[:, : 8 * own].reshape(n, 8, own).transpose(1, 0, 2).reshape(8, width)
    bu_full = gathered[:, 8 * own : split].reshape(-1)
    qvb, bo_full, norm_gain_pair = narrow_full[0:2], narrow_full[2], narrow_full[3:5]
    norm_offset_pair, bd_full = narrow_full[5:7], narrow_full[7]
    bias_row = jnp.concatenate([qvb[0], jnp.zeros((width,), f32), qvb[1]])
    qkv = (jnp.dot(tokens, wq_full, preferred_element_type=f32) + bias_row).astype(bf16)
    query = qkv[:, :width]
    kv = gather_kv(qkv, width, depth)
    attn, lse = attend(query, kv)
    first_hidden = (
        tokens.astype(f32)
        + jnp.dot(attn, wo_full, preferred_element_type=f32)
        + bo_full
    )
    first_norm_output, first_normalized, first_inverse_deviation = layernorm_forward(
        first_hidden, norm_gain_pair[0], norm_offset_pair[0]
    )
    y1_low = first_norm_output.astype(bf16)
    up = jnp.dot(y1_low, wu_full, preferred_element_type=f32) + bu_full
    act = jax.nn.gelu(up, approximate=False).astype(bf16)
    second_hidden = (
        first_norm_output + jnp.dot(act, wd_full, preferred_element_type=f32) + bd_full
    )
    output_float, second_normalized, second_inverse_deviation = layernorm_forward(
        second_hidden, norm_gain_pair[1], norm_offset_pair[1]
    )
    output = output_float.astype(bf16)
    wq_b, wo_b, wu_b, wd_b = wq_full, wo_full, wu_full, wd_full
    gain_pair_block = norm_gain_pair
    incoming_gradient = cotangent.astype(f32)
    second_gain_gradient = jnp.sum(incoming_gradient * second_normalized, axis=0)
    d_shift2 = jnp.sum(incoming_gradient, axis=0)
    second_hidden_gradient = layernorm_backward(
        incoming_gradient, second_normalized, second_inverse_deviation, gain_pair_block[1]
    )
    dh2_low = second_hidden_gradient.astype(bf16)
    d_w_down = contract_rows(act, dh2_low)
    d_down_bias = jnp.sum(second_hidden_gradient, axis=0)
    d_up_f = contract_cols(dh2_low, wd_b) * gelu_grad(up)
    d_up_bias = jnp.sum(d_up_f, axis=0)
    d_up = d_up_f.astype(bf16)
    d_w_up = contract_rows(y1_low, d_up)
    first_output_gradient = second_hidden_gradient + contract_cols(d_up, wu_b)
    first_gain_gradient = jnp.sum(first_output_gradient * first_normalized, axis=0)
    d_shift1 = jnp.sum(first_output_gradient, axis=0)
    first_hidden_gradient = layernorm_backward(
        first_output_gradient, first_normalized, first_inverse_deviation, gain_pair_block[0]
    )
    dh1_low = first_hidden_gradient.astype(bf16)
    d_w_out = contract_rows(attn, dh1_low)
    d_out_bias = jnp.sum(first_hidden_gradient, axis=0)
    d_gains = jnp.stack([first_gain_gradient, second_gain_gradient])
    d_shifts = jnp.stack([d_shift1, d_shift2])
    d_attn = contract_cols(dh1_low, wo_b).astype(bf16)
    delta = jnp.sum((d_attn.astype(f32) * attn.astype(f32)).reshape(rows, heads, HEAD), axis=-1).T
    d_query, d_kv_all = attend_back(
        query, kv, d_attn, lse.transpose(0, 2, 1), delta.reshape(heads // 2, 2, rows)
    )
    d_kv = scatter_kv(d_kv_all, rows, depth)
    d_key = d_kv[:, :width]
    d_value = d_kv[:, width:]
    d_qv = jnp.stack([jnp.sum(d_query, axis=0), jnp.sum(d_value, axis=0)])
    d_qkv = jnp.concatenate([d_query, d_key, d_value], axis=1).astype(bf16)
    d_w_qkv = contract_rows(tokens, d_qkv)
    d_tokens = first_hidden_gradient + contract_cols(d_qkv, wq_b)
    rows_of_8 = jnp.concatenate([d_qv, d_out_bias[None], d_gains, d_shifts, d_down_bias[None]])
    row = jnp.concatenate(
        [
            rows_of_8.reshape(8, n, own).transpose(1, 0, 2).reshape(n, 8 * own),
            d_up_bias.reshape(n, -1),
        ],
        axis=1,
    )
    row = jnp.pad(row, ((0, 0), (0, flat.size - split))).reshape(-1, 128)
    grads = [d.astype(bf16) for d in (d_w_qkv, d_w_out, d_w_up, d_w_down)]
    g_wqkv, g_wout, g_wup, g_wdown, row = scatter_weights(grads + [row], large + [flat], depth)
    row = row.reshape(-1)
    row8 = row[: 8 * own].reshape(8, own)
    g_qv, g_bout, g_gain = row8[0:2], row8[2], row8[3:5]
    g_shift, g_bdown, g_bup = row8[5:7], row8[7], row[8 * own : split]
    return (
        output,
        d_tokens,
        g_wqkv,
        g_qv,
        g_wout,
        g_bout,
        g_gain,
        g_shift,
        g_wup,
        g_bup,
        g_wdown,
        g_bdown,
    )


def solution(mesh):
    return jax.shard_map(
        on_device,
        mesh=mesh,
        in_specs=(
            P(("dp", "blk"), None),
            P(("dp", "blk"), None),
            P(None, ("dp", "blk")),
            P(("dp", "blk"), None),
            P(("dp", "blk")),
            P(None, ("dp", "blk")),
            P(None, ("dp", "blk")),
            P(("dp", "blk"), None),
            P(("dp", "blk")),
            P(("dp", "blk"), None),
            P(("dp", "blk")),
            P(("dp", "blk"), None),
        ),
        out_specs=(
            P(("dp", "blk"), None),
            P(("dp", "blk"), None),
            P(("dp", "blk"), None),
            P(None, ("dp", "blk")),
            P(("dp", "blk"), None),
            P(("dp", "blk")),
            P(None, ("dp", "blk")),
            P(None, ("dp", "blk")),
            P(("dp", "blk"), None),
            P(("dp", "blk")),
            P(("dp", "blk"), None),
            P(("dp", "blk")),
        ),
        check_vma=False,
    )
```

```python
import functools
import itertools

import jax
import jax.numpy as jnp
import numpy as np
from jax import lax
from jax.experimental import pallas as pl
from jax.experimental.pallas import tpu as pltpu
from jax.sharding import PartitionSpec as P

HEAD = 64


EPS = 1e-05
SCALE = 0.125


def layernorm_forward(h, norm_gain_vector, norm_offset):
    row_average = jnp.mean(h, axis=-1, keepdims=True)
    centered_input = h - row_average
    var = jnp.mean(centered_input * centered_input, axis=-1, keepdims=True)
    inverse_deviation = lax.rsqrt(var + EPS)
    normalized_input = centered_input * inverse_deviation
    return (normalized_input * norm_gain_vector + norm_offset, normalized_input, inverse_deviation)


def layernorm_backward(incoming_gradient, normalized_input, inverse_deviation, norm_gain_vector):
    scaled_values = incoming_gradient * norm_gain_vector
    return inverse_deviation * (
        scaled_values
        - jnp.mean(scaled_values, axis=-1, keepdims=True)
        - normalized_input * jnp.mean(scaled_values * normalized_input, axis=-1, keepdims=True)
    )


def gelu_grad(up):
    cdf = 0.5 * (1.0 + jax.scipy.special.erf(up * 0.7071067811865476))
    return cdf + up * jnp.exp(-0.5 * up * up) * 0.3989422804014327


def contract_rows(left, right):
    return lax.dot_general(
        left, right, (((0,), (0,)), ((), ())), preferred_element_type=jnp.float32
    )


def contract_cols(left, right):
    return lax.dot_general(
        left, right, (((1,), (1,)), ((), ())), preferred_element_type=jnp.float32
    )


PAIR = 2 * HEAD


def attend_pair(width, q_ref, keys_of, attn_ref, lse_ref, i):
    at = pl.ds(pl.multiple_of(i * PAIR, PAIR), PAIR)
    q2 = q_ref[:, at]
    k2 = keys_of(at)
    v2 = keys_of(pl.ds(pl.multiple_of(width + i * PAIR, PAIR), PAIR))
    outs, logs = [], []
    for j in range(2):
        own = slice(j * HEAD, (j + 1) * HEAD)
        scores = contract_cols(q2[:, own], k2[:, own]) * SCALE
        peak = jnp.max(scores, axis=1, keepdims=True)
        weights = jnp.exp(scores - peak)
        total = jnp.sum(weights, axis=1, keepdims=True)
        part = jnp.dot(
            weights.astype(jnp.bfloat16), v2[:, own], preferred_element_type=jnp.float32
        )
        outs.append((part / total).astype(jnp.bfloat16))
        logs.append(peak + jnp.log(total))
    attn_ref[:, at] = jnp.concatenate(outs, axis=1)
    lse_ref[i] = jnp.concatenate(logs, axis=1)


def attend_back_pair(
    width, q_ref, keys_of, do_ref, lse_ref, delta_ref, dq_ref, put_keys, put_values, i
):
    at = pl.ds(pl.multiple_of(i * PAIR, PAIR), PAIR)
    val = pl.ds(pl.multiple_of(width + i * PAIR, PAIR), PAIR)
    q2 = q_ref[:, at]
    do2 = do_ref[:, at]
    k2 = keys_of(at)
    v2 = keys_of(val)
    lse2 = lse_ref[i]
    delta2 = delta_ref[i]
    dqs, dks, dvs = [], [], []
    for j in range(2):
        own = slice(j * HEAD, (j + 1) * HEAD)
        q_h, do_h, k_h, v_h = q2[:, own], do2[:, own], k2[:, own], v2[:, own]
        scores = contract_cols(k_h, q_h) * SCALE
        probs = jnp.exp(scores - lse2[j : j + 1])
        dprobs = contract_cols(v_h, do_h)
        dscores = (probs * (dprobs - delta2[j : j + 1])).astype(jnp.bfloat16)
        dqs.append(SCALE * contract_rows(dscores, k_h))
        dks.append(SCALE * jnp.dot(dscores, q_h, preferred_element_type=jnp.float32))
        dvs.append(jnp.dot(probs.astype(jnp.bfloat16), do_h, preferred_element_type=jnp.float32))
    dq_ref[:, at] = jnp.concatenate(dqs, axis=1)
    put_keys(at, jnp.concatenate(dks, axis=1))
    put_values(at, val, jnp.concatenate(dvs, axis=1))


def attend_kernel(width, q_ref, kv_ref, attn_ref, lse_ref):
    def pair(i, carry):
        attend_pair(width, q_ref, lambda at: kv_ref[:, at], attn_ref, lse_ref, i)
        return carry

    lax.fori_loop(0, width // PAIR, pair, 0)


def attend(query, kv):
    rows, width = query.shape
    vmem = pl.BlockSpec(memory_space=pltpu.VMEM)
    return pl.pallas_call(
        functools.partial(attend_kernel, width),
        out_shape=attend_shapes(rows, width),
        in_specs=[vmem] * 2,
        out_specs=(vmem, vmem),
        compiler_params=pltpu.CompilerParams(vmem_limit_bytes=60 << 20),
    )(query, kv)


def attend_shapes(rows, width):
    return (
        jax.ShapeDtypeStruct((rows, width), jnp.bfloat16),
        jax.ShapeDtypeStruct((width // PAIR, rows, 2), jnp.float32),
    )


def attend_back_kernel(width, q_ref, kv_ref, do_ref, lse_ref, delta_ref, dq_ref, dkv_ref):
    def put(at, value):
        dkv_ref[:, at] = value.astype(jnp.bfloat16)

    def pair(i, carry):
        attend_back_pair(
            width,
            q_ref,
            lambda at: kv_ref[:, at],
            do_ref,
            lse_ref,
            delta_ref,
            dq_ref,
            put,
            lambda at, val, value: put(val, value),
            i,
        )
        return carry

    lax.fori_loop(0, width // PAIR, pair, 0)


def attend_back(query, kv, d_attn, lse, delta):
    rows, width = query.shape
    vmem = pl.BlockSpec(memory_space=pltpu.VMEM)
    return pl.pallas_call(
        functools.partial(attend_back_kernel, width),
        out_shape=(
            jax.ShapeDtypeStruct((rows, width), jnp.float32),
            jax.ShapeDtypeStruct(kv.shape, jnp.bfloat16),
        ),
        in_specs=[vmem] * 5,
        out_specs=(vmem, vmem),
        compiler_params=pltpu.CompilerParams(vmem_limit_bytes=60 << 20),
    )(query, kv, d_attn, lse, delta)


def in_steps(pairs, steps, pair):
    bounds = [pairs * k // steps for k in range(steps + 1)]

    def step(low, high):
        def body(i, carry):
            pair(i)
            return carry

        lax.fori_loop(low, high, body, 0)

    return [functools.partial(step, lo, hi) for lo, hi in zip(bounds, bounds[1:])]


MESH = pl.DeviceIdType.MESH
CORES = 2


def tree_events(order, depth):
    spans = {"x": [0, 1], "y": [0, 1], "z": [0] + [s * k for k in range(1, depth) for s in (1, -1)]}
    sides = {"x": [("x", 1)], "y": [("y", 1)], "z": [("z", 1), ("z", -1)]}
    found = []
    for offsets in itertools.product(*(spans[d] for d in order)):
        moved = [i for i, o in enumerate(offsets) if o]
        last = moved[-1] if moved else -1
        parent, children = None, []
        if moved:
            toward = 1 if offsets[last] > 0 else -1
            parent = (order[last], toward)
            if order[last] == "z":
                children.append(("z", -toward))
        for d in order[last + 1 :]:
            children += sides[d]
        found.append((sum(abs(o) for o in offsets), dict(zip(order, offsets)), parent, children))
    return found


def here(depth):
    dp, blk = lax.axis_index("dp"), lax.axis_index("blk")
    return {"y": dp // CORES, "c": lax.rem(dp, CORES), "z": blk // 2, "x": lax.rem(blk, 2)}


def device_of(pos):
    return (pos["y"] * CORES + pos["c"], pos["z"] * 2 + pos["x"])


def beside(pos, side):
    d, step = side
    moved = dict(pos)
    moved[d] = pos[d] + step if d == "z" else 1 - pos[d]
    return moved


def exists(pos, side, depth):
    if side[0] != "z":
        return None
    return pos["z"] + 1 < depth if side[1] > 0 else pos["z"] >= 1


def source_of(pos, offsets):
    moved = dict(pos)
    for d, o in offsets.items():
        if o:
            moved[d] = pos[d] + o if d == "z" else 1 - pos[d]
    return moved


def in_line(pos, offsets, depth):
    o = offsets.get("z", 0)
    if o == 0:
        return None
    return pos["z"] + o < depth if o > 0 else pos["z"] >= -o


def when(cond, body):
    if cond is None:
        body()
    else:
        pl.when(cond)(body)


def greet(pos, sides, depth):
    barrier = pltpu.get_barrier_semaphore()
    for side in sides:
        when(
            exists(pos, side, depth),
            lambda side=side: pl.semaphore_signal(
                barrier, inc=1, device_id=device_of(beside(pos, side)), device_id_type=MESH
            ),
        )
    peers = sum(1 for d, _ in sides if d != "z")
    if any(d == "z" for d, _ in sides):
        up = jnp.where(pos["z"] + 1 < depth, 1, 0)
        peers = peers + up + jnp.where(pos["z"] >= 1, 1, 0)
    pl.semaphore_wait(barrier, peers)


def schedule(flows, depth, back=False):
    events = []
    for f, flow in enumerate(flows):
        tree = tree_events(flow["order"], depth)
        most = max(e[0] for e in tree)
        for hops, offsets, parent, children in tree:
            key = flow["when"][most - hops if back else hops]
            events.append((key, f, offsets, parent, children))
    events.sort(key=lambda e: (e[0], e[1]))
    return events


def group_of(offsets):
    return tuple(sorted((d, o) for d, o in offsets.items() if d != "z"))


def flat_sides(flows):
    axes = sorted({d for flow in flows for d in flow["order"]})
    sides = [s for d in axes for s in ([("z", 1), ("z", -1)] if d == "z" else [(d, 1)])]
    return sides + ([("c", 1)] if any(flow["cores"] for flow in flows) else [])


def block(ref, flow, src):
    lead = (src["y"], src["c"], src["z"], src["x"]) if flow["cores"] else (src["z"], src["x"])
    low, wide = flow["columns"]
    return ref.at[lead + (slice(None), pl.ds(low, wide))]


def column(ref, flow, src):
    lead = (src["y"], src["c"], slice(None), src["x"]) if flow["cores"] else (slice(None), src["x"])
    low, wide = flow["columns"]
    return ref.at[lead + (slice(None), pl.ds(low, wide))]


def gather_kernel(flows, depth, n_in, n_out, work, *refs):
    ins, outs = refs[:n_in], refs[n_in : n_in + n_out]
    recv, sent, core_recv, core_sent, local = refs[n_in + n_out :]
    pos = here(depth)
    greet(pos, flat_sides(flows), depth)
    copies, waits, arrivals = {}, [], {}
    for f, flow in enumerate(flows):
        if not flow["made"]:
            low, wide = flow["in_columns"]
            own = ins[flow["in"]].at[:, pl.ds(low, wide)]
            copies[f] = pltpu.make_async_copy(own, block(outs[flow["out"]], flow, pos), local.at[f])
            copies[f].start()
    events = schedule(flows, depth)
    items = [(e[0], 0, e) for e in events]
    items += [(key, 1, step) for key, step in (work(pos, ins, outs) if work else [])]
    items.sort(key=lambda item: item[0])
    last = {}
    for i, (_, kind, e) in enumerate(items):
        if kind == 0:
            last[(e[1], group_of(e[2]))] = i
    sites = 0
    for i, (_, kind, item) in enumerate(items):
        if kind == 1:
            needed, step = item
            for f in needed:
                if f in copies:
                    copies.pop(f).wait()
                for arrival in arrivals.pop(f, []):
                    arrival.wait()
            step()
            continue
        _, f, offsets, parent, children = item
        flow = flows[f]
        src = source_of(pos, offsets)
        out = outs[flow["out"]]
        low, wide = flow["in_columns"]
        target = block(out, flow, src)
        origin = target
        if parent is None and not flow["made"]:
            origin = ins[flow["in"]].at[:, pl.ds(low, wide)]
        mark = recv.at[f, src["y"] if "y" in flow["order"] else 0, src["z"], src["x"]]
        sends = []
        for side in children:
            sends.append(
                (
                    side,
                    functools.partial(
                        pltpu.make_async_remote_copy,
                        origin,
                        target,
                        sent.at[sites],
                        mark,
                        device_id=device_of(beside(pos, side)),
                        device_id_type=MESH,
                    ),
                )
            )
            sites += 1

        def arrive():
            if parent is not None:
                pltpu.make_async_copy(target, target, mark).wait()
            for side, send in sends:
                when(exists(pos, side, depth), lambda: send().start())

        def finish(sends=sends):
            for side, send in sends:
                when(exists(pos, side, depth), lambda: send().wait_send())

        cond = in_line(pos, offsets, depth)
        when(cond, arrive)
        if sends:
            waits.append((cond, finish))
        if flow["cores"] and last[(f, group_of(offsets))] == i:
            if f in copies and not any(o for d, o in offsets.items() if d != "z"):
                copies.pop(f).wait()
            other = beside(src, ("c", 1))
            whole = column(out, flow, src)
            core = pltpu.make_async_remote_copy(
                whole,
                whole,
                core_sent.at[f, src["y"], src["x"]],
                core_recv.at[f, src["y"], src["x"]],
                device_id=device_of(beside(pos, ("c", 1))),
                device_id_type=MESH,
            )
            core.start()
            landed = column(out, flow, other)
            arrivals.setdefault(f, []).append(
                pltpu.make_async_copy(landed, landed, core_recv.at[f, src["y"], src["x"]])
            )
            waits.append((None, core.wait_send))
    for copy in copies.values():
        copy.wait()
    for some in arrivals.values():
        for arrival in some:
            arrival.wait()
    for cond, finish in waits:
        when(cond, finish)


def count_sites(flows, depth):
    return sum(len(e[4]) for e in schedule(flows, depth))


def gather(flows, depth, inputs, out_shapes, spare, collective_id, work, in_vmem, out_vmem):
    hbm = pl.BlockSpec(memory_space=pl.ANY)
    vmem = pl.BlockSpec(memory_space=pltpu.VMEM)
    n = len(flows)
    kernel = functools.partial(
        gather_kernel, flows, depth, len(inputs), len(out_shapes) + len(spare), work
    )
    return pl.pallas_call(
        kernel,
        out_shape=tuple(out_shapes),
        in_specs=[vmem if i in in_vmem else hbm for i in range(len(inputs))],
        out_specs=tuple(vmem if i in out_vmem else hbm for i in range(len(out_shapes))),
        scratch_shapes=[pltpu.VMEM(v.shape, v.dtype) for v in spare]
        + [
            pltpu.SemaphoreType.DMA((n, 2, depth, 2)),
            pltpu.SemaphoreType.DMA((count_sites(flows, depth),)),
            pltpu.SemaphoreType.DMA((n, 2, 2)),
            pltpu.SemaphoreType.DMA((n, 2, 2)),
            pltpu.SemaphoreType.DMA((n,)),
        ],
        compiler_params=pltpu.CompilerParams(
            collective_id=collective_id, has_side_effects=True, vmem_limit_bytes=62 << 20
        ),
    )(*inputs)


def slots_of(flow, d, depth):
    sizes = {"x": 2, "y": 2, "z": depth}
    before = flow["order"][: flow["order"].index(d)]
    return ([2] if d == "z" else []) + [sizes[k] for k in before] + ([depth] if d == "z" else [])


def slot(flow, d, src, side):
    before = flow["order"][: flow["order"].index(d)]
    return (
        ([0 if side > 0 else 1] if d == "z" else [])
        + [src[k] for k in before]
        + ([src["z"]] if d == "z" else [])
    )


def chunk_of(rows, columns):
    wide = 128
    while columns % (2 * wide) == 0 and rows * 2 * wide <= 12 * 1024:
        wide *= 2
    return wide


def scatter_kernel(flows, depth, n_in, n_out, n_made, work, *refs):
    ins, outs = refs[:n_in], refs[n_in : n_in + n_out]
    at = n_in + n_out
    made = refs[at : at + n_made]
    at += n_made
    mine, theirs, slots, marks = [], [], [], []
    for flow in flows:
        if flow["made"]:
            mine.append(made[flow["in"]])
        else:
            mine.append(refs[at])
            at += 1
        theirs.append(refs[at] if flow["cores"] else None)
        at += 1 if flow["cores"] else 0
        slots.append({})
        marks.append({})
        for d in flow["order"]:
            slots[-1][d], marks[-1][d] = refs[at], refs[at + 1]
            at += 2
    sent, core_recv, core_sent, local = refs[at:]
    pos = here(depth)
    greet(pos, flat_sides(flows), depth)
    events = schedule(flows, depth, True)

    def lead(flow, src):
        if not flow["cores"]:
            return (src["z"], src["x"])
        return (src["y"],) + ((src["c"],) if flow["made"] else ()) + (src["z"], src["x"])

    def col(src):
        return (src["y"], slice(None), src["x"])

    def parts(f, own, cols):
        low = flows[f]["columns"][0] if flows[f]["made"] else 0
        return own + (slice(None), pl.ds(pl.multiple_of(low + cols.start, 128), cols.size))

    ready, waits, sites = {}, [], 0

    def begin(chosen):
        for _, f, offsets, parent, children in events:
            key = (f, group_of(offsets))
            if key in ready or f not in chosen:
                continue
            flow = flows[f]
            src = source_of(pos, {d: o for d, o in offsets.items() if d != "z"})
            y = src["y"] if flow["cores"] else 0
            whole = made[flow["in"]] if flow["made"] else ins[flow["in"]]
            loads = []
            if flow["cores"]:
                core = pltpu.make_async_remote_copy(
                    column(whole, flow, beside(src, ("c", 1))),
                    theirs[f].at[col(src)],
                    core_sent.at[f, y, src["x"]],
                    core_recv.at[f, y, src["x"]],
                    device_id=device_of(beside(pos, ("c", 1))),
                    device_id_type=MESH,
                )
                core.start()
                loads.append(core.wait_recv)
                waits.append((None, core.wait_send))
            if not flow["made"]:
                copy = pltpu.make_async_copy(
                    column(whole, flow, src), mine[f].at[col(src)], local.at[f, y, src["x"]]
                )
                copy.start()
                loads.append(copy.wait)
            ready[key] = loads

    begin([f for f, flow in enumerate(flows) if not flow["made"]])
    items = [(e[0], 0, e) for e in events]
    items += [(key, 1, step) for key, step in (work(pos, ins, outs, made) if work else [])]
    items.sort(key=lambda item: item[0])
    for _, kind, item in items:
        if kind == 1:
            after, step = item
            step()
            begin(after)
            continue
        _, f, offsets, parent, children = item
        flow = flows[f]
        for load in ready.get((f, group_of(offsets)), []):
            load()
        ready[(f, group_of(offsets))] = []
        src = source_of(pos, offsets)
        own = lead(flow, src)
        send = None
        if parent is not None:
            d, toward = parent
            place = tuple(slot(flow, d, src, -toward))
            send = pltpu.make_async_remote_copy(
                mine[f].at[parts(f, own, pl.ds(0, flow["columns"][1]))],
                slots[f][d].at[place] if place else slots[f][d],
                sent.at[sites],
                marks[f][d].at[place if place else (0,)],
                device_id=device_of(beside(pos, parent)),
                device_id_type=MESH,
            )
            sites += 1

        def step():
            rows, columns = mine[f].shape[-2], flow["columns"][1]
            wide = chunk_of(rows, columns)
            terms = []
            for side in children:
                d = side[0]
                place = tuple(slot(flow, d, src, side[1]))
                buf = slots[f][d].at[place] if place else slots[f][d]
                there = exists(pos, side, depth)
                when(
                    there,
                    lambda: pltpu.make_async_copy(
                        buf, buf, marks[f][d].at[place if place else (0,)]
                    ).wait(),
                )
                terms.append((place, d, there))

            def total(cols):
                value = mine[f][parts(f, own, cols)].astype(jnp.float32)
                if flow["cores"]:
                    core = (src["y"], src["z"], src["x"], slice(None), cols)
                    value += theirs[f][core].astype(jnp.float32)
                return value

            def put(cols, value):
                if send is None:
                    low = flow["out_low"]
                    outs[flow["out"]][:, pl.ds(pl.multiple_of(low + cols.start, 128), wide)] = value
                else:
                    mine[f][parts(f, own, cols)] = value.astype(mine[f].dtype)

            def with_terms(chosen):
                def go():
                    def body(k, carry):
                        cols = pl.ds(pl.multiple_of(k * wide, wide), wide)
                        value = total(cols)
                        for place, d in chosen:
                            value += slots[f][d][place + (slice(None), cols)].astype(jnp.float32)
                        put(cols, value)
                        return carry

                    lax.fori_loop(0, columns // wide, body, 0)

                return go

            always = [(p, d) for p, d, there in terms if there is None]
            maybe = [(p, d, there) for p, d, there in terms if there is not None]
            if flow["cores"] or always or maybe:
                for picks in itertools.product((True, False), repeat=len(maybe)):
                    cond = None
                    for (p, d, there), pick in zip(maybe, picks):
                        test = there if pick else jnp.logical_not(there)
                        cond = test if cond is None else jnp.logical_and(cond, test)
                    chosen = always + [(p, d) for (p, d, _), pick in zip(maybe, picks) if pick]
                    if not chosen and not flow["cores"] and send is not None:
                        continue
                    when(cond, with_terms(chosen))
            if send is not None:
                send.start()

        cond = in_line(pos, offsets, depth)
        when(cond, step)
        if send is not None:
            waits.append((cond, send.wait_send))
    for cond, finish in waits:
        when(cond, finish)


def scatter(flows, depth, inputs, out_shapes, collective_id, work, made, in_vmem, spare):
    hbm = pl.BlockSpec(memory_space=pl.ANY)
    vmem = pl.BlockSpec(memory_space=pltpu.VMEM)
    n = len(flows)
    scratch = [pltpu.VMEM(m.shape, m.dtype) for m in made + spare]
    for flow in flows:
        source = made[flow["in"]] if flow["made"] else inputs[flow["in"]]
        rows, kind = source.shape[-2], source.dtype
        unit = (rows, flow["columns"][1])
        whole = ((2, depth, 2) if flow["cores"] else (depth, 2)) + unit
        if not flow["made"]:
            scratch.append(pltpu.VMEM(whole, kind))
        if flow["cores"]:
            scratch.append(pltpu.VMEM(whole, kind))
        for d in flow["order"]:
            places = tuple(slots_of(flow, d, depth))
            scratch.append(pltpu.VMEM(places + unit, kind))
            scratch.append(pltpu.SemaphoreType.DMA(places if places else (1,)))
    scratch += [
        pltpu.SemaphoreType.DMA((len(schedule(flows, depth)),)),
        pltpu.SemaphoreType.DMA((n, 2, 2)),
        pltpu.SemaphoreType.DMA((n, 2, 2)),
        pltpu.SemaphoreType.DMA((n, 2, 2)),
    ]
    kernel = functools.partial(
        scatter_kernel, flows, depth, len(inputs), len(out_shapes), len(made + spare), work
    )
    return pl.pallas_call(
        kernel,
        out_shape=tuple(out_shapes),
        in_specs=[vmem if i in in_vmem else hbm for i in range(len(inputs))],
        out_specs=tuple([vmem] * len(out_shapes)),
        scratch_shapes=scratch,
        compiler_params=pltpu.CompilerParams(
            collective_id=collective_id, has_side_effects=True, vmem_limit_bytes=62 << 20
        ),
    )(*inputs)


ZXY, ZYX, XZY, YZX = ("z", "x", "y"), ("z", "y", "x"), ("x", "z", "y"), ("y", "z", "x")


def flow_of(order, source, which, low, wide, place, cores=True, made=False):
    return dict(
        order=order,
        cores=cores,
        columns=(low, wide),
        in_columns=(low, wide),
        out_low=low,
        made=made,
        out=which,
        when=place,
        **{"in": source},
    )


def layout_of(large, own, split):
    dp, blk = lax.axis_size("dp"), lax.axis_size("blk")
    fits = all(v.shape[0] % 8 == 0 and v.shape[1] % 128 == 0 for v in large)
    fits = fits and large[0].shape[0] % 8 == 0 and 2 * own <= 128 and split <= 7 * 128
    if fits and dp == 2 * CORES and blk % 2 == 0 and 2 <= blk // 2 <= 4:
        return blk // 2
    return None


def flat_rows(whole):
    return whole.reshape(-1, whole.shape[-1])


def flat_rows(whole):
    return whole.reshape(-1, whole.shape[-1])


def forward_kernel(tokens, w_qkv, flat, large, depth):
    rows, width = tokens.shape
    n, own, high = 4 * CORES * depth, w_qkv.shape[0], flat.shape[0]
    bf16, f32 = jnp.bfloat16, jnp.float32
    column_of = np.arange(3 * width)
    lane = column_of % width % own + np.where(column_of >= 2 * width, own, 0)
    lanes = (np.arange(128)[:, None] == lane) & (column_of // width != 1)
    place = (np.arange(n)[:, None] == column_of % width // own).astype(np.float32)
    pick = np.arange(n)[:, None] * high == np.arange(n * high)

    def work(pos, ins, outs):
        pick_ref, lanes_ref, place_ref = ins[-3:]
        small, every, dense, kv_ref, q_ref, attn_ref, lse_ref, blocks = outs[3:]

        def unpack():
            for k in range(3):
                at = pl.ds(k * width, width)
                part = blocks[:, :, :, :, :, at].astype(f32).reshape(width, width)
                dense[:, at] = part.astype(bf16)

        def project():
            first = jnp.dot(
                pick_ref[...], small[...].reshape(n * high, 128), preferred_element_type=f32
            )
            first = jnp.dot(first.astype(bf16), lanes_ref[...], preferred_element_type=f32)
            bias = jnp.sum(first * place_ref[...], axis=0, keepdims=True)
            mine = every[pos["z"], pos["x"]]
            query = jnp.dot(mine, dense[:, :width], preferred_element_type=f32)
            q_ref[...] = (query + bias[:, :width]).astype(bf16)
            later = bias[:, width:]

            def line(z, carry):
                some = every[z].reshape(2 * rows, width)
                part = jnp.dot(some, dense[:, width:], preferred_element_type=f32) + later
                kv_ref[z] = part.astype(bf16).reshape(2, rows, 2 * width)
                return carry

            lax.fori_loop(0, depth, line, 0)

        def keys_of(at):
            return kv_ref[:, :, :, at].reshape(-1, PAIR)

        pair = functools.partial(attend_pair, width, q_ref, keys_of, attn_ref, lse_ref)
        steps = in_steps(width // PAIR, len(ATTEND), pair)
        found = [(UNPACK, ((0,), unpack)), (PROJECT, ((1, 2), project))]
        return found + [(key, ((), step)) for key, step in zip(ATTEND, steps)]

    shapes = whole_shapes(list(large) + [flat], depth) + [
        jax.ShapeDtypeStruct((depth, 2, rows, width), bf16),
        jax.ShapeDtypeStruct((width, 3 * width), bf16),
        jax.ShapeDtypeStruct((depth, 2, rows, 2 * width), bf16),
        jax.ShapeDtypeStruct((rows, width), bf16),
    ]
    shapes += list(attend_shapes(rows, width))
    inputs = [w_qkv, flat, tokens] + list(large)
    flows = [
        flow_of(GATHER_ORDERS[0], 0, len(shapes), 0, 3 * width, FIRST),
        flow_of(GATHER_ORDERS[1], 1, 3, 0, 128, FIRST),
        flow_of(("z", "x"), 2, 4, 0, width, FIRST, cores=False),
    ]
    for i, (order, v) in enumerate(zip(GATHER_ORDERS[2:], large)):
        flows.append(flow_of(order, 3 + i, i, 0, v.shape[1], LATER))
    inputs += [jnp.asarray(v, bf16) for v in (pick, lanes)] + [jnp.asarray(place)]
    return gather(
        flows,
        depth,
        inputs,
        shapes,
        whole_shapes([w_qkv], depth),
        1,
        work,
        in_vmem=range(len(inputs) - 3, len(inputs)),
        out_vmem=range(3, len(shapes)),
    )


GATHER_ORDERS = (ZXY, ZYX, ZXY, XZY, YZX)
FIRST, LATER = (0, 1, 2, 3, 4, 5), (0.1, 1.6, 3.1, 4.6, 6.1, 7.6)
UNPACK, PROJECT, ATTEND = 5.1, 5.2, (6.2, 6.7, 7.7)
SCATTER_ORDERS = (ZXY, XZY, YZX, ZXY, ZYX)
BACK, EARLY = (0, 1.5, 2.5), (1.1, 2.1, 3.1, 4.1, 5.1, 6.1)
WEIGHTS, TOKENS, LAST = 2.6, 2.7, (3.2, 4.2, 5.2, 6.2, 7.2, 8.2)


def whole_shapes(large, depth):
    return [jax.ShapeDtypeStruct((2, CORES, depth, 2) + v.shape, v.dtype) for v in large]


def backward_kernel(query, kv, d_attn, lse, delta, every, dense, small, grads, large, depth):
    bf16, f32 = jnp.bfloat16, jnp.float32
    rows, width = query.shape
    n = 4 * CORES * depth
    own = width // n
    column_of = np.arange(width)
    line = np.arange(8 * n)[:, None]
    place = (line % 8 == 7) & (line // 8 == column_of // own)
    lanes = [column_of[:, None] % own + shift == np.arange(128) for shift in (0, own)]

    def work(pos, ins, outs, made):
        q_ref, kv_ref, do_ref, lse_ref, delta_ref, every_ref, w_ref, small_ref = ins[-11:-3]
        place_ref, query_lanes, value_lanes = ins[-3:]
        token_part, d_whole, small_made, dq_ref, dkv_ref, sum_ref = made

        def keys_of(at):
            return kv_ref[:, :, :, at].reshape(-1, PAIR)

        def put_keys(at, value):
            dkv_ref[:, at] = value.astype(bf16)

        def put_values(at, val, value):
            sum_ref[:, at] = jnp.sum(value, axis=0, keepdims=True)
            dkv_ref[:, val] = value.astype(bf16)

        pair = functools.partial(
            attend_back_pair,
            width,
            q_ref,
            keys_of,
            do_ref,
            lse_ref,
            delta_ref,
            dq_ref,
            put_keys,
            put_values,
        )

        def weights():
            whole = every_ref[...].reshape(-1, width)
            for k in range(3):
                if k == 0:
                    part = contract_rows(every_ref[pos["z"], pos["x"]], dq_ref[...].astype(bf16))
                else:
                    part = contract_rows(whole, dkv_ref[:, (k - 1) * width : k * width])
                part = part.reshape(2, CORES, depth, 2, own, width).astype(bf16)
                d_whole[:, :, :, :, :, k * width : (k + 1) * width] = part
            sums = jnp.zeros((8 * n, 128), f32)
            query_sum = jnp.sum(dq_ref[...], axis=0, keepdims=True)
            for value, lane in ((query_sum, query_lanes), (sum_ref[...], value_lanes)):
                sums += jnp.dot(
                    place_ref[...] * value,
                    lane[...],
                    preferred_element_type=f32,
                    precision=lax.Precision.HIGHEST,
                )
            small_made[...] = small_ref[...] + sums.reshape(small_ref.shape)

        def tokens_gradient():
            def line(z, carry):
                at = pl.ds(pl.multiple_of(z * 2 * rows, 2 * rows), 2 * rows)
                part = contract_cols(dkv_ref[at, :], w_ref[:, width:])
                token_part[z] = part.astype(bf16).reshape(2, rows, width)
                return carry

            lax.fori_loop(0, depth, line, 0)
            outs[-1][...] = contract_cols(dq_ref[...].astype(bf16), w_ref[:, :width])

        steps = in_steps(width // PAIR, len(BACK), pair)
        found = [(key, ((), step)) for key, step in zip(BACK, steps)]
        return found + [(WEIGHTS, ((3, 4), weights)), (TOKENS, ((5,), tokens_gradient))]

    blocks = [g.reshape((2, CORES, depth, 2) + v.shape) for g, v in zip(grads, large)]
    made = [
        jax.ShapeDtypeStruct(every.shape, bf16),
        jax.ShapeDtypeStruct((2, CORES, depth, 2, own, 3 * width), bf16),
        jax.ShapeDtypeStruct(small.shape, f32),
    ]
    spare = [
        jax.ShapeDtypeStruct((rows, width), f32),
        jax.ShapeDtypeStruct((2 * depth * rows, 2 * width), bf16),
        jax.ShapeDtypeStruct((1, width), f32),
    ]
    flows = []
    for i, (order, v) in enumerate(zip(SCATTER_ORDERS, large)):
        flows.append(flow_of(order, i, i, 0, v.shape[1], EARLY))
    flows.append(flow_of(SCATTER_ORDERS[3], 1, 3, 0, 3 * width, LAST, made=True))
    flows.append(flow_of(SCATTER_ORDERS[4], 2, 4, 0, 128, LAST, made=True))
    flows.append(flow_of(("z", "x"), 0, 5, 0, width, LAST, cores=False, made=True))
    shapes = [jax.ShapeDtypeStruct(v.shape, f32) for v in large]
    shapes += [
        jax.ShapeDtypeStruct((own, 3 * width), f32),
        jax.ShapeDtypeStruct(small.shape[-2:], f32),
        jax.ShapeDtypeStruct((rows, width), f32),
        jax.ShapeDtypeStruct((rows, width), f32),
    ]
    inputs = blocks + [query, kv, d_attn, lse, delta, every, dense, small]
    inputs += [jnp.asarray(v, f32) for v in [place] + lanes]
    return scatter(
        flows, depth, inputs, shapes, 2, work, made, range(len(blocks), len(inputs)), spare
    )


SPARE = 16


def split_owner(full, count):
    p = full.shape[0]
    return full.reshape(p, count, -1).transpose(1, 0, 2).reshape(count, -1)


def join_owner(parts, p):
    count = parts.shape[0]
    return parts.reshape(count, p, -1).transpose(1, 0, 2).reshape(p, -1)


def plain_on_device(
    tokens,
    w_qkv,
    qv_bias,
    w_out,
    out_bias,
    norm_gain,
    norm_bias,
    w_up,
    up_bias,
    w_down,
    down_bias,
    cotangent,
):
    f32 = jnp.float32
    bf16 = jnp.bfloat16
    rows, width = tokens.shape
    heads = width // HEAD
    n = lax.axis_size("dp") * lax.axis_size("blk")
    small = [qv_bias, out_bias, norm_gain, norm_bias, up_bias, down_bias]
    sizes = [v.size for v in small]
    flat = jnp.concatenate([v.reshape(-1) for v in small])
    flat = jnp.pad(flat, (0, SPARE * width - flat.size)).reshape(SPARE, width)
    large = [w_qkv, w_out, w_up, w_down]
    shard = jnp.concatenate(
        [v[:, i : i + width] for v in large for i in range(0, v.shape[1], width)] + [flat]
    )
    packed = lax.all_gather(shard, ("dp", "blk"), axis=0)
    wholes, at = [], 0
    for v in large:
        high, columns = v.shape
        blocks = []
        for _ in range(columns // width):
            blocks.append(packed[:, at : at + high].reshape(n * high, width))
            at += high
        wholes.append(jnp.concatenate(blocks, axis=1))
    wq_full, wo_full, wu_full, wd_full = wholes
    row_full = packed[:, at:].reshape(n, -1)
    parts, at = [], 0
    for size, v in zip(sizes, small):
        parts.append(join_owner(row_full[:, at : at + size], 2 if v.ndim == 2 else 1))
        at += size
    qvb_full, bo_full, gain_full, shift_full, bu_full, bd_full = parts
    bo_full, bu_full, bd_full = bo_full[0], bu_full[0], bd_full[0]
    norm_gain_pair = gain_full.astype(f32)
    norm_offset_pair = shift_full.astype(f32)
    qvb = qvb_full.astype(f32)
    bias_row = jnp.concatenate([qvb[0], jnp.zeros((width,), f32), qvb[1]])
    qkv = (jnp.dot(tokens, wq_full, preferred_element_type=f32) + bias_row).astype(bf16)
    query = qkv[:, :width]
    kv = lax.all_gather(qkv[:, width:], "blk", axis=0, tiled=True)
    attn, lse = attend(query, kv)
    first_hidden = (
        tokens.astype(f32)
        + jnp.dot(attn, wo_full, preferred_element_type=f32)
        + bo_full.astype(f32)
    )
    first_norm_output, first_normalized, first_inverse_deviation = layernorm_forward(
        first_hidden, norm_gain_pair[0], norm_offset_pair[0]
    )
    y1_low = first_norm_output.astype(bf16)
    up = jnp.dot(y1_low, wu_full, preferred_element_type=f32) + bu_full.astype(f32)
    act = jax.nn.gelu(up, approximate=False).astype(bf16)
    second_hidden = (
        first_norm_output + jnp.dot(act, wd_full, preferred_element_type=f32) + bd_full.astype(f32)
    )
    output_float, second_normalized, second_inverse_deviation = layernorm_forward(
        second_hidden, norm_gain_pair[1], norm_offset_pair[1]
    )
    output = output_float.astype(bf16)
    wq_b, wo_b, wu_b, wd_b = wq_full, wo_full, wu_full, wd_full
    gain_pair_block = norm_gain_pair
    incoming_gradient = cotangent.astype(f32)
    second_gain_gradient = jnp.sum(incoming_gradient * second_normalized, axis=0)
    d_shift2 = jnp.sum(incoming_gradient, axis=0)
    second_hidden_gradient = layernorm_backward(
        incoming_gradient, second_normalized, second_inverse_deviation, gain_pair_block[1]
    )
    dh2_low = second_hidden_gradient.astype(bf16)
    d_w_down = contract_rows(act, dh2_low)
    d_down_bias = jnp.sum(second_hidden_gradient, axis=0)
    d_up_f = contract_cols(dh2_low, wd_b) * gelu_grad(up)
    d_up_bias = jnp.sum(d_up_f, axis=0)
    d_up = d_up_f.astype(bf16)
    d_w_up = contract_rows(y1_low, d_up)
    first_output_gradient = second_hidden_gradient + contract_cols(d_up, wu_b)
    first_gain_gradient = jnp.sum(first_output_gradient * first_normalized, axis=0)
    d_shift1 = jnp.sum(first_output_gradient, axis=0)
    first_hidden_gradient = layernorm_backward(
        first_output_gradient, first_normalized, first_inverse_deviation, gain_pair_block[0]
    )
    dh1_low = first_hidden_gradient.astype(bf16)
    d_w_out = contract_rows(attn, dh1_low)
    d_out_bias = jnp.sum(first_hidden_gradient, axis=0)
    d_gains = jnp.stack([first_gain_gradient, second_gain_gradient])
    d_shifts = jnp.stack([d_shift1, d_shift2])
    d_attn = contract_cols(dh1_low, wo_b).astype(bf16)
    delta = jnp.sum((d_attn.astype(f32) * attn.astype(f32)).reshape(rows, heads, HEAD), axis=-1).T
    d_query, d_kv_all = attend_back(
        query, kv, d_attn, lse.transpose(0, 2, 1), delta.reshape(heads // 2, 2, rows)
    )
    d_kv = lax.psum_scatter(d_kv_all, "blk", scatter_dimension=0, tiled=True).astype(f32)
    d_key = d_kv[:, :width]
    d_value = d_kv[:, width:]
    d_qv = jnp.stack([jnp.sum(d_query, axis=0), jnp.sum(d_value, axis=0)])
    d_qkv = jnp.concatenate([d_query, d_key, d_value], axis=1).astype(bf16)
    d_w_qkv = contract_rows(tokens, d_qkv)
    d_tokens = first_hidden_gradient + contract_cols(d_qkv, wq_b)
    grads = [d_qv, d_out_bias[None], d_gains, d_shifts, d_up_bias[None], d_down_bias[None]]
    row = jnp.concatenate([split_owner(v, n) for v in grads], axis=1)
    row = jnp.pad(row, ((0, 0), (0, SPARE * width - row.shape[1]))).reshape(n, SPARE, width)
    blocks = []
    for d_full, v in zip((d_w_qkv, d_w_out, d_w_up, d_w_down), large):
        d_low = d_full.astype(bf16).reshape((n,) + v.shape)
        blocks += [d_low[:, :, i : i + width] for i in range(0, v.shape[1], width)]
    packed = jnp.concatenate(blocks + [row.astype(bf16)], axis=1)
    packed = lax.psum_scatter(packed, ("dp", "blk"), scatter_dimension=0, tiled=True)[0]
    wholes, at = [], 0
    for v in large:
        high, columns = v.shape
        blocks = []
        for _ in range(columns // width):
            blocks.append(packed[at : at + high])
            at += high
        wholes.append(jnp.concatenate(blocks, axis=1).astype(f32))
    g_wqkv, g_wout, g_wup, g_wdown = wholes
    row, at, parts = packed[at:].reshape(-1).astype(f32), 0, []
    for size, v in zip(sizes, small):
        parts.append(row[at : at + size].reshape(v.shape))
        at += size
    g_qv, g_bout, g_gain, g_shift, g_bup, g_bdown = parts
    return (
        output,
        d_tokens,
        g_wqkv,
        g_qv,
        g_wout,
        g_bout,
        g_gain,
        g_shift,
        g_wup,
        g_bup,
        g_wdown,
        g_bdown,
    )


def on_device(
    tokens,
    w_qkv,
    qv_bias,
    w_out,
    out_bias,
    norm_gain,
    norm_bias,
    w_up,
    up_bias,
    w_down,
    down_bias,
    cotangent,
):
    f32 = jnp.float32
    bf16 = jnp.bfloat16
    rows, width = tokens.shape
    heads = width // HEAD
    n = lax.axis_size("dp") * lax.axis_size("blk")
    own = out_bias.shape[0]
    split = 8 * own + up_bias.size
    depth = layout_of([w_qkv, w_out, w_up, w_down], own, split)
    if depth is None:
        return plain_on_device(
            tokens,
            w_qkv,
            qv_bias,
            w_out,
            out_bias,
            norm_gain,
            norm_bias,
            w_up,
            up_bias,
            w_down,
            down_bias,
            cotangent,
        )
    large = [w_out, w_up, w_down]
    narrow = jnp.concatenate([qv_bias, out_bias[None], norm_gain, norm_bias, down_bias[None]])
    flat = jnp.concatenate([narrow.reshape(-1), up_bias])
    high = -(-split // 2048) * 16
    flat = jnp.pad(flat, (0, high * 128 - split)).reshape(high, 128)
    wo_full, wu_full, wd_full, gathered, every, dense, kv, query, attn, lse = forward_kernel(
        tokens, w_qkv, flat, large, depth
    )
    wo_full, wu_full, wd_full = flat_rows(wo_full), flat_rows(wu_full), flat_rows(wd_full)
    gathered = gathered.astype(f32).reshape(n, -1)
    narrow_full = gathered[:, : 8 * own].reshape(n, 8, own).transpose(1, 0, 2).reshape(8, width)
    bu_full = gathered[:, 8 * own : split].reshape(-1)
    bo_full, norm_gain_pair = narrow_full[2], narrow_full[3:5]
    norm_offset_pair, bd_full = narrow_full[5:7], narrow_full[7]
    first_hidden = (
        tokens.astype(f32)
        + jnp.dot(attn, wo_full, preferred_element_type=f32)
        + bo_full
    )
    first_norm_output, first_normalized, first_inverse_deviation = layernorm_forward(
        first_hidden, norm_gain_pair[0], norm_offset_pair[0]
    )
    y1_low = first_norm_output.astype(bf16)
    up = jnp.dot(y1_low, wu_full, preferred_element_type=f32) + bu_full
    act = jax.nn.gelu(up, approximate=False).astype(bf16)
    second_hidden = (
        first_norm_output + jnp.dot(act, wd_full, preferred_element_type=f32) + bd_full
    )
    output_float, second_normalized, second_inverse_deviation = layernorm_forward(
        second_hidden, norm_gain_pair[1], norm_offset_pair[1]
    )
    output = output_float.astype(bf16)
    wo_b, wu_b, wd_b = wo_full, wu_full, wd_full
    gain_pair_block = norm_gain_pair
    incoming_gradient = cotangent.astype(f32)
    second_gain_gradient = jnp.sum(incoming_gradient * second_normalized, axis=0)
    d_shift2 = jnp.sum(incoming_gradient, axis=0)
    second_hidden_gradient = layernorm_backward(
        incoming_gradient, second_normalized, second_inverse_deviation, gain_pair_block[1]
    )
    dh2_low = second_hidden_gradient.astype(bf16)
    d_w_down = contract_rows(act, dh2_low)
    d_down_bias = jnp.sum(second_hidden_gradient, axis=0)
    d_up_f = contract_cols(dh2_low, wd_b) * gelu_grad(up)
    d_up_bias = jnp.sum(d_up_f, axis=0)
    d_up = d_up_f.astype(bf16)
    d_w_up = contract_rows(y1_low, d_up)
    first_output_gradient = second_hidden_gradient + contract_cols(d_up, wu_b)
    first_gain_gradient = jnp.sum(first_output_gradient * first_normalized, axis=0)
    d_shift1 = jnp.sum(first_output_gradient, axis=0)
    first_hidden_gradient = layernorm_backward(
        first_output_gradient, first_normalized, first_inverse_deviation, gain_pair_block[0]
    )
    dh1_low = first_hidden_gradient.astype(bf16)
    d_w_out = contract_rows(attn, dh1_low)
    d_out_bias = jnp.sum(first_hidden_gradient, axis=0)
    d_gains = jnp.stack([first_gain_gradient, second_gain_gradient])
    d_shifts = jnp.stack([d_shift1, d_shift2])
    d_attn = contract_cols(dh1_low, wo_b).astype(bf16)
    delta = jnp.sum((d_attn.astype(f32) * attn.astype(f32)).reshape(rows, heads, HEAD), axis=-1).T
    rows_of_8 = jnp.concatenate(
        [
            jnp.zeros((2, width), f32),
            d_out_bias[None],
            d_gains,
            d_shifts,
            d_down_bias[None],
        ]
    )
    row = jnp.concatenate(
        [
            rows_of_8.reshape(8, n, own).transpose(1, 0, 2).reshape(n, 8 * own),
            d_up_bias.reshape(n, -1),
        ],
        axis=1,
    )
    row = jnp.pad(row, ((0, 0), (0, 8 * 128 - split))).reshape(2, CORES, depth, 2, 8, 128)
    g_wout, g_wup, g_wdown, g_wqkv, row, token_sum, query_part = backward_kernel(
        query,
        kv,
        d_attn,
        lse.transpose(0, 2, 1),
        delta.reshape(heads // 2, 2, rows),
        every,
        dense,
        row,
        [d.astype(bf16) for d in (d_w_out, d_w_up, d_w_down)],
        large,
        depth,
    )
    d_tokens = first_hidden_gradient + query_part + token_sum
    g_qv = row[7, : 2 * own].reshape(2, own)
    row = row.reshape(-1)
    row8 = row[: 8 * own].reshape(8, own)
    g_bout, g_gain = row8[2], row8[3:5]
    g_shift, g_bdown, g_bup = row8[5:7], row8[7], row[8 * own : split]
    return (
        output,
        d_tokens,
        g_wqkv,
        g_qv,
        g_wout,
        g_bout,
        g_gain,
        g_shift,
        g_wup,
        g_bup,
        g_wdown,
        g_bdown,
    )


def solution(mesh):
    return jax.shard_map(
        on_device,
        mesh=mesh,
        in_specs=(
            P(("dp", "blk"), None),
            P(("dp", "blk"), None),
            P(None, ("dp", "blk")),
            P(("dp", "blk"), None),
            P(("dp", "blk")),
            P(None, ("dp", "blk")),
            P(None, ("dp", "blk")),
            P(("dp", "blk"), None),
            P(("dp", "blk")),
            P(("dp", "blk"), None),
            P(("dp", "blk")),
            P(("dp", "blk"), None),
        ),
        out_specs=(
            P(("dp", "blk"), None),
            P(("dp", "blk"), None),
            P(("dp", "blk"), None),
            P(None, ("dp", "blk")),
            P(("dp", "blk"), None),
            P(("dp", "blk")),
            P(None, ("dp", "blk")),
            P(None, ("dp", "blk")),
            P(("dp", "blk"), None),
            P(("dp", "blk")),
            P(("dp", "blk"), None),
            P(("dp", "blk")),
        ),
        check_vma=False,
    )
```

```python
import functools
import itertools

import jax
import jax.numpy as jnp
import numpy as np
from jax import lax
from jax.experimental import pallas as pl
from jax.experimental.pallas import tpu as pltpu
from jax.sharding import PartitionSpec as P

HEAD = 64


EPS = 1e-05
SCALE = 0.125


def layernorm_forward(h, norm_gain_vector, norm_offset):
    row_average = jnp.mean(h, axis=-1, keepdims=True)
    centered_input = h - row_average
    var = jnp.mean(centered_input * centered_input, axis=-1, keepdims=True)
    inverse_deviation = lax.rsqrt(var + EPS)
    normalized_input = centered_input * inverse_deviation
    return (normalized_input * norm_gain_vector + norm_offset, normalized_input, inverse_deviation)


def layernorm_backward(incoming_gradient, normalized_input, inverse_deviation, norm_gain_vector):
    scaled_values = incoming_gradient * norm_gain_vector
    return inverse_deviation * (
        scaled_values
        - jnp.mean(scaled_values, axis=-1, keepdims=True)
        - normalized_input * jnp.mean(scaled_values * normalized_input, axis=-1, keepdims=True)
    )


def gelu_grad(up):
    cdf = 0.5 * (1.0 + jax.scipy.special.erf(up * 0.7071067811865476))
    return cdf + up * jnp.exp(-0.5 * up * up) * 0.3989422804014327


def contract_rows(left, right):
    return lax.dot_general(
        left, right, (((0,), (0,)), ((), ())), preferred_element_type=jnp.float32
    )


def contract_cols(left, right):
    return lax.dot_general(
        left, right, (((1,), (1,)), ((), ())), preferred_element_type=jnp.float32
    )


PAIR = 2 * HEAD


def attend_pair(width, q_ref, keys_of, attn_ref, lse_ref, i):
    at = pl.ds(pl.multiple_of(i * PAIR, PAIR), PAIR)
    q2 = q_ref[:, at]
    k2 = keys_of(at)
    v2 = keys_of(pl.ds(pl.multiple_of(width + i * PAIR, PAIR), PAIR))
    outs, logs = [], []
    for j in range(2):
        own = slice(j * HEAD, (j + 1) * HEAD)
        scores = contract_cols(q2[:, own], k2[:, own]) * SCALE
        peak = jnp.max(scores, axis=1, keepdims=True)
        weights = jnp.exp(scores - peak)
        total = jnp.sum(weights, axis=1, keepdims=True)
        part = jnp.dot(
            weights.astype(jnp.bfloat16), v2[:, own], preferred_element_type=jnp.float32
        )
        outs.append((part / total).astype(jnp.bfloat16))
        logs.append(peak + jnp.log(total))
    attn_ref[:, at] = jnp.concatenate(outs, axis=1)
    lse_ref[i] = jnp.concatenate(logs, axis=1)


def attend_back_pair(
    width, q_ref, keys_of, do_ref, lse_of, delta_of, dq_ref, put_keys, put_values, i
):
    at = pl.ds(pl.multiple_of(i * PAIR, PAIR), PAIR)
    val = pl.ds(pl.multiple_of(width + i * PAIR, PAIR), PAIR)
    q2 = q_ref[:, at]
    do2 = do_ref[:, at]
    k2 = keys_of(at)
    v2 = keys_of(val)
    dqs, dks, dvs = [], [], []
    for j in range(2):
        own = slice(j * HEAD, (j + 1) * HEAD)
        q_h, do_h, k_h, v_h = q2[:, own], do2[:, own], k2[:, own], v2[:, own]
        scores = contract_cols(k_h, q_h) * SCALE
        probs = jnp.exp(scores - lse_of(j))
        dprobs = contract_cols(v_h, do_h)
        dscores = (probs * (dprobs - delta_of(j))).astype(jnp.bfloat16)
        dqs.append(SCALE * contract_rows(dscores, k_h))
        dks.append(SCALE * jnp.dot(dscores, q_h, preferred_element_type=jnp.float32))
        dvs.append(jnp.dot(probs.astype(jnp.bfloat16), do_h, preferred_element_type=jnp.float32))
    dq_ref[:, at] = jnp.concatenate(dqs, axis=1)
    put_keys(at, jnp.concatenate(dks, axis=1))
    put_values(at, val, jnp.concatenate(dvs, axis=1))


def attend_kernel(width, q_ref, kv_ref, attn_ref, lse_ref):
    def pair(i, carry):
        attend_pair(width, q_ref, lambda at: kv_ref[:, at], attn_ref, lse_ref, i)
        return carry

    lax.fori_loop(0, width // PAIR, pair, 0)


def attend(query, kv):
    rows, width = query.shape
    vmem = pl.BlockSpec(memory_space=pltpu.VMEM)
    return pl.pallas_call(
        functools.partial(attend_kernel, width),
        out_shape=attend_shapes(rows, width),
        in_specs=[vmem] * 2,
        out_specs=(vmem, vmem),
        compiler_params=pltpu.CompilerParams(vmem_limit_bytes=60 << 20),
    )(query, kv)


def attend_shapes(rows, width):
    return (
        jax.ShapeDtypeStruct((rows, width), jnp.bfloat16),
        jax.ShapeDtypeStruct((width // PAIR, rows, 2), jnp.float32),
    )


def attend_back_kernel(width, q_ref, kv_ref, do_ref, lse_ref, delta_ref, dq_ref, dkv_ref):
    def put(at, value):
        dkv_ref[:, at] = value.astype(jnp.bfloat16)

    def pair(i, carry):
        attend_back_pair(
            width,
            q_ref,
            lambda at: kv_ref[:, at],
            do_ref,
            lambda k: lse_ref[i, k : k + 1],
            lambda k: delta_ref[i, k : k + 1],
            dq_ref,
            put,
            lambda at, val, value: put(val, value),
            i,
        )
        return carry

    lax.fori_loop(0, width // PAIR, pair, 0)


def attend_back(query, kv, d_attn, lse, delta):
    rows, width = query.shape
    vmem = pl.BlockSpec(memory_space=pltpu.VMEM)
    return pl.pallas_call(
        functools.partial(attend_back_kernel, width),
        out_shape=(
            jax.ShapeDtypeStruct((rows, width), jnp.float32),
            jax.ShapeDtypeStruct(kv.shape, jnp.bfloat16),
        ),
        in_specs=[vmem] * 5,
        out_specs=(vmem, vmem),
        compiler_params=pltpu.CompilerParams(vmem_limit_bytes=60 << 20),
    )(query, kv, d_attn, lse, delta)


def in_steps(pairs, steps, pair):
    bounds = [pairs * k // steps for k in range(steps + 1)]

    def step(low, high):
        def body(i, carry):
            pair(i)
            return carry

        lax.fori_loop(low, high, body, 0)

    return [functools.partial(step, lo, hi) for lo, hi in zip(bounds, bounds[1:])]


MESH = pl.DeviceIdType.MESH
CORES = 2


def tree_events(order, depth):
    spans = {"x": [0, 1], "y": [0, 1], "z": [0] + [s * k for k in range(1, depth) for s in (1, -1)]}
    sides = {"x": [("x", 1)], "y": [("y", 1)], "z": [("z", 1), ("z", -1)]}
    found = []
    for offsets in itertools.product(*(spans[d] for d in order)):
        moved = [i for i, o in enumerate(offsets) if o]
        last = moved[-1] if moved else -1
        parent, children = None, []
        if moved:
            toward = 1 if offsets[last] > 0 else -1
            parent = (order[last], toward)
            if order[last] == "z":
                children.append(("z", -toward))
        for d in order[last + 1 :]:
            children += sides[d]
        found.append((sum(abs(o) for o in offsets), dict(zip(order, offsets)), parent, children))
    return found


def here(depth):
    dp, blk = lax.axis_index("dp"), lax.axis_index("blk")
    return {"y": dp // CORES, "c": lax.rem(dp, CORES), "z": blk // 2, "x": lax.rem(blk, 2)}


def device_of(pos):
    return (pos["y"] * CORES + pos["c"], pos["z"] * 2 + pos["x"])


def beside(pos, side):
    d, step = side
    moved = dict(pos)
    moved[d] = pos[d] + step if d == "z" else 1 - pos[d]
    return moved


def exists(pos, side, depth):
    if side[0] != "z":
        return None
    return pos["z"] + 1 < depth if side[1] > 0 else pos["z"] >= 1


def source_of(pos, offsets):
    moved = dict(pos)
    for d, o in offsets.items():
        if o:
            moved[d] = pos[d] + o if d == "z" else 1 - pos[d]
    return moved


def in_line(pos, offsets, depth):
    o = offsets.get("z", 0)
    if o == 0:
        return None
    return pos["z"] + o < depth if o > 0 else pos["z"] >= -o


def when(cond, body):
    if cond is None:
        body()
    else:
        pl.when(cond)(body)


def greet(pos, sides, depth):
    barrier = pltpu.get_barrier_semaphore()
    for side in sides:
        when(
            exists(pos, side, depth),
            lambda side=side: pl.semaphore_signal(
                barrier, inc=1, device_id=device_of(beside(pos, side)), device_id_type=MESH
            ),
        )
    peers = sum(1 for d, _ in sides if d != "z")
    if any(d == "z" for d, _ in sides):
        up = jnp.where(pos["z"] + 1 < depth, 1, 0)
        peers = peers + up + jnp.where(pos["z"] >= 1, 1, 0)
    pl.semaphore_wait(barrier, peers)


def schedule(flows, depth, back=False):
    events = []
    for f, flow in enumerate(flows):
        tree = tree_events(flow["order"], depth)
        most = max(e[0] for e in tree)
        for hops, offsets, parent, children in tree:
            key = flow["when"][most - hops if back else hops]
            events.append((key, f, offsets, parent, children))
    events.sort(key=lambda e: (e[0], e[1]))
    return events


def group_of(offsets):
    return tuple(sorted((d, o) for d, o in offsets.items() if d != "z"))


def flat_sides(flows):
    axes = sorted({d for flow in flows for d in flow["order"]})
    sides = [s for d in axes for s in ([("z", 1), ("z", -1)] if d == "z" else [(d, 1)])]
    return sides + ([("c", 1)] if any(flow["cores"] for flow in flows) else [])


def block(ref, flow, src):
    lead = (src["y"], src["c"], src["z"], src["x"]) if flow["cores"] else (src["z"], src["x"])
    low, wide = flow["columns"]
    return ref.at[lead + (slice(None), pl.ds(low, wide))]


def column(ref, flow, src):
    lead = (src["y"], src["c"], slice(None), src["x"]) if flow["cores"] else (slice(None), src["x"])
    low, wide = flow["columns"]
    return ref.at[lead + (slice(None), pl.ds(low, wide))]


def gather_kernel(flows, depth, n_in, n_out, work, *refs):
    ins, outs = refs[:n_in], refs[n_in : n_in + n_out]
    recv, sent, core_recv, core_sent, local = refs[n_in + n_out :]
    pos = here(depth)
    greet(pos, flat_sides(flows), depth)
    copies, waits, arrivals = {}, [], {}
    for f, flow in enumerate(flows):
        if not flow["made"]:
            low, wide = flow["in_columns"]
            own = ins[flow["in"]].at[:, pl.ds(low, wide)]
            copies[f] = pltpu.make_async_copy(own, block(outs[flow["out"]], flow, pos), local.at[f])
            copies[f].start()
    events = schedule(flows, depth)
    items = [(e[0], 0, e) for e in events]
    items += [(key, 1, step) for key, step in (work(pos, ins, outs) if work else [])]
    items.sort(key=lambda item: item[0])
    last = {}
    for i, (_, kind, e) in enumerate(items):
        if kind == 0:
            last[(e[1], group_of(e[2]))] = i
    sites = 0
    for i, (_, kind, item) in enumerate(items):
        if kind == 1:
            needed, step = item
            for f in needed:
                if f in copies:
                    copies.pop(f).wait()
                for arrival in arrivals.pop(f, []):
                    arrival.wait()
            step()
            continue
        _, f, offsets, parent, children = item
        flow = flows[f]
        src = source_of(pos, offsets)
        out = outs[flow["out"]]
        low, wide = flow["in_columns"]
        target = block(out, flow, src)
        origin = target
        if parent is None and not flow["made"]:
            origin = ins[flow["in"]].at[:, pl.ds(low, wide)]
        mark = recv.at[f, src["y"] if "y" in flow["order"] else 0, src["z"], src["x"]]
        sends = []
        for side in children:
            sends.append(
                (
                    side,
                    functools.partial(
                        pltpu.make_async_remote_copy,
                        origin,
                        target,
                        sent.at[sites],
                        mark,
                        device_id=device_of(beside(pos, side)),
                        device_id_type=MESH,
                    ),
                )
            )
            sites += 1

        def arrive():
            if parent is not None:
                pltpu.make_async_copy(target, target, mark).wait()
            for side, send in sends:
                when(exists(pos, side, depth), lambda: send().start())

        def finish(sends=sends):
            for side, send in sends:
                when(exists(pos, side, depth), lambda: send().wait_send())

        cond = in_line(pos, offsets, depth)
        when(cond, arrive)
        if sends:
            waits.append((cond, finish))
        if flow["cores"] and last[(f, group_of(offsets))] == i:
            if f in copies and not any(o for d, o in offsets.items() if d != "z"):
                copies.pop(f).wait()
            other = beside(src, ("c", 1))
            whole = column(out, flow, src)
            core = pltpu.make_async_remote_copy(
                whole,
                whole,
                core_sent.at[f, src["y"], src["x"]],
                core_recv.at[f, src["y"], src["x"]],
                device_id=device_of(beside(pos, ("c", 1))),
                device_id_type=MESH,
            )
            core.start()
            landed = column(out, flow, other)
            arrivals.setdefault(f, []).append(
                pltpu.make_async_copy(landed, landed, core_recv.at[f, src["y"], src["x"]])
            )
            waits.append((None, core.wait_send))
    for copy in copies.values():
        copy.wait()
    for some in arrivals.values():
        for arrival in some:
            arrival.wait()
    for cond, finish in waits:
        when(cond, finish)


def count_sites(flows, depth):
    return sum(len(e[4]) for e in schedule(flows, depth))


def gather(flows, depth, inputs, out_shapes, spare, collective_id, work, in_vmem, out_vmem):
    hbm = pl.BlockSpec(memory_space=pl.ANY)
    vmem = pl.BlockSpec(memory_space=pltpu.VMEM)
    n = len(flows)
    kernel = functools.partial(
        gather_kernel, flows, depth, len(inputs), len(out_shapes) + len(spare), work
    )
    return pl.pallas_call(
        kernel,
        out_shape=tuple(out_shapes),
        in_specs=[vmem if i in in_vmem else hbm for i in range(len(inputs))],
        out_specs=tuple(vmem if i in out_vmem else hbm for i in range(len(out_shapes))),
        scratch_shapes=[pltpu.VMEM(v.shape, v.dtype) for v in spare]
        + [
            pltpu.SemaphoreType.DMA((n, 2, depth, 2)),
            pltpu.SemaphoreType.DMA((count_sites(flows, depth),)),
            pltpu.SemaphoreType.DMA((n, 2, 2)),
            pltpu.SemaphoreType.DMA((n, 2, 2)),
            pltpu.SemaphoreType.DMA((n,)),
        ],
        compiler_params=pltpu.CompilerParams(
            collective_id=collective_id, has_side_effects=True, vmem_limit_bytes=62 << 20
        ),
    )(*inputs)


def slots_of(flow, d, depth):
    sizes = {"x": 2, "y": 2, "z": depth}
    before = flow["order"][: flow["order"].index(d)]
    return ([2] if d == "z" else []) + [sizes[k] for k in before] + ([depth] if d == "z" else [])


def slot(flow, d, src, side):
    before = flow["order"][: flow["order"].index(d)]
    return (
        ([0 if side > 0 else 1] if d == "z" else [])
        + [src[k] for k in before]
        + ([src["z"]] if d == "z" else [])
    )


def chunk_of(rows, columns):
    wide = 128
    while columns % (2 * wide) == 0 and rows * 2 * wide <= 12 * 1024:
        wide *= 2
    return wide


def scatter_kernel(flows, depth, n_in, n_out, n_made, work, *refs):
    ins, outs = refs[:n_in], refs[n_in : n_in + n_out]
    at = n_in + n_out
    made = refs[at : at + n_made]
    at += n_made
    mine, theirs, slots, marks = [], [], [], []
    for flow in flows:
        if flow["made"]:
            mine.append(made[flow["in"]])
        else:
            mine.append(refs[at])
            at += 1
        theirs.append(refs[at] if flow["cores"] else None)
        at += 1 if flow["cores"] else 0
        slots.append({})
        marks.append({})
        for d in flow["order"]:
            slots[-1][d], marks[-1][d] = refs[at], refs[at + 1]
            at += 2
    sent, core_recv, core_sent, local = refs[at:]
    pos = here(depth)
    greet(pos, flat_sides(flows), depth)
    events = schedule(flows, depth, True)

    def lead(flow, src):
        if not flow["cores"]:
            return (src["z"], src["x"])
        return (src["y"],) + ((src["c"],) if flow["made"] else ()) + (src["z"], src["x"])

    def col(src):
        return (src["y"], slice(None), src["x"])

    def parts(f, own, cols):
        low = flows[f]["columns"][0] if flows[f]["made"] else 0
        return own + (slice(None), pl.ds(pl.multiple_of(low + cols.start, 128), cols.size))

    ready, waits, sites = {}, [], 0

    def begin(chosen):
        for _, f, offsets, parent, children in events:
            key = (f, group_of(offsets))
            if key in ready or f not in chosen:
                continue
            flow = flows[f]
            src = source_of(pos, {d: o for d, o in offsets.items() if d != "z"})
            y = src["y"] if flow["cores"] else 0
            whole = made[flow["in"]] if flow["made"] else ins[flow["in"]]
            loads = []
            if flow["cores"]:
                core = pltpu.make_async_remote_copy(
                    column(whole, flow, beside(src, ("c", 1))),
                    theirs[f].at[col(src)],
                    core_sent.at[f, y, src["x"]],
                    core_recv.at[f, y, src["x"]],
                    device_id=device_of(beside(pos, ("c", 1))),
                    device_id_type=MESH,
                )
                core.start()
                loads.append(core.wait_recv)
                waits.append((None, core.wait_send))
            if not flow["made"]:
                copy = pltpu.make_async_copy(
                    column(whole, flow, src), mine[f].at[col(src)], local.at[f, y, src["x"]]
                )
                copy.start()
                loads.append(copy.wait)
            ready[key] = loads

    begin([f for f, flow in enumerate(flows) if not flow["made"]])
    items = [(e[0], 0, e) for e in events]
    items += [(key, 1, step) for key, step in (work(pos, ins, outs, made) if work else [])]
    items.sort(key=lambda item: item[0])
    for _, kind, item in items:
        if kind == 1:
            after, step = item
            step()
            begin(after)
            continue
        _, f, offsets, parent, children = item
        flow = flows[f]
        for load in ready.get((f, group_of(offsets)), []):
            load()
        ready[(f, group_of(offsets))] = []
        src = source_of(pos, offsets)
        own = lead(flow, src)
        send = None
        if parent is not None:
            d, toward = parent
            place = tuple(slot(flow, d, src, -toward))
            send = pltpu.make_async_remote_copy(
                mine[f].at[parts(f, own, pl.ds(0, flow["columns"][1]))],
                slots[f][d].at[place] if place else slots[f][d],
                sent.at[sites],
                marks[f][d].at[place if place else (0,)],
                device_id=device_of(beside(pos, parent)),
                device_id_type=MESH,
            )
            sites += 1

        def step():
            rows, columns = mine[f].shape[-2], flow["columns"][1]
            wide = chunk_of(rows, columns)
            terms = []
            for side in children:
                d = side[0]
                place = tuple(slot(flow, d, src, side[1]))
                buf = slots[f][d].at[place] if place else slots[f][d]
                there = exists(pos, side, depth)
                when(
                    there,
                    lambda: pltpu.make_async_copy(
                        buf, buf, marks[f][d].at[place if place else (0,)]
                    ).wait(),
                )
                terms.append((place, d, there))

            def total(cols):
                value = mine[f][parts(f, own, cols)].astype(jnp.float32)
                if flow["cores"]:
                    core = (src["y"], src["z"], src["x"], slice(None), cols)
                    value += theirs[f][core].astype(jnp.float32)
                return value

            def put(cols, value):
                if send is None:
                    low = flow["out_low"]
                    outs[flow["out"]][:, pl.ds(pl.multiple_of(low + cols.start, 128), wide)] = value
                else:
                    mine[f][parts(f, own, cols)] = value.astype(mine[f].dtype)

            def with_terms(chosen):
                def go():
                    def body(k, carry):
                        cols = pl.ds(pl.multiple_of(k * wide, wide), wide)
                        value = total(cols)
                        for place, d in chosen:
                            value += slots[f][d][place + (slice(None), cols)].astype(jnp.float32)
                        put(cols, value)
                        return carry

                    lax.fori_loop(0, columns // wide, body, 0)

                return go

            always = [(p, d) for p, d, there in terms if there is None]
            maybe = [(p, d, there) for p, d, there in terms if there is not None]
            if flow["cores"] or always or maybe:
                for picks in itertools.product((True, False), repeat=len(maybe)):
                    cond = None
                    for (p, d, there), pick in zip(maybe, picks):
                        test = there if pick else jnp.logical_not(there)
                        cond = test if cond is None else jnp.logical_and(cond, test)
                    chosen = always + [(p, d) for (p, d, _), pick in zip(maybe, picks) if pick]
                    if not chosen and not flow["cores"] and send is not None:
                        continue
                    when(cond, with_terms(chosen))
            if send is not None:
                send.start()

        cond = in_line(pos, offsets, depth)
        when(cond, step)
        if send is not None:
            waits.append((cond, send.wait_send))
    for cond, finish in waits:
        when(cond, finish)


def scatter(flows, depth, inputs, out_shapes, collective_id, work, made, in_vmem, spare):
    hbm = pl.BlockSpec(memory_space=pl.ANY)
    vmem = pl.BlockSpec(memory_space=pltpu.VMEM)
    n = len(flows)
    scratch = [pltpu.VMEM(m.shape, m.dtype) for m in made + spare]
    for flow in flows:
        source = made[flow["in"]] if flow["made"] else inputs[flow["in"]]
        rows, kind = source.shape[-2], source.dtype
        unit = (rows, flow["columns"][1])
        whole = ((2, depth, 2) if flow["cores"] else (depth, 2)) + unit
        if not flow["made"]:
            scratch.append(pltpu.VMEM(whole, kind))
        if flow["cores"]:
            scratch.append(pltpu.VMEM(whole, kind))
        for d in flow["order"]:
            places = tuple(slots_of(flow, d, depth))
            scratch.append(pltpu.VMEM(places + unit, kind))
            scratch.append(pltpu.SemaphoreType.DMA(places if places else (1,)))
    scratch += [
        pltpu.SemaphoreType.DMA((len(schedule(flows, depth)),)),
        pltpu.SemaphoreType.DMA((n, 2, 2)),
        pltpu.SemaphoreType.DMA((n, 2, 2)),
        pltpu.SemaphoreType.DMA((n, 2, 2)),
    ]
    kernel = functools.partial(
        scatter_kernel, flows, depth, len(inputs), len(out_shapes), len(made + spare), work
    )
    return pl.pallas_call(
        kernel,
        out_shape=tuple(out_shapes),
        in_specs=[vmem if i in in_vmem else hbm for i in range(len(inputs))],
        out_specs=tuple([vmem] * len(out_shapes)),
        scratch_shapes=scratch,
        compiler_params=pltpu.CompilerParams(
            collective_id=collective_id, has_side_effects=True, vmem_limit_bytes=62 << 20
        ),
    )(*inputs)


ZXY, ZYX, XZY, YZX = ("z", "x", "y"), ("z", "y", "x"), ("x", "z", "y"), ("y", "z", "x")


def flow_of(order, source, which, low, wide, place, cores=True, made=False):
    return dict(
        order=order,
        cores=cores,
        columns=(low, wide),
        in_columns=(low, wide),
        out_low=low,
        made=made,
        out=which,
        when=place,
        **{"in": source},
    )


def layout_of(large, own, span):
    dp, blk = lax.axis_size("dp"), lax.axis_size("blk")
    fits = all(v.shape[0] % 8 == 0 and v.shape[1] % 128 == 0 for v in large)
    fits = fits and own <= 128 and span <= 128
    width, wide = large[1].shape[1], large[2].shape[1]
    fits = fits and wide % width == 0 and dp * blk % (wide // width) == 0
    if fits and dp == 2 * CORES and blk % 2 == 0 and 2 <= blk // 2 <= 4:
        return blk // 2
    return None


def flat_rows(whole):
    return whole.reshape(-1, whole.shape[-1])


def flat_rows(whole):
    return whole.reshape(-1, whole.shape[-1])


def forward_kernel(tokens, w_qkv, flat, large, depth):
    rows, width = tokens.shape
    n, high = 4 * CORES * depth, flat.shape[0]
    own, wide = width // n, large[1].shape[1]
    count, span = wide // width, wide // n
    bf16, f32 = jnp.bfloat16, jnp.float32
    column_of, lane_of = np.arange(width), np.arange(128)[:, None]
    lanes = np.stack([lane_of == column_of % k for k in (own, span)])
    places = [np.arange(k)[:, None, None] == column_of // (width // k) for k in (n, n // count)]

    def work(pos, ins, outs):
        lanes_ref, place_ref, up_place_ref = ins[-3:]
        small, every, dense, kv_ref, q_ref, narrow, up_bias, attn_ref, lse_ref, blocks = outs[3:]

        def unpack():
            for k in range(3):
                at = pl.ds(k * width, width)
                part = blocks[:, :, :, :, :, at].astype(f32).reshape(width, width)
                dense[:, at] = part.astype(bf16)

        def project():
            rows_of = small[...].reshape(n * high, 128)
            spread = jnp.dot(rows_of, lanes_ref[0], preferred_element_type=f32)
            narrow[...] = jnp.sum(spread.reshape(n, high, width) * place_ref[...], axis=0)
            spread = jnp.dot(rows_of, lanes_ref[1], preferred_element_type=f32)
            spread = spread.reshape(count, n // count, high, width)
            for k in range(count):
                up_bias[k] = jnp.sum(spread[k] * up_place_ref[...], axis=0)
            query_bias, value_bias = narrow[0:1, :], narrow[1:2, :]
            mine = every[pos["z"], pos["x"]]
            query = jnp.dot(mine, dense[:, :width], preferred_element_type=f32)
            q_ref[...] = (query + query_bias).astype(bf16)
            later = jnp.concatenate([jnp.zeros_like(value_bias), value_bias], axis=1)

            def line(z, carry):
                some = every[z].reshape(2 * rows, width)
                part = jnp.dot(some, dense[:, width:], preferred_element_type=f32) + later
                kv_ref[z] = part.astype(bf16).reshape(2, rows, 2 * width)
                return carry

            lax.fori_loop(0, depth, line, 0)

        def keys_of(at):
            return kv_ref[:, :, :, at].reshape(-1, PAIR)

        pair = functools.partial(attend_pair, width, q_ref, keys_of, attn_ref, lse_ref)
        steps = in_steps(width // PAIR, len(ATTEND), pair)
        found = [(UNPACK, ((0,), unpack)), (PROJECT, ((1, 2), project))]
        return found + [(key, ((), step)) for key, step in zip(ATTEND, steps)]

    shapes = whole_shapes(list(large) + [flat], depth) + [
        jax.ShapeDtypeStruct((depth, 2, rows, width), bf16),
        jax.ShapeDtypeStruct((width, 3 * width), bf16),
        jax.ShapeDtypeStruct((depth, 2, rows, 2 * width), bf16),
        jax.ShapeDtypeStruct((rows, width), bf16),
        jax.ShapeDtypeStruct((high, width), f32),
        jax.ShapeDtypeStruct((count, high, width), f32),
    ]
    shapes += list(attend_shapes(rows, width))
    inputs = [w_qkv, flat, tokens] + list(large)
    flows = [
        flow_of(GATHER_ORDERS[0], 0, len(shapes), 0, 3 * width, FIRST),
        flow_of(GATHER_ORDERS[1], 1, 3, 0, 128, FIRST),
        flow_of(("z", "x"), 2, 4, 0, width, FIRST, cores=False),
    ]
    for i, (order, v) in enumerate(zip(GATHER_ORDERS[2:], large)):
        flows.append(flow_of(order, 3 + i, i, 0, v.shape[1], LATER))
    inputs += [jnp.asarray(lanes, bf16)]
    inputs += [jnp.asarray(np.broadcast_to(p, (len(p), high, width)), f32) for p in places]
    return gather(
        flows,
        depth,
        inputs,
        shapes,
        whole_shapes([w_qkv], depth),
        1,
        work,
        in_vmem=range(len(inputs) - 3, len(inputs)),
        out_vmem=range(3, len(shapes)),
    )


GATHER_ORDERS = (ZXY, ZYX, ZXY, XZY, YZX)
FIRST, LATER = (0, 1, 2, 3, 4, 5), (0.1, 1.1, 2.1, 3.1, 4.1, 6.0)
UNPACK, PROJECT, ATTEND = 5.1, 5.2, (6.2, 6.7, 7.7)
SCATTER_ORDERS = (ZXY, XZY, YZX, ZXY, ZYX)
BACK, EARLY = (0, 1.5, 2.5), (1.1, 2.1, 3.3, 4.3, 5.3, 6.3)
WEIGHTS, TOKENS, LAST = 2.6, 2.7, (3.2, 4.2, 5.2, 6.2, 7.2, 8.2)


def whole_shapes(large, depth):
    return [jax.ShapeDtypeStruct((2, CORES, depth, 2) + v.shape, v.dtype) for v in large]


def backward_kernel(query, kv, d_attn, lse, delta, every, dense, sums, d_up_bias, grads, large, depth):
    bf16, f32 = jnp.bfloat16, jnp.float32
    rows, width = query.shape
    n = 4 * CORES * depth
    own = width // n
    wide = d_up_bias.shape[1]
    count, span = wide // width, wide // n
    column_of = np.arange(width)
    line = np.arange(8 * n)[:, None] // 8
    places = [line == column_of // own, line % (n // count) == column_of // span]
    lanes = [column_of[:, None] % k == np.arange(128) for k in (own, span)]
    small = jax.ShapeDtypeStruct((2, CORES, depth, 2, 16, 128), f32)

    def work(pos, ins, outs, made):
        q_ref, kv_ref, do_ref, lse_ref, delta_ref, every_ref, w_ref = ins[-13:-6]
        sums_ref, up_ref, place_ref, up_place_ref, lanes_ref, up_lanes_ref = ins[-6:]
        token_part, d_whole, small_made, dq_ref, dkv_ref, sum_ref = made

        def keys_of(at):
            return kv_ref[:, :, :, at].reshape(-1, PAIR)

        def put_keys(at, value):
            dkv_ref[:, at] = value.astype(bf16)

        def put_values(at, val, value):
            sum_ref[:, at] = jnp.sum(value, axis=0, keepdims=True)
            dkv_ref[:, val] = value.astype(bf16)

        def pair(i):
            attend_back_pair(
                width,
                q_ref,
                keys_of,
                do_ref,
                lambda k: lse_ref[pl.ds(2 * i + k, 1), :],
                lambda k: delta_ref[pl.ds(2 * i + k, 1), :],
                dq_ref,
                put_keys,
                put_values,
                i,
            )

        def weights():
            whole = every_ref[...].reshape(-1, width)
            for k in range(3):
                if k == 0:
                    part = contract_rows(every_ref[pos["z"], pos["x"]], dq_ref[...].astype(bf16))
                else:
                    part = contract_rows(whole, dkv_ref[:, (k - 1) * width : k * width])
                part = part.reshape(2, CORES, depth, 2, own, width).astype(bf16)
                d_whole[:, :, :, :, :, k * width : (k + 1) * width] = part
            query_sum = jnp.sum(dq_ref[...], axis=0, keepdims=True)
            eight = jnp.concatenate([query_sum, sum_ref[...], sums_ref[2:8, :]], axis=0)
            whole = jnp.broadcast_to(eight[None], (n, 8, width)).reshape(8 * n, width)
            narrow = jnp.dot(
                whole * place_ref[...],
                lanes_ref[...],
                preferred_element_type=f32,
                precision=lax.Precision.HIGHEST,
            )
            spread = [
                jnp.broadcast_to(up_ref[:, k * width : (k + 1) * width], (8 * n // count, width))
                for k in range(count)
            ]
            up = jnp.dot(
                jnp.concatenate(spread, axis=0) * up_place_ref[...],
                up_lanes_ref[...],
                preferred_element_type=f32,
                precision=lax.Precision.HIGHEST,
            )
            lead = (2, CORES, depth, 2, 8, 128)
            small_made[:, :, :, :, 0:8, :] = narrow.reshape(lead)
            small_made[:, :, :, :, 8:16, :] = up.reshape(lead)

        def tokens_gradient():
            def line(z, carry):
                at = pl.ds(pl.multiple_of(z * 2 * rows, 2 * rows), 2 * rows)
                part = contract_cols(dkv_ref[at, :], w_ref[:, width:])
                token_part[z] = part.astype(bf16).reshape(2, rows, width)
                return carry

            lax.fori_loop(0, depth, line, 0)
            outs[-1][...] = contract_cols(dq_ref[...].astype(bf16), w_ref[:, :width])

        steps = in_steps(width // PAIR, len(BACK), pair)
        found = [(key, ((), step)) for key, step in zip(BACK, steps)]
        return found + [(WEIGHTS, ((3, 4), weights)), (TOKENS, ((5,), tokens_gradient))]

    blocks = [g.reshape((2, CORES, depth, 2) + v.shape) for g, v in zip(grads, large)]
    made = [
        jax.ShapeDtypeStruct(every.shape, bf16),
        jax.ShapeDtypeStruct((2, CORES, depth, 2, own, 3 * width), bf16),
        jax.ShapeDtypeStruct(small.shape, f32),
    ]
    spare = [
        jax.ShapeDtypeStruct((rows, width), f32),
        jax.ShapeDtypeStruct((2 * depth * rows, 2 * width), bf16),
        jax.ShapeDtypeStruct((1, width), f32),
    ]
    flows = []
    for i, (order, v) in enumerate(zip(SCATTER_ORDERS, large)):
        flows.append(flow_of(order, i, i, 0, v.shape[1], EARLY))
    flows.append(flow_of(SCATTER_ORDERS[3], 1, 3, 0, 3 * width, LAST, made=True))
    flows.append(flow_of(SCATTER_ORDERS[4], 2, 4, 0, 128, LAST, made=True))
    flows.append(flow_of(("z", "x"), 0, 5, 0, width, LAST, cores=False, made=True))
    shapes = [jax.ShapeDtypeStruct(v.shape, f32) for v in large]
    shapes += [
        jax.ShapeDtypeStruct((own, 3 * width), f32),
        jax.ShapeDtypeStruct(small.shape[-2:], f32),
        jax.ShapeDtypeStruct((rows, width), f32),
        jax.ShapeDtypeStruct((rows, width), f32),
    ]
    inputs = blocks + [query, kv, d_attn, lse, delta, every, dense, sums, d_up_bias]
    inputs += [jnp.asarray(v, f32) for v in places + lanes]
    return scatter(
        flows, depth, inputs, shapes, 2, work, made, range(len(blocks), len(inputs)), spare
    )


def middle_kernel(chunk, *refs):
    bf16, f32 = jnp.bfloat16, jnp.float32
    tokens, attn, lse, cotangent, narrow, up_bias, head_of, wo_in, wu_in, wd_in = refs[:10]
    out, dh1_out, d_attn_out, delta_out, lse_out, sums, d_up_bias = refs[10:17]
    d_wo_out, d_wu_out, d_wd_out = refs[17:20]
    wo, wu, wd, d_wo, d_wu, d_wd, slope, act, arrived, left = refs[20:]
    count = wu.shape[0]

    def cut(c):
        return pl.ds(c * chunk, chunk)

    loads = [pltpu.make_async_copy(wo_in, wo, arrived.at[0])]
    for c in range(count):
        loads.append(pltpu.make_async_copy(wu_in.at[:, cut(c)], wu.at[c], arrived.at[1 + 2 * c]))
        loads.append(pltpu.make_async_copy(wd_in.at[cut(c), :], wd.at[c], arrived.at[2 + 2 * c]))
    for load in loads:
        load.start()

    def line(k):
        return narrow[k : k + 1, :]

    def total(value):
        return jnp.sum(value, axis=0, keepdims=True)

    logs = [lse[k] for k in range(lse.shape[0])]
    rows = tokens.shape[0]
    logs.append(jnp.zeros((rows, 128 - 2 * len(logs)), f32))
    lse_out[...] = jnp.concatenate(logs, axis=1).T[: lse_out.shape[0]]
    loads[0].wait()
    hidden = tokens[...].astype(f32) + line(2)
    hidden += jnp.dot(attn[...], wo[...], preferred_element_type=f32)
    y1, xhat1, rstd1 = layernorm_forward(hidden, line(3), line(5))
    y1_low = y1.astype(bf16)
    hidden = y1 + line(7)
    for c in range(count):
        loads[1 + 2 * c].wait()
        up = jnp.dot(y1_low, wu[c], preferred_element_type=f32) + up_bias[c, 8:9, :]
        cdf = 0.5 * (1.0 + lax.erf(up * 0.7071067811865476))
        slope[:, cut(c)] = cdf + up * jnp.exp(-0.5 * up * up) * 0.3989422804014327
        act[:, cut(c)] = (up * cdf).astype(bf16)
        loads[2 + 2 * c].wait()
        hidden += jnp.dot(act[:, cut(c)], wd[c], preferred_element_type=f32)
    y2, xhat2, rstd2 = layernorm_forward(hidden, line(4), line(6))
    out[...] = y2.astype(bf16)
    gradient = cotangent[...].astype(f32)
    dh2 = layernorm_backward(gradient, xhat2, rstd2, line(4))
    sums[0:2, :] = jnp.zeros((2, sums.shape[1]), f32)
    sums[4:5, :] = total(gradient * xhat2)
    sums[6:7, :] = total(gradient)
    sums[7:8, :] = total(dh2)
    dh2_low = dh2.astype(bf16)
    stores = []
    dy1 = dh2
    for c in range(count):
        d_wd[c] = contract_rows(act[:, cut(c)], dh2_low).astype(bf16)
        stores.append(pltpu.make_async_copy(d_wd.at[c], d_wd_out.at[cut(c), :], left.at[1 + 2 * c]))
        stores[-1].start()
        d_up_f = contract_cols(dh2_low, wd[c]) * slope[:, cut(c)]
        d_up_bias[:, cut(c)] = total(d_up_f)
        d_up = d_up_f.astype(bf16)
        d_wu[c] = contract_rows(y1_low, d_up).astype(bf16)
        stores.append(pltpu.make_async_copy(d_wu.at[c], d_wu_out.at[:, cut(c)], left.at[2 + 2 * c]))
        stores[-1].start()
        dy1 += contract_cols(d_up, wu[c])
    dh1 = layernorm_backward(dy1, xhat1, rstd1, line(3))
    sums[2:3, :] = total(dh1)
    sums[3:4, :] = total(dy1 * xhat1)
    sums[5:6, :] = total(dy1)
    dh1_out[...] = dh1
    dh1_low = dh1.astype(bf16)
    d_wo[...] = contract_rows(attn[...], dh1_low).astype(bf16)
    stores.append(pltpu.make_async_copy(d_wo, d_wo_out, left.at[0]))
    stores[-1].start()
    d_attn = contract_cols(dh1_low, wo[...]).astype(bf16)
    d_attn_out[...] = d_attn
    delta_out[...] = lax.dot_general(
        head_of[...],
        d_attn.astype(f32) * attn[...].astype(f32),
        (((1,), (1,)), ((), ())),
        preferred_element_type=f32,
        precision=lax.Precision.HIGHEST,
    )
    for store in stores:
        store.wait()


def middle(tokens, attn, lse, cotangent, narrow, up_bias, w_out, w_up, w_down):
    bf16, f32 = jnp.bfloat16, jnp.float32
    rows, width = tokens.shape
    wide = w_up.shape[1]
    chunk = width
    count = wide // chunk
    lines = -(-(width // HEAD) // 8) * 8
    head_of = np.arange(lines)[:, None] == np.arange(width) // HEAD
    vmem, hbm = pl.BlockSpec(memory_space=pltpu.VMEM), pl.BlockSpec(memory_space=pl.ANY)
    shapes = [
        ((rows, width), bf16),
        ((rows, width), f32),
        ((rows, width), bf16),
        ((lines, rows), f32),
        ((lines, rows), f32),
        ((8, width), f32),
        ((1, wide), f32),
        (w_out.shape, bf16),
        (w_up.shape, bf16),
        (w_down.shape, bf16),
    ]
    chunks = (count, width, chunk)
    return pl.pallas_call(
        functools.partial(middle_kernel, chunk),
        out_shape=tuple(jax.ShapeDtypeStruct(*v) for v in shapes),
        in_specs=[vmem] * 7 + [hbm] * 3,
        out_specs=tuple([vmem] * 7 + [hbm] * 3),
        scratch_shapes=[
            pltpu.VMEM(w_out.shape, bf16),
            pltpu.VMEM(chunks, bf16),
            pltpu.VMEM(chunks, bf16),
            pltpu.VMEM(w_out.shape, bf16),
            pltpu.VMEM(chunks, bf16),
            pltpu.VMEM(chunks, bf16),
            pltpu.VMEM((rows, wide), f32),
            pltpu.VMEM((rows, wide), bf16),
            pltpu.SemaphoreType.DMA((1 + 2 * count,)),
            pltpu.SemaphoreType.DMA((1 + 2 * count,)),
        ],
        compiler_params=pltpu.CompilerParams(vmem_limit_bytes=60 << 20),
        name="ffn",
    )(
        tokens, attn, lse, cotangent, narrow, up_bias, jnp.asarray(head_of, f32), w_out, w_up, w_down
    )


def finish_kernel(*refs):
    parts, row, dh1, query_part, token_sum = refs[:4], refs[4], refs[5], refs[6], refs[7]
    d_tokens, grads, pairs, singles, up = refs[8], refs[9:13], refs[13:16], refs[16:18], refs[18]
    d_tokens[...] = dh1[...] + query_part[...] + token_sum[...]
    for part, grad in zip(parts, grads):
        grad[...] = part[...]
    own = pairs[0].shape[1]
    for k, pair in zip((0, 3, 5), pairs):
        pair[...] = row[k : k + 2, :own]
    for k, single in zip((2, 7), singles):
        single[...] = row[k : k + 1, :own]
    up[...] = row[8:9, : up.shape[1]]


def finish(parts, row, dh1, query_part, token_sum, own, span):
    f32 = jnp.float32
    shapes = [dh1.shape] + [p.shape for p in parts] + [(2, own)] * 3 + [(1, own)] * 2 + [(1, span)]
    vmem = pl.BlockSpec(memory_space=pltpu.VMEM)
    return pl.pallas_call(
        finish_kernel,
        out_shape=tuple(jax.ShapeDtypeStruct(shape, f32) for shape in shapes),
        in_specs=[vmem] * 8,
        out_specs=tuple([vmem] * len(shapes)),
        name="finish",
    )(*parts, row, dh1, query_part, token_sum)


SPARE = 16


def split_owner(full, count):
    p = full.shape[0]
    return full.reshape(p, count, -1).transpose(1, 0, 2).reshape(count, -1)


def join_owner(parts, p):
    count = parts.shape[0]
    return parts.reshape(count, p, -1).transpose(1, 0, 2).reshape(p, -1)


def plain_on_device(
    tokens,
    w_qkv,
    qv_bias,
    w_out,
    out_bias,
    norm_gain,
    norm_bias,
    w_up,
    up_bias,
    w_down,
    down_bias,
    cotangent,
):
    f32 = jnp.float32
    bf16 = jnp.bfloat16
    rows, width = tokens.shape
    heads = width // HEAD
    n = lax.axis_size("dp") * lax.axis_size("blk")
    small = [qv_bias, out_bias, norm_gain, norm_bias, up_bias, down_bias]
    sizes = [v.size for v in small]
    flat = jnp.concatenate([v.reshape(-1) for v in small])
    flat = jnp.pad(flat, (0, SPARE * width - flat.size)).reshape(SPARE, width)
    large = [w_qkv, w_out, w_up, w_down]
    shard = jnp.concatenate(
        [v[:, i : i + width] for v in large for i in range(0, v.shape[1], width)] + [flat]
    )
    packed = lax.all_gather(shard, ("dp", "blk"), axis=0)
    wholes, at = [], 0
    for v in large:
        high, columns = v.shape
        blocks = []
        for _ in range(columns // width):
            blocks.append(packed[:, at : at + high].reshape(n * high, width))
            at += high
        wholes.append(jnp.concatenate(blocks, axis=1))
    wq_full, wo_full, wu_full, wd_full = wholes
    row_full = packed[:, at:].reshape(n, -1)
    parts, at = [], 0
    for size, v in zip(sizes, small):
        parts.append(join_owner(row_full[:, at : at + size], 2 if v.ndim == 2 else 1))
        at += size
    qvb_full, bo_full, gain_full, shift_full, bu_full, bd_full = parts
    bo_full, bu_full, bd_full = bo_full[0], bu_full[0], bd_full[0]
    norm_gain_pair = gain_full.astype(f32)
    norm_offset_pair = shift_full.astype(f32)
    qvb = qvb_full.astype(f32)
    bias_row = jnp.concatenate([qvb[0], jnp.zeros((width,), f32), qvb[1]])
    qkv = (jnp.dot(tokens, wq_full, preferred_element_type=f32) + bias_row).astype(bf16)
    query = qkv[:, :width]
    kv = lax.all_gather(qkv[:, width:], "blk", axis=0, tiled=True)
    attn, lse = attend(query, kv)
    first_hidden = (
        tokens.astype(f32)
        + jnp.dot(attn, wo_full, preferred_element_type=f32)
        + bo_full.astype(f32)
    )
    first_norm_output, first_normalized, first_inverse_deviation = layernorm_forward(
        first_hidden, norm_gain_pair[0], norm_offset_pair[0]
    )
    y1_low = first_norm_output.astype(bf16)
    up = jnp.dot(y1_low, wu_full, preferred_element_type=f32) + bu_full.astype(f32)
    act = jax.nn.gelu(up, approximate=False).astype(bf16)
    second_hidden = (
        first_norm_output + jnp.dot(act, wd_full, preferred_element_type=f32) + bd_full.astype(f32)
    )
    output_float, second_normalized, second_inverse_deviation = layernorm_forward(
        second_hidden, norm_gain_pair[1], norm_offset_pair[1]
    )
    output = output_float.astype(bf16)
    wq_b, wo_b, wu_b, wd_b = wq_full, wo_full, wu_full, wd_full
    gain_pair_block = norm_gain_pair
    incoming_gradient = cotangent.astype(f32)
    second_gain_gradient = jnp.sum(incoming_gradient * second_normalized, axis=0)
    d_shift2 = jnp.sum(incoming_gradient, axis=0)
    second_hidden_gradient = layernorm_backward(
        incoming_gradient, second_normalized, second_inverse_deviation, gain_pair_block[1]
    )
    dh2_low = second_hidden_gradient.astype(bf16)
    d_w_down = contract_rows(act, dh2_low)
    d_down_bias = jnp.sum(second_hidden_gradient, axis=0)
    d_up_f = contract_cols(dh2_low, wd_b) * gelu_grad(up)
    d_up_bias = jnp.sum(d_up_f, axis=0)
    d_up = d_up_f.astype(bf16)
    d_w_up = contract_rows(y1_low, d_up)
    first_output_gradient = second_hidden_gradient + contract_cols(d_up, wu_b)
    first_gain_gradient = jnp.sum(first_output_gradient * first_normalized, axis=0)
    d_shift1 = jnp.sum(first_output_gradient, axis=0)
    first_hidden_gradient = layernorm_backward(
        first_output_gradient, first_normalized, first_inverse_deviation, gain_pair_block[0]
    )
    dh1_low = first_hidden_gradient.astype(bf16)
    d_w_out = contract_rows(attn, dh1_low)
    d_out_bias = jnp.sum(first_hidden_gradient, axis=0)
    d_gains = jnp.stack([first_gain_gradient, second_gain_gradient])
    d_shifts = jnp.stack([d_shift1, d_shift2])
    d_attn = contract_cols(dh1_low, wo_b).astype(bf16)
    delta = jnp.sum((d_attn.astype(f32) * attn.astype(f32)).reshape(rows, heads, HEAD), axis=-1).T
    d_query, d_kv_all = attend_back(
        query, kv, d_attn, lse.transpose(0, 2, 1), delta.reshape(heads // 2, 2, rows)
    )
    d_kv = lax.psum_scatter(d_kv_all, "blk", scatter_dimension=0, tiled=True).astype(f32)
    d_key = d_kv[:, :width]
    d_value = d_kv[:, width:]
    d_qv = jnp.stack([jnp.sum(d_query, axis=0), jnp.sum(d_value, axis=0)])
    d_qkv = jnp.concatenate([d_query, d_key, d_value], axis=1).astype(bf16)
    d_w_qkv = contract_rows(tokens, d_qkv)
    d_tokens = first_hidden_gradient + contract_cols(d_qkv, wq_b)
    grads = [d_qv, d_out_bias[None], d_gains, d_shifts, d_up_bias[None], d_down_bias[None]]
    row = jnp.concatenate([split_owner(v, n) for v in grads], axis=1)
    row = jnp.pad(row, ((0, 0), (0, SPARE * width - row.shape[1]))).reshape(n, SPARE, width)
    blocks = []
    for d_full, v in zip((d_w_qkv, d_w_out, d_w_up, d_w_down), large):
        d_low = d_full.astype(bf16).reshape((n,) + v.shape)
        blocks += [d_low[:, :, i : i + width] for i in range(0, v.shape[1], width)]
    packed = jnp.concatenate(blocks + [row.astype(bf16)], axis=1)
    packed = lax.psum_scatter(packed, ("dp", "blk"), scatter_dimension=0, tiled=True)[0]
    wholes, at = [], 0
    for v in large:
        high, columns = v.shape
        blocks = []
        for _ in range(columns // width):
            blocks.append(packed[at : at + high])
            at += high
        wholes.append(jnp.concatenate(blocks, axis=1).astype(f32))
    g_wqkv, g_wout, g_wup, g_wdown = wholes
    row, at, parts = packed[at:].reshape(-1).astype(f32), 0, []
    for size, v in zip(sizes, small):
        parts.append(row[at : at + size].reshape(v.shape))
        at += size
    g_qv, g_bout, g_gain, g_shift, g_bup, g_bdown = parts
    return (
        output,
        d_tokens,
        g_wqkv,
        g_qv,
        g_wout,
        g_bout,
        g_gain,
        g_shift,
        g_wup,
        g_bup,
        g_wdown,
        g_bdown,
    )


def on_device(
    tokens,
    w_qkv,
    qv_bias,
    w_out,
    out_bias,
    norm_gain,
    norm_bias,
    w_up,
    up_bias,
    w_down,
    down_bias,
    cotangent,
):
    f32 = jnp.float32
    bf16 = jnp.bfloat16
    rows, width = tokens.shape
    n = lax.axis_size("dp") * lax.axis_size("blk")
    own = out_bias.shape[0]
    span = up_bias.shape[0]
    depth = layout_of([w_qkv, w_out, w_up, w_down], own, span)
    if depth is None:
        return plain_on_device(
            tokens,
            w_qkv,
            qv_bias,
            w_out,
            out_bias,
            norm_gain,
            norm_bias,
            w_up,
            up_bias,
            w_down,
            down_bias,
            cotangent,
        )
    large = [w_out, w_up, w_down]
    narrow = jnp.concatenate([qv_bias, out_bias[None], norm_gain, norm_bias, down_bias[None]])
    flat = jnp.concatenate(
        [
            jnp.pad(narrow, ((0, 0), (0, 128 - own))),
            jnp.pad(up_bias[None], ((0, 7), (0, 128 - span))),
        ]
    )
    outs = forward_kernel(tokens, w_qkv, flat, large, depth)
    wo_full, wu_full, wd_full = [flat_rows(w) for w in outs[:3]]
    every, dense, kv, query, narrow_full, bu_full, attn, lse = outs[4:]
    output, dh1, d_attn, delta, lse, sums, d_up_bias, d_w_out, d_w_up, d_w_down = middle(
        tokens, attn, lse, cotangent, narrow_full, bu_full, wo_full, wu_full, wd_full
    )
    g_wout, g_wup, g_wdown, g_wqkv, row, token_sum, query_part = backward_kernel(
        query,
        kv,
        d_attn,
        lse,
        delta,
        every,
        dense,
        sums,
        d_up_bias,
        [d_w_out, d_w_up, d_w_down],
        large,
        depth,
    )
    d_tokens, g_wqkv, g_wout, g_wup, g_wdown, g_qv, g_gain, g_shift, g_bout, g_bdown, g_bup = finish(
        [g_wqkv, g_wout, g_wup, g_wdown], row, dh1, query_part, token_sum, own, span
    )
    g_bout, g_bdown, g_bup = g_bout[0], g_bdown[0], g_bup[0]
    return (
        output,
        d_tokens,
        g_wqkv,
        g_qv,
        g_wout,
        g_bout,
        g_gain,
        g_shift,
        g_wup,
        g_bup,
        g_wdown,
        g_bdown,
    )


def solution(mesh):
    return jax.shard_map(
        on_device,
        mesh=mesh,
        in_specs=(
            P(("dp", "blk"), None),
            P(("dp", "blk"), None),
            P(None, ("dp", "blk")),
            P(("dp", "blk"), None),
            P(("dp", "blk")),
            P(None, ("dp", "blk")),
            P(None, ("dp", "blk")),
            P(("dp", "blk"), None),
            P(("dp", "blk")),
            P(("dp", "blk"), None),
            P(("dp", "blk")),
            P(("dp", "blk"), None),
        ),
        out_specs=(
            P(("dp", "blk"), None),
            P(("dp", "blk"), None),
            P(("dp", "blk"), None),
            P(None, ("dp", "blk")),
            P(("dp", "blk"), None),
            P(("dp", "blk")),
            P(None, ("dp", "blk")),
            P(None, ("dp", "blk")),
            P(("dp", "blk"), None),
            P(("dp", "blk")),
            P(("dp", "blk"), None),
            P(("dp", "blk")),
        ),
        check_vma=False,
    )
```

```python
import functools
import itertools

import jax
import jax.numpy as jnp
import numpy as np
from jax import lax
from jax.experimental import pallas as pl
from jax.experimental.pallas import tpu as pltpu
from jax.sharding import PartitionSpec as P

HEAD = 64


EPS = 1e-05
SCALE = 0.125


def layernorm_forward(h, norm_gain_vector, norm_offset):
    row_average = jnp.mean(h, axis=-1, keepdims=True)
    centered_input = h - row_average
    var = jnp.mean(centered_input * centered_input, axis=-1, keepdims=True)
    inverse_deviation = lax.rsqrt(var + EPS)
    normalized_input = centered_input * inverse_deviation
    return (normalized_input * norm_gain_vector + norm_offset, normalized_input, inverse_deviation)


def layernorm_backward(incoming_gradient, normalized_input, inverse_deviation, norm_gain_vector):
    scaled_values = incoming_gradient * norm_gain_vector
    return inverse_deviation * (
        scaled_values
        - jnp.mean(scaled_values, axis=-1, keepdims=True)
        - normalized_input * jnp.mean(scaled_values * normalized_input, axis=-1, keepdims=True)
    )


def gelu_grad(up):
    cdf = 0.5 * (1.0 + jax.scipy.special.erf(up * 0.7071067811865476))
    return cdf + up * jnp.exp(-0.5 * up * up) * 0.3989422804014327


def contract_rows(left, right):
    return lax.dot_general(
        left, right, (((0,), (0,)), ((), ())), preferred_element_type=jnp.float32
    )


def contract_cols(left, right):
    return lax.dot_general(
        left, right, (((1,), (1,)), ((), ())), preferred_element_type=jnp.float32
    )


PAIR = 2 * HEAD


def attend_pair(width, q_ref, keys_of, attn_ref, lse_ref, i):
    at = pl.ds(pl.multiple_of(i * PAIR, PAIR), PAIR)
    q2 = q_ref[:, at]
    k2 = keys_of(at)
    v2 = keys_of(pl.ds(pl.multiple_of(width + i * PAIR, PAIR), PAIR))
    outs, logs = [], []
    for j in range(2):
        own = slice(j * HEAD, (j + 1) * HEAD)
        scores = contract_cols(q2[:, own], k2[:, own]) * SCALE
        peak = jnp.max(scores, axis=1, keepdims=True)
        weights = jnp.exp(scores - peak)
        total = jnp.sum(weights, axis=1, keepdims=True)
        part = jnp.dot(
            weights.astype(jnp.bfloat16), v2[:, own], preferred_element_type=jnp.float32
        )
        outs.append((part / total).astype(jnp.bfloat16))
        logs.append(peak + jnp.log(total))
    attn_ref[:, at] = jnp.concatenate(outs, axis=1)
    lse_ref[i] = jnp.concatenate(logs, axis=1)


def attend_back_pair(
    width, q_ref, keys_of, do_ref, lse_of, delta_of, dq_ref, put_keys, put_values, i
):
    at = pl.ds(pl.multiple_of(i * PAIR, PAIR), PAIR)
    val = pl.ds(pl.multiple_of(width + i * PAIR, PAIR), PAIR)
    q2 = q_ref[:, at]
    do2 = do_ref[:, at]
    k2 = keys_of(at)
    v2 = keys_of(val)
    dqs, dks, dvs = [], [], []
    for j in range(2):
        own = slice(j * HEAD, (j + 1) * HEAD)
        q_h, do_h, k_h, v_h = q2[:, own], do2[:, own], k2[:, own], v2[:, own]
        scores = contract_cols(k_h, q_h) * SCALE
        probs = jnp.exp(scores - lse_of(j))
        dprobs = contract_cols(v_h, do_h)
        dscores = (probs * (dprobs - delta_of(j))).astype(jnp.bfloat16)
        dqs.append(SCALE * contract_rows(dscores, k_h))
        dks.append(SCALE * jnp.dot(dscores, q_h, preferred_element_type=jnp.float32))
        dvs.append(jnp.dot(probs.astype(jnp.bfloat16), do_h, preferred_element_type=jnp.float32))
    dq_ref[:, at] = jnp.concatenate(dqs, axis=1)
    put_keys(at, jnp.concatenate(dks, axis=1))
    put_values(at, val, jnp.concatenate(dvs, axis=1))


def attend_kernel(width, q_ref, kv_ref, attn_ref, lse_ref):
    def pair(i, carry):
        attend_pair(width, q_ref, lambda at: kv_ref[:, at], attn_ref, lse_ref, i)
        return carry

    lax.fori_loop(0, width // PAIR, pair, 0)


def attend(query, kv):
    rows, width = query.shape
    vmem = pl.BlockSpec(memory_space=pltpu.VMEM)
    return pl.pallas_call(
        functools.partial(attend_kernel, width),
        out_shape=attend_shapes(rows, width),
        in_specs=[vmem] * 2,
        out_specs=(vmem, vmem),
        compiler_params=pltpu.CompilerParams(vmem_limit_bytes=60 << 20),
    )(query, kv)


def attend_shapes(rows, width):
    return (
        jax.ShapeDtypeStruct((rows, width), jnp.bfloat16),
        jax.ShapeDtypeStruct((width // PAIR, rows, 2), jnp.float32),
    )


def attend_back_kernel(width, q_ref, kv_ref, do_ref, lse_ref, delta_ref, dq_ref, dkv_ref):
    def put(at, value):
        dkv_ref[:, at] = value.astype(jnp.bfloat16)

    def pair(i, carry):
        attend_back_pair(
            width,
            q_ref,
            lambda at: kv_ref[:, at],
            do_ref,
            lambda k: lse_ref[i, k : k + 1],
            lambda k: delta_ref[i, k : k + 1],
            dq_ref,
            put,
            lambda at, val, value: put(val, value),
            i,
        )
        return carry

    lax.fori_loop(0, width // PAIR, pair, 0)


def attend_back(query, kv, d_attn, lse, delta):
    rows, width = query.shape
    vmem = pl.BlockSpec(memory_space=pltpu.VMEM)
    return pl.pallas_call(
        functools.partial(attend_back_kernel, width),
        out_shape=(
            jax.ShapeDtypeStruct((rows, width), jnp.float32),
            jax.ShapeDtypeStruct(kv.shape, jnp.bfloat16),
        ),
        in_specs=[vmem] * 5,
        out_specs=(vmem, vmem),
        compiler_params=pltpu.CompilerParams(vmem_limit_bytes=60 << 20),
    )(query, kv, d_attn, lse, delta)


def in_steps(pairs, steps, pair):
    bounds = [pairs * k // steps for k in range(steps + 1)]

    def step(low, high):
        def body(i, carry):
            pair(i)
            return carry

        lax.fori_loop(low, high, body, 0)

    return [functools.partial(step, lo, hi) for lo, hi in zip(bounds, bounds[1:])]


MESH = pl.DeviceIdType.MESH
CORES = 2


def tree_events(order, depth):
    spans = {"x": [0, 1], "y": [0, 1], "z": [0] + [s * k for k in range(1, depth) for s in (1, -1)]}
    sides = {"x": [("x", 1)], "y": [("y", 1)], "z": [("z", 1), ("z", -1)]}
    found = []
    for offsets in itertools.product(*(spans[d] for d in order)):
        moved = [i for i, o in enumerate(offsets) if o]
        last = moved[-1] if moved else -1
        parent, children = None, []
        if moved:
            toward = 1 if offsets[last] > 0 else -1
            parent = (order[last], toward)
            if order[last] == "z":
                children.append(("z", -toward))
        for d in order[last + 1 :]:
            children += sides[d]
        found.append((sum(abs(o) for o in offsets), dict(zip(order, offsets)), parent, children))
    return found


def here(depth):
    dp, blk = lax.axis_index("dp"), lax.axis_index("blk")
    return {"y": dp // CORES, "c": lax.rem(dp, CORES), "z": blk // 2, "x": lax.rem(blk, 2)}


def device_of(pos):
    return (pos["y"] * CORES + pos["c"], pos["z"] * 2 + pos["x"])


def beside(pos, side):
    d, step = side
    moved = dict(pos)
    moved[d] = pos[d] + step if d == "z" else 1 - pos[d]
    return moved


def exists(pos, side, depth):
    if side[0] != "z":
        return None
    return pos["z"] + 1 < depth if side[1] > 0 else pos["z"] >= 1


def source_of(pos, offsets):
    moved = dict(pos)
    for d, o in offsets.items():
        if o:
            moved[d] = pos[d] + o if d == "z" else 1 - pos[d]
    return moved


def in_line(pos, offsets, depth):
    o = offsets.get("z", 0)
    if o == 0:
        return None
    return pos["z"] + o < depth if o > 0 else pos["z"] >= -o


def when(cond, body):
    if cond is None:
        body()
    else:
        pl.when(cond)(body)


def greet(pos, sides, depth):
    barrier = pltpu.get_barrier_semaphore()
    for side in sides:
        when(
            exists(pos, side, depth),
            lambda side=side: pl.semaphore_signal(
                barrier, inc=1, device_id=device_of(beside(pos, side)), device_id_type=MESH
            ),
        )
    peers = sum(1 for d, _ in sides if d != "z")
    if any(d == "z" for d, _ in sides):
        up = jnp.where(pos["z"] + 1 < depth, 1, 0)
        peers = peers + up + jnp.where(pos["z"] >= 1, 1, 0)
    pl.semaphore_wait(barrier, peers)


def schedule(flows, depth, back=False):
    events = []
    for f, flow in enumerate(flows):
        tree = tree_events(flow["order"], depth)
        most = max(e[0] for e in tree)
        for hops, offsets, parent, children in tree:
            key = flow["when"][most - hops if back else hops]
            events.append((key, f, offsets, parent, children))
    events.sort(key=lambda e: (e[0], e[1]))
    return events


def group_of(offsets):
    return tuple(sorted((d, o) for d, o in offsets.items() if d != "z"))


def flat_sides(flows):
    axes = sorted({d for flow in flows for d in flow["order"]})
    sides = [s for d in axes for s in ([("z", 1), ("z", -1)] if d == "z" else [(d, 1)])]
    return sides + ([("c", 1)] if any(flow["cores"] for flow in flows) else [])


def block(ref, flow, src):
    lead = (src["y"], src["c"], src["z"], src["x"]) if flow["cores"] else (src["z"], src["x"])
    low, wide = flow["columns"]
    return ref.at[lead + (slice(None), pl.ds(low, wide))]


def column(ref, flow, src):
    lead = (src["y"], src["c"], slice(None), src["x"]) if flow["cores"] else (slice(None), src["x"])
    low, wide = flow["columns"]
    return ref.at[lead + (slice(None), pl.ds(low, wide))]


def gather_kernel(flows, depth, n_in, n_out, work, *refs):
    ins, outs = refs[:n_in], refs[n_in : n_in + n_out]
    recv, sent, core_recv, core_sent, local, extra = refs[n_in + n_out :]
    pos = here(depth)
    greet(pos, flat_sides(flows), depth)
    copies, waits, arrivals = {}, [], {}
    for f, flow in enumerate(flows):
        if not flow["made"]:
            low, wide = flow["in_columns"]
            own = ins[flow["in"]].at[:, pl.ds(low, wide)]
            copies[f] = pltpu.make_async_copy(own, block(outs[flow["out"]], flow, pos), local.at[f])
            copies[f].start()
    events = schedule(flows, depth)
    items = [(e[0], 0, e) for e in events]
    items += [(key, 1, step) for key, step in (work(pos, ins, outs, extra) if work else [])]
    items.sort(key=lambda item: item[0])
    last = {}
    for i, (_, kind, e) in enumerate(items):
        if kind == 0:
            last[(e[1], group_of(e[2]))] = i
    sites = 0
    for i, (_, kind, item) in enumerate(items):
        if kind == 1:
            needed, step = item
            for f in needed:
                if f in copies:
                    copies.pop(f).wait()
                for arrival in arrivals.pop(f, []):
                    arrival.wait()
            step()
            continue
        _, f, offsets, parent, children = item
        flow = flows[f]
        src = source_of(pos, offsets)
        out = outs[flow["out"]]
        low, wide = flow["in_columns"]
        target = block(out, flow, src)
        origin = target
        if parent is None and not flow["made"]:
            origin = ins[flow["in"]].at[:, pl.ds(low, wide)]
        mark = recv.at[f, src["y"] if "y" in flow["order"] else 0, src["z"], src["x"]]
        sends = []
        for side in children:
            sends.append(
                (
                    side,
                    functools.partial(
                        pltpu.make_async_remote_copy,
                        origin,
                        target,
                        sent.at[sites],
                        mark,
                        device_id=device_of(beside(pos, side)),
                        device_id_type=MESH,
                    ),
                )
            )
            sites += 1

        def arrive():
            if parent is not None:
                pltpu.make_async_copy(target, target, mark).wait()
            for side, send in sends:
                when(exists(pos, side, depth), lambda: send().start())

        def finish(sends=sends):
            for side, send in sends:
                when(exists(pos, side, depth), lambda: send().wait_send())

        cond = in_line(pos, offsets, depth)
        when(cond, arrive)
        if sends:
            waits.append((cond, finish))
        if flow["cores"] and last[(f, group_of(offsets))] == i:
            if f in copies and not any(o for d, o in offsets.items() if d != "z"):
                copies.pop(f).wait()
            other = beside(src, ("c", 1))
            whole = column(out, flow, src)
            core = pltpu.make_async_remote_copy(
                whole,
                whole,
                core_sent.at[f, src["y"], src["x"]],
                core_recv.at[f, src["y"], src["x"]],
                device_id=device_of(beside(pos, ("c", 1))),
                device_id_type=MESH,
            )
            core.start()
            landed = column(out, flow, other)
            arrivals.setdefault(f, []).append(
                pltpu.make_async_copy(landed, landed, core_recv.at[f, src["y"], src["x"]])
            )
            waits.append((None, core.wait_send))
    for copy in copies.values():
        copy.wait()
    for some in arrivals.values():
        for arrival in some:
            arrival.wait()
    for cond, finish in waits:
        when(cond, finish)


def count_sites(flows, depth):
    return sum(len(e[4]) for e in schedule(flows, depth))


def gather(flows, depth, inputs, out_shapes, spare, collective_id, work, in_vmem, out_vmem):
    hbm = pl.BlockSpec(memory_space=pl.ANY)
    vmem = pl.BlockSpec(memory_space=pltpu.VMEM)
    n = len(flows)
    kernel = functools.partial(
        gather_kernel, flows, depth, len(inputs), len(out_shapes) + len(spare), work
    )
    return pl.pallas_call(
        kernel,
        out_shape=tuple(out_shapes),
        in_specs=[vmem if i in in_vmem else hbm for i in range(len(inputs))],
        out_specs=tuple(vmem if i in out_vmem else hbm for i in range(len(out_shapes))),
        scratch_shapes=[pltpu.VMEM(v.shape, v.dtype) for v in spare]
        + [
            pltpu.SemaphoreType.DMA((n, 2, depth, 2)),
            pltpu.SemaphoreType.DMA((count_sites(flows, depth),)),
            pltpu.SemaphoreType.DMA((n, 2, 2)),
            pltpu.SemaphoreType.DMA((n, 2, 2)),
            pltpu.SemaphoreType.DMA((n,)),
            pltpu.SemaphoreType.DMA((3,)),
        ],
        compiler_params=pltpu.CompilerParams(
            collective_id=collective_id, has_side_effects=True, vmem_limit_bytes=62 << 20
        ),
    )(*inputs)


def slots_of(flow, d, depth):
    sizes = {"x": 2, "y": 2, "z": depth}
    before = flow["order"][: flow["order"].index(d)]
    return ([2] if d == "z" else []) + [sizes[k] for k in before] + ([depth] if d == "z" else [])


def slot(flow, d, src, side):
    before = flow["order"][: flow["order"].index(d)]
    return (
        ([0 if side > 0 else 1] if d == "z" else [])
        + [src[k] for k in before]
        + ([src["z"]] if d == "z" else [])
    )


def chunk_of(rows, columns):
    wide = 128
    while columns % (2 * wide) == 0 and rows * 2 * wide <= 24 * 1024:
        wide *= 2
    return wide


def scatter_kernel(flows, depth, n_in, n_out, n_made, work, *refs):
    ins, outs = refs[:n_in], refs[n_in : n_in + n_out]
    at = n_in + n_out
    made = refs[at : at + n_made]
    at += n_made
    mine, theirs, slots, marks = [], [], [], []
    for flow in flows:
        if flow["made"]:
            mine.append(made[flow["in"]])
        else:
            mine.append(refs[at])
            at += 1
        theirs.append(refs[at] if flow["cores"] else None)
        at += 1 if flow["cores"] else 0
        slots.append({})
        marks.append({})
        for d in flow["order"]:
            slots[-1][d], marks[-1][d] = refs[at], refs[at + 1]
            at += 2
    sent, core_recv, core_sent, local, extra = refs[at:]
    pos = here(depth)
    greet(pos, flat_sides(flows), depth)
    events = schedule(flows, depth, True)

    def lead(flow, src):
        if not flow["cores"]:
            return (src["z"], src["x"])
        return (src["y"],) + ((src["c"],) if flow["made"] else ()) + (src["z"], src["x"])

    def col(src):
        return (src["y"], slice(None), src["x"])

    def parts(f, own, cols):
        low = flows[f]["columns"][0] if flows[f]["made"] else 0
        return own + (slice(None), pl.ds(pl.multiple_of(low + cols.start, 128), cols.size))

    ready, waits, sites = {}, [], 0

    def begin(chosen):
        for _, f, offsets, parent, children in events:
            key = (f, group_of(offsets))
            if key in ready or f not in chosen:
                continue
            flow = flows[f]
            src = source_of(pos, {d: o for d, o in offsets.items() if d != "z"})
            y = src["y"] if flow["cores"] else 0
            whole = made[flow["in"]] if flow["made"] else ins[flow["in"]]
            loads = []
            if flow["cores"]:
                core = pltpu.make_async_remote_copy(
                    column(whole, flow, beside(src, ("c", 1))),
                    theirs[f].at[col(src)],
                    core_sent.at[f, y, src["x"]],
                    core_recv.at[f, y, src["x"]],
                    device_id=device_of(beside(pos, ("c", 1))),
                    device_id_type=MESH,
                )
                core.start()
                loads.append(core.wait_recv)
                waits.append((None, core.wait_send))
            if not flow["made"]:
                copy = pltpu.make_async_copy(
                    column(whole, flow, src), mine[f].at[col(src)], local.at[f, y, src["x"]]
                )
                copy.start()
                loads.append(copy.wait)
            ready[key] = loads

    begin([f for f, flow in enumerate(flows) if not flow["made"]])
    items = [(e[0], 0, e) for e in events]
    items += [(key, 1, step) for key, step in (work(pos, ins, outs, made, extra) if work else [])]
    items.sort(key=lambda item: item[0])
    for _, kind, item in items:
        if kind == 1:
            after, step = item
            step()
            begin(after)
            continue
        _, f, offsets, parent, children = item
        flow = flows[f]
        for load in ready.get((f, group_of(offsets)), []):
            load()
        ready[(f, group_of(offsets))] = []
        src = source_of(pos, offsets)
        own = lead(flow, src)
        send = None
        if parent is not None:
            d, toward = parent
            place = tuple(slot(flow, d, src, -toward))
            send = pltpu.make_async_remote_copy(
                mine[f].at[parts(f, own, pl.ds(0, flow["columns"][1]))],
                slots[f][d].at[place] if place else slots[f][d],
                sent.at[sites],
                marks[f][d].at[place if place else (0,)],
                device_id=device_of(beside(pos, parent)),
                device_id_type=MESH,
            )
            sites += 1

        def step():
            rows, columns = mine[f].shape[-2], flow["columns"][1]
            wide = chunk_of(rows, columns)
            terms = []
            for side in children:
                d = side[0]
                place = tuple(slot(flow, d, src, side[1]))
                buf = slots[f][d].at[place] if place else slots[f][d]
                there = exists(pos, side, depth)
                when(
                    there,
                    lambda: pltpu.make_async_copy(
                        buf, buf, marks[f][d].at[place if place else (0,)]
                    ).wait(),
                )
                terms.append((place, d, there))

            def total(cols):
                value = mine[f][parts(f, own, cols)].astype(jnp.float32)
                if flow["cores"]:
                    core = (src["y"], src["z"], src["x"], slice(None), cols)
                    value += theirs[f][core].astype(jnp.float32)
                return value

            def put(cols, value):
                if send is None:
                    low = flow["out_low"]
                    outs[flow["out"]][:, pl.ds(pl.multiple_of(low + cols.start, 128), wide)] = value
                else:
                    mine[f][parts(f, own, cols)] = value.astype(mine[f].dtype)

            def with_terms(chosen):
                def go():
                    def body(k, carry):
                        cols = pl.ds(pl.multiple_of(k * wide, wide), wide)
                        value = total(cols)
                        for place, d in chosen:
                            value += slots[f][d][place + (slice(None), cols)].astype(jnp.float32)
                        put(cols, value)
                        return carry

                    lax.fori_loop(0, columns // wide, body, 0)

                return go

            always = [(p, d) for p, d, there in terms if there is None]
            maybe = [(p, d, there) for p, d, there in terms if there is not None]
            if flow["cores"] or always or maybe:
                for picks in itertools.product((True, False), repeat=len(maybe)):
                    cond = None
                    for (p, d, there), pick in zip(maybe, picks):
                        test = there if pick else jnp.logical_not(there)
                        cond = test if cond is None else jnp.logical_and(cond, test)
                    chosen = always + [(p, d) for (p, d, _), pick in zip(maybe, picks) if pick]
                    if not chosen and not flow["cores"] and send is not None:
                        continue
                    when(cond, with_terms(chosen))
            if send is not None:
                send.start()

        cond = in_line(pos, offsets, depth)
        when(cond, step)
        if send is not None:
            waits.append((cond, send.wait_send))
    for cond, finish in waits:
        when(cond, finish)


def scatter(flows, depth, inputs, out_shapes, collective_id, work, made, in_vmem, spare):
    hbm = pl.BlockSpec(memory_space=pl.ANY)
    vmem = pl.BlockSpec(memory_space=pltpu.VMEM)
    n = len(flows)
    scratch = [pltpu.VMEM(m.shape, m.dtype) for m in made + spare]
    for flow in flows:
        source = made[flow["in"]] if flow["made"] else inputs[flow["in"]]
        rows, kind = source.shape[-2], source.dtype
        unit = (rows, flow["columns"][1])
        whole = ((2, depth, 2) if flow["cores"] else (depth, 2)) + unit
        if not flow["made"]:
            scratch.append(pltpu.VMEM(whole, kind))
        if flow["cores"]:
            scratch.append(pltpu.VMEM(whole, kind))
        for d in flow["order"]:
            places = tuple(slots_of(flow, d, depth))
            scratch.append(pltpu.VMEM(places + unit, kind))
            scratch.append(pltpu.SemaphoreType.DMA(places if places else (1,)))
    scratch += [
        pltpu.SemaphoreType.DMA((len(schedule(flows, depth)),)),
        pltpu.SemaphoreType.DMA((n, 2, 2)),
        pltpu.SemaphoreType.DMA((n, 2, 2)),
        pltpu.SemaphoreType.DMA((n, 2, 2)),
        pltpu.SemaphoreType.DMA((3,)),
    ]
    kernel = functools.partial(
        scatter_kernel, flows, depth, len(inputs), len(out_shapes), len(made + spare), work
    )
    return pl.pallas_call(
        kernel,
        out_shape=tuple(out_shapes),
        in_specs=[vmem if i in in_vmem else hbm for i in range(len(inputs))],
        out_specs=tuple([vmem] * len(out_shapes)),
        scratch_shapes=scratch,
        compiler_params=pltpu.CompilerParams(
            collective_id=collective_id, has_side_effects=True, vmem_limit_bytes=62 << 20
        ),
    )(*inputs)


ZXY, ZYX, XZY, YZX = ("z", "x", "y"), ("z", "y", "x"), ("x", "z", "y"), ("y", "z", "x")


def flow_of(order, source, which, low, wide, place, cores=True, made=False):
    return dict(
        order=order,
        cores=cores,
        columns=(low, wide),
        in_columns=(low, wide),
        out_low=low,
        made=made,
        out=which,
        when=place,
        **{"in": source},
    )


def layout_of(large, own, span):
    dp, blk = lax.axis_size("dp"), lax.axis_size("blk")
    fits = all(v.shape[0] % 8 == 0 and v.shape[1] % 128 == 0 for v in large)
    fits = fits and own <= 128 and span <= 128
    width, wide = large[1].shape[1], large[2].shape[1]
    fits = fits and wide % width == 0 and dp * blk % (wide // width) == 0
    if fits and dp == 2 * CORES and blk % 2 == 0 and 2 <= blk // 2 <= 4:
        return blk // 2
    return None


def flat_rows(whole):
    return whole.reshape(-1, whole.shape[-1])


def flat_rows(whole):
    return whole.reshape(-1, whole.shape[-1])


def forward_kernel(tokens, w_qkv, flat, large, depth):
    rows, width = tokens.shape
    n, high = 4 * CORES * depth, flat.shape[0]
    own, wide = width // n, large[1].shape[1]
    count, span = wide // width, wide // n
    bf16, f32 = jnp.bfloat16, jnp.float32
    column_of, lane_of = np.arange(width), np.arange(128)[:, None]
    lanes = np.stack([lane_of == column_of % k for k in (own, span)])
    places = [np.arange(k)[:, None, None] == column_of // (width // k) for k in (n, n // count)]

    def work(pos, ins, outs, extra):
        lanes_ref, place_ref, up_place_ref = ins[-3:]
        small, q_ref, narrow, up_bias, attn_ref, lse_ref, blocks, every, dense, kv_ref = (
            outs[3:4] + outs[7:]
        )
        saves = [
            pltpu.make_async_copy(held, kept, extra.at[k])
            for k, (held, kept) in enumerate(zip((every, dense, kv_ref), outs[4:7]))
        ]

        def unpack():
            for k in range(3):
                at = pl.ds(k * width, width)
                part = blocks[:, :, :, :, :, at].astype(f32).reshape(width, width)
                dense[:, at] = part.astype(bf16)
            saves[1].start()

        def project():
            rows_of = small[...].reshape(n * high, 128)
            spread = jnp.dot(rows_of, lanes_ref[0], preferred_element_type=f32)
            narrow[...] = jnp.sum(spread.reshape(n, high, width) * place_ref[...], axis=0)
            spread = jnp.dot(rows_of, lanes_ref[1], preferred_element_type=f32)
            spread = spread.reshape(count, n // count, high, width)
            for k in range(count):
                up_bias[k] = jnp.sum(spread[k] * up_place_ref[...], axis=0)
            query_bias, value_bias = narrow[0:1, :], narrow[1:2, :]
            mine = every[pos["z"], pos["x"]]
            query = jnp.dot(mine, dense[:, :width], preferred_element_type=f32)
            q_ref[...] = (query + query_bias).astype(bf16)
            later = jnp.concatenate([jnp.zeros_like(value_bias), value_bias], axis=1)

            def line(z, carry):
                some = every[z].reshape(2 * rows, width)
                part = jnp.dot(some, dense[:, width:], preferred_element_type=f32) + later
                kv_ref[z] = part.astype(bf16).reshape(2, rows, 2 * width)
                return carry

            lax.fori_loop(0, depth, line, 0)
            saves[0].start()
            saves[2].start()

        def saved():
            for save in saves:
                save.wait()

        def keys_of(at):
            return kv_ref[:, :, :, at].reshape(-1, PAIR)

        pair = functools.partial(attend_pair, width, q_ref, keys_of, attn_ref, lse_ref)
        steps = in_steps(width // PAIR, len(ATTEND), pair)
        found = [(UNPACK, ((0,), unpack)), (PROJECT, ((1, 2), project)), (99, ((), saved))]
        return found + [(key, ((), step)) for key, step in zip(ATTEND, steps)]

    shapes = whole_shapes(list(large) + [flat], depth) + [
        jax.ShapeDtypeStruct((depth, 2, rows, width), bf16),
        jax.ShapeDtypeStruct((width, 3 * width), bf16),
        jax.ShapeDtypeStruct((depth, 2, rows, 2 * width), bf16),
        jax.ShapeDtypeStruct((rows, width), bf16),
        jax.ShapeDtypeStruct((high, width), f32),
        jax.ShapeDtypeStruct((count, high, width), f32),
    ]
    shapes += list(attend_shapes(rows, width))
    inputs = [w_qkv, flat, tokens] + list(large)
    flows = [
        flow_of(GATHER_ORDERS[0], 0, len(shapes), 0, 3 * width, FIRST),
        flow_of(GATHER_ORDERS[1], 1, 3, 0, 128, FIRST),
        flow_of(("z", "x"), 2, len(shapes) + 1, 0, width, FIRST, cores=False),
    ]
    for i, (order, v) in enumerate(zip(GATHER_ORDERS[2:], large)):
        flows.append(flow_of(order, 3 + i, i, 0, v.shape[1], LATER))
    inputs += [jnp.asarray(lanes, bf16)]
    inputs += [jnp.asarray(np.broadcast_to(p, (len(p), high, width)), f32) for p in places]
    return gather(
        flows,
        depth,
        inputs,
        shapes,
        whole_shapes([w_qkv], depth) + shapes[4:7],
        1,
        work,
        in_vmem=range(len(inputs) - 3, len(inputs)),
        out_vmem=(3,) + tuple(range(7, len(shapes))),
    )


GATHER_ORDERS = (ZXY, ZYX, ZXY, XZY, YZX)
FIRST, LATER = (0, 1, 2, 3, 4, 5), (1.5, 2.5, 3.5, 4.5, 5.05, 6.0)
UNPACK, PROJECT, ATTEND = 5.1, 5.2, (6.2, 6.7, 7.7)
SCATTER_ORDERS = (ZXY, XZY, YZX, ZXY, ZYX)
BACK, EARLY = (0, 1.5, 2.5), (1.1, 2.1, 3.3, 4.3, 5.3, 6.3)
WEIGHTS, TOKENS, LAST = 2.6, 2.7, (3.0, 3.4, 4.4, 5.4, 6.4, 7.4)


def whole_shapes(large, depth):
    return [jax.ShapeDtypeStruct((2, CORES, depth, 2) + v.shape, v.dtype) for v in large]


def backward_kernel(query, kv, d_attn, lse, delta, every, dense, sums, d_up_bias, grads, large, depth):
    bf16, f32 = jnp.bfloat16, jnp.float32
    rows, width = query.shape
    n = 4 * CORES * depth
    own = width // n
    wide = d_up_bias.shape[1]
    count, span = wide // width, wide // n
    column_of = np.arange(width)
    line = np.arange(8 * n)[:, None] // 8
    places = [line == column_of // own, line % (n // count) == column_of // span]
    lanes = [column_of[:, None] % k == np.arange(128) for k in (own, span)]
    small = jax.ShapeDtypeStruct((2, CORES, depth, 2, 16, 128), f32)

    def work(pos, ins, outs, made, extra):
        q_ref, do_ref, lse_ref, delta_ref = ins[-10:-6]
        sums_ref, up_ref, place_ref, up_place_ref, lanes_ref, up_lanes_ref = ins[-6:]
        token_part, d_whole, small_made, dq_ref, dkv_ref, sum_ref, kv_ref, every_ref, w_ref = made
        loads = [
            pltpu.make_async_copy(kept, held, extra.at[k])
            for k, (kept, held) in enumerate(zip(ins[-13:-10], (kv_ref, every_ref, w_ref)))
        ]
        for load in loads:
            load.start()

        def keys_of(at):
            return kv_ref[:, :, :, at].reshape(-1, PAIR)

        def put_keys(at, value):
            dkv_ref[:, at] = value.astype(bf16)

        def put_values(at, val, value):
            sum_ref[:, at] = jnp.sum(value, axis=0, keepdims=True)
            dkv_ref[:, val] = value.astype(bf16)

        def pair(i):
            attend_back_pair(
                width,
                q_ref,
                keys_of,
                do_ref,
                lambda k: lse_ref[pl.ds(2 * i + k, 1), :],
                lambda k: delta_ref[pl.ds(2 * i + k, 1), :],
                dq_ref,
                put_keys,
                put_values,
                i,
            )

        def weights():
            loads[1].wait()
            whole = every_ref[...].reshape(-1, width)
            for k in range(3):
                if k == 0:
                    part = contract_rows(every_ref[pos["z"], pos["x"]], dq_ref[...].astype(bf16))
                else:
                    part = contract_rows(whole, dkv_ref[:, (k - 1) * width : k * width])
                part = part.reshape(2, CORES, depth, 2, own, width).astype(bf16)
                d_whole[:, :, :, :, :, k * width : (k + 1) * width] = part
            query_sum = jnp.sum(dq_ref[...], axis=0, keepdims=True)
            eight = jnp.concatenate([query_sum, sum_ref[...], sums_ref[2:8, :]], axis=0)
            whole = jnp.broadcast_to(eight[None], (n, 8, width)).reshape(8 * n, width)
            narrow = jnp.dot(
                whole * place_ref[...],
                lanes_ref[...],
                preferred_element_type=f32,
                precision=lax.Precision.HIGHEST,
            )
            spread = [
                jnp.broadcast_to(up_ref[:, k * width : (k + 1) * width], (8 * n // count, width))
                for k in range(count)
            ]
            up = jnp.dot(
                jnp.concatenate(spread, axis=0) * up_place_ref[...],
                up_lanes_ref[...],
                preferred_element_type=f32,
                precision=lax.Precision.HIGHEST,
            )
            lead = (2, CORES, depth, 2, 8, 128)
            small_made[:, :, :, :, 0:8, :] = narrow.reshape(lead)
            small_made[:, :, :, :, 8:16, :] = up.reshape(lead)

        def tokens_gradient():
            loads[2].wait()

            def line(z, carry):
                at = pl.ds(pl.multiple_of(z * 2 * rows, 2 * rows), 2 * rows)
                part = contract_cols(dkv_ref[at, :], w_ref[:, width:])
                token_part[z] = part.astype(bf16).reshape(2, rows, width)
                return carry

            lax.fori_loop(0, depth, line, 0)
            outs[-1][...] = contract_cols(dq_ref[...].astype(bf16), w_ref[:, :width])

        steps = in_steps(width // PAIR, len(BACK), pair)
        found = [(-1, ((), loads[0].wait))]
        found += [(key, ((), step)) for key, step in zip(BACK, steps)]
        return found + [(WEIGHTS, ((3, 4), weights)), (TOKENS, ((5,), tokens_gradient))]

    blocks = [g.reshape((2, CORES, depth, 2) + v.shape) for g, v in zip(grads, large)]
    made = [
        jax.ShapeDtypeStruct(every.shape, bf16),
        jax.ShapeDtypeStruct((2, CORES, depth, 2, own, 3 * width), bf16),
        jax.ShapeDtypeStruct(small.shape, f32),
    ]
    spare = [
        jax.ShapeDtypeStruct((rows, width), f32),
        jax.ShapeDtypeStruct((2 * depth * rows, 2 * width), bf16),
        jax.ShapeDtypeStruct((1, width), f32),
        kv,
        every,
        dense,
    ]
    flows = []
    for i, (order, v) in enumerate(zip(SCATTER_ORDERS, large)):
        flows.append(flow_of(order, i, i, 0, v.shape[1], EARLY))
    flows.append(flow_of(SCATTER_ORDERS[3], 1, 3, 0, 3 * width, LAST, made=True))
    flows.append(flow_of(SCATTER_ORDERS[4], 2, 4, 0, 128, LAST, made=True))
    flows.append(flow_of(("z", "x"), 0, 5, 0, width, LAST, cores=False, made=True))
    shapes = [jax.ShapeDtypeStruct(v.shape, f32) for v in large]
    shapes += [
        jax.ShapeDtypeStruct((own, 3 * width), f32),
        jax.ShapeDtypeStruct(small.shape[-2:], f32),
        jax.ShapeDtypeStruct((rows, width), f32),
        jax.ShapeDtypeStruct((rows, width), f32),
    ]
    inputs = blocks + [kv, every, dense, query, d_attn, lse, delta, sums, d_up_bias]
    inputs += [jnp.asarray(v, f32) for v in places + lanes]
    return scatter(
        flows, depth, inputs, shapes, 2, work, made, range(len(blocks) + 3, len(inputs)), spare
    )


def middle_kernel(chunk, *refs):
    bf16, f32 = jnp.bfloat16, jnp.float32
    tokens, attn, lse, cotangent, narrow, up_bias, head_of, wo_in, wu_in, wd_in = refs[:10]
    out, dh1_out, d_attn_out, delta_out, lse_out, sums, d_up_bias = refs[10:17]
    d_wo_out, d_wu_out, d_wd_out = refs[17:20]
    wo, wu, wd, d_wo, d_wu, d_wd, slope, act, arrived, left = refs[20:]
    count = wu.shape[0]

    def cut(c):
        return pl.ds(c * chunk, chunk)

    loads = [pltpu.make_async_copy(wo_in, wo, arrived.at[0])]
    for c in range(count):
        loads.append(pltpu.make_async_copy(wu_in.at[:, cut(c)], wu.at[c], arrived.at[1 + 2 * c]))
        loads.append(pltpu.make_async_copy(wd_in.at[cut(c), :], wd.at[c], arrived.at[2 + 2 * c]))
    for load in loads:
        load.start()

    def line(k):
        return narrow[k : k + 1, :]

    def total(value):
        return jnp.sum(value, axis=0, keepdims=True)

    logs = [lse[k] for k in range(lse.shape[0])]
    rows = tokens.shape[0]
    logs.append(jnp.zeros((rows, 128 - 2 * len(logs)), f32))
    lse_out[...] = jnp.concatenate(logs, axis=1).T[: lse_out.shape[0]]
    loads[0].wait()
    hidden = tokens[...].astype(f32) + line(2)
    hidden += jnp.dot(attn[...], wo[...], preferred_element_type=f32)
    y1, xhat1, rstd1 = layernorm_forward(hidden, line(3), line(5))
    y1_low = y1.astype(bf16)
    hidden = y1 + line(7)
    for c in range(count):
        loads[1 + 2 * c].wait()
        up = jnp.dot(y1_low, wu[c], preferred_element_type=f32) + up_bias[c, 8:9, :]
        cdf = 0.5 * (1.0 + lax.erf(up * 0.7071067811865476))
        slope[:, cut(c)] = cdf + up * jnp.exp(-0.5 * up * up) * 0.3989422804014327
        act[:, cut(c)] = (up * cdf).astype(bf16)
        loads[2 + 2 * c].wait()
        hidden += jnp.dot(act[:, cut(c)], wd[c], preferred_element_type=f32)
    y2, xhat2, rstd2 = layernorm_forward(hidden, line(4), line(6))
    out[...] = y2.astype(bf16)
    gradient = cotangent[...].astype(f32)
    dh2 = layernorm_backward(gradient, xhat2, rstd2, line(4))
    sums[0:2, :] = jnp.zeros((2, sums.shape[1]), f32)
    sums[4:5, :] = total(gradient * xhat2)
    sums[6:7, :] = total(gradient)
    sums[7:8, :] = total(dh2)
    dh2_low = dh2.astype(bf16)
    stores = []
    dy1 = dh2
    for c in range(count):
        d_wd[c] = contract_rows(act[:, cut(c)], dh2_low).astype(bf16)
        stores.append(pltpu.make_async_copy(d_wd.at[c], d_wd_out.at[cut(c), :], left.at[1 + 2 * c]))
        stores[-1].start()
        d_up_f = contract_cols(dh2_low, wd[c]) * slope[:, cut(c)]
        d_up_bias[:, cut(c)] = total(d_up_f)
        d_up = d_up_f.astype(bf16)
        d_wu[c] = contract_rows(y1_low, d_up).astype(bf16)
        stores.append(pltpu.make_async_copy(d_wu.at[c], d_wu_out.at[:, cut(c)], left.at[2 + 2 * c]))
        stores[-1].start()
        dy1 += contract_cols(d_up, wu[c])
    dh1 = layernorm_backward(dy1, xhat1, rstd1, line(3))
    sums[2:3, :] = total(dh1)
    sums[3:4, :] = total(dy1 * xhat1)
    sums[5:6, :] = total(dy1)
    dh1_out[...] = dh1
    dh1_low = dh1.astype(bf16)
    d_wo[...] = contract_rows(attn[...], dh1_low).astype(bf16)
    stores.append(pltpu.make_async_copy(d_wo, d_wo_out, left.at[0]))
    stores[-1].start()
    d_attn = contract_cols(dh1_low, wo[...]).astype(bf16)
    d_attn_out[...] = d_attn
    delta_out[...] = lax.dot_general(
        head_of[...],
        d_attn.astype(f32) * attn[...].astype(f32),
        (((1,), (1,)), ((), ())),
        preferred_element_type=f32,
        precision=lax.Precision.HIGHEST,
    )
    for store in stores:
        store.wait()


def middle(tokens, attn, lse, cotangent, narrow, up_bias, w_out, w_up, w_down):
    bf16, f32 = jnp.bfloat16, jnp.float32
    rows, width = tokens.shape
    wide = w_up.shape[1]
    chunk = width
    count = wide // chunk
    lines = -(-(width // HEAD) // 8) * 8
    head_of = np.arange(lines)[:, None] == np.arange(width) // HEAD
    vmem, hbm = pl.BlockSpec(memory_space=pltpu.VMEM), pl.BlockSpec(memory_space=pl.ANY)
    shapes = [
        ((rows, width), bf16),
        ((rows, width), f32),
        ((rows, width), bf16),
        ((lines, rows), f32),
        ((lines, rows), f32),
        ((8, width), f32),
        ((1, wide), f32),
        (w_out.shape, bf16),
        (w_up.shape, bf16),
        (w_down.shape, bf16),
    ]
    chunks = (count, width, chunk)
    return pl.pallas_call(
        functools.partial(middle_kernel, chunk),
        out_shape=tuple(jax.ShapeDtypeStruct(*v) for v in shapes),
        in_specs=[vmem] * 7 + [hbm] * 3,
        out_specs=tuple([vmem] * 7 + [hbm] * 3),
        scratch_shapes=[
            pltpu.VMEM(w_out.shape, bf16),
            pltpu.VMEM(chunks, bf16),
            pltpu.VMEM(chunks, bf16),
            pltpu.VMEM(w_out.shape, bf16),
            pltpu.VMEM(chunks, bf16),
            pltpu.VMEM(chunks, bf16),
            pltpu.VMEM((rows, wide), f32),
            pltpu.VMEM((rows, wide), bf16),
            pltpu.SemaphoreType.DMA((1 + 2 * count,)),
            pltpu.SemaphoreType.DMA((1 + 2 * count,)),
        ],
        compiler_params=pltpu.CompilerParams(vmem_limit_bytes=60 << 20),
        name="ffn",
    )(
        tokens, attn, lse, cotangent, narrow, up_bias, jnp.asarray(head_of, f32), w_out, w_up, w_down
    )


def finish_kernel(*refs):
    parts, row, dh1, query_part, token_sum = refs[:4], refs[4], refs[5], refs[6], refs[7]
    d_tokens, grads, pairs, singles, up = refs[8], refs[9:13], refs[13:16], refs[16:18], refs[18]
    d_tokens[...] = dh1[...] + query_part[...] + token_sum[...]
    for part, grad in zip(parts, grads):
        grad[...] = part[...]
    own = pairs[0].shape[1]
    for k, pair in zip((0, 3, 5), pairs):
        pair[...] = row[k : k + 2, :own]
    for k, single in zip((2, 7), singles):
        single[...] = row[k : k + 1, :own]
    up[...] = row[8:9, : up.shape[1]]


def finish(parts, row, dh1, query_part, token_sum, own, span):
    f32 = jnp.float32
    shapes = [dh1.shape] + [p.shape for p in parts] + [(2, own)] * 3 + [(1, own)] * 2 + [(1, span)]
    vmem = pl.BlockSpec(memory_space=pltpu.VMEM)
    return pl.pallas_call(
        finish_kernel,
        out_shape=tuple(jax.ShapeDtypeStruct(shape, f32) for shape in shapes),
        in_specs=[vmem] * 8,
        out_specs=tuple([vmem] * len(shapes)),
        name="finish",
    )(*parts, row, dh1, query_part, token_sum)


SPARE = 16


def split_owner(full, count):
    p = full.shape[0]
    return full.reshape(p, count, -1).transpose(1, 0, 2).reshape(count, -1)


def join_owner(parts, p):
    count = parts.shape[0]
    return parts.reshape(count, p, -1).transpose(1, 0, 2).reshape(p, -1)


def plain_on_device(
    tokens,
    w_qkv,
    qv_bias,
    w_out,
    out_bias,
    norm_gain,
    norm_bias,
    w_up,
    up_bias,
    w_down,
    down_bias,
    cotangent,
):
    f32 = jnp.float32
    bf16 = jnp.bfloat16
    rows, width = tokens.shape
    heads = width // HEAD
    n = lax.axis_size("dp") * lax.axis_size("blk")
    small = [qv_bias, out_bias, norm_gain, norm_bias, up_bias, down_bias]
    sizes = [v.size for v in small]
    flat = jnp.concatenate([v.reshape(-1) for v in small])
    flat = jnp.pad(flat, (0, SPARE * width - flat.size)).reshape(SPARE, width)
    large = [w_qkv, w_out, w_up, w_down]
    shard = jnp.concatenate(
        [v[:, i : i + width] for v in large for i in range(0, v.shape[1], width)] + [flat]
    )
    packed = lax.all_gather(shard, ("dp", "blk"), axis=0)
    wholes, at = [], 0
    for v in large:
        high, columns = v.shape
        blocks = []
        for _ in range(columns // width):
            blocks.append(packed[:, at : at + high].reshape(n * high, width))
            at += high
        wholes.append(jnp.concatenate(blocks, axis=1))
    wq_full, wo_full, wu_full, wd_full = wholes
    row_full = packed[:, at:].reshape(n, -1)
    parts, at = [], 0
    for size, v in zip(sizes, small):
        parts.append(join_owner(row_full[:, at : at + size], 2 if v.ndim == 2 else 1))
        at += size
    qvb_full, bo_full, gain_full, shift_full, bu_full, bd_full = parts
    bo_full, bu_full, bd_full = bo_full[0], bu_full[0], bd_full[0]
    norm_gain_pair = gain_full.astype(f32)
    norm_offset_pair = shift_full.astype(f32)
    qvb = qvb_full.astype(f32)
    bias_row = jnp.concatenate([qvb[0], jnp.zeros((width,), f32), qvb[1]])
    qkv = (jnp.dot(tokens, wq_full, preferred_element_type=f32) + bias_row).astype(bf16)
    query = qkv[:, :width]
    kv = lax.all_gather(qkv[:, width:], "blk", axis=0, tiled=True)
    attn, lse = attend(query, kv)
    first_hidden = (
        tokens.astype(f32)
        + jnp.dot(attn, wo_full, preferred_element_type=f32)
        + bo_full.astype(f32)
    )
    first_norm_output, first_normalized, first_inverse_deviation = layernorm_forward(
        first_hidden, norm_gain_pair[0], norm_offset_pair[0]
    )
    y1_low = first_norm_output.astype(bf16)
    up = jnp.dot(y1_low, wu_full, preferred_element_type=f32) + bu_full.astype(f32)
    act = jax.nn.gelu(up, approximate=False).astype(bf16)
    second_hidden = (
        first_norm_output + jnp.dot(act, wd_full, preferred_element_type=f32) + bd_full.astype(f32)
    )
    output_float, second_normalized, second_inverse_deviation = layernorm_forward(
        second_hidden, norm_gain_pair[1], norm_offset_pair[1]
    )
    output = output_float.astype(bf16)
    wq_b, wo_b, wu_b, wd_b = wq_full, wo_full, wu_full, wd_full
    gain_pair_block = norm_gain_pair
    incoming_gradient = cotangent.astype(f32)
    second_gain_gradient = jnp.sum(incoming_gradient * second_normalized, axis=0)
    d_shift2 = jnp.sum(incoming_gradient, axis=0)
    second_hidden_gradient = layernorm_backward(
        incoming_gradient, second_normalized, second_inverse_deviation, gain_pair_block[1]
    )
    dh2_low = second_hidden_gradient.astype(bf16)
    d_w_down = contract_rows(act, dh2_low)
    d_down_bias = jnp.sum(second_hidden_gradient, axis=0)
    d_up_f = contract_cols(dh2_low, wd_b) * gelu_grad(up)
    d_up_bias = jnp.sum(d_up_f, axis=0)
    d_up = d_up_f.astype(bf16)
    d_w_up = contract_rows(y1_low, d_up)
    first_output_gradient = second_hidden_gradient + contract_cols(d_up, wu_b)
    first_gain_gradient = jnp.sum(first_output_gradient * first_normalized, axis=0)
    d_shift1 = jnp.sum(first_output_gradient, axis=0)
    first_hidden_gradient = layernorm_backward(
        first_output_gradient, first_normalized, first_inverse_deviation, gain_pair_block[0]
    )
    dh1_low = first_hidden_gradient.astype(bf16)
    d_w_out = contract_rows(attn, dh1_low)
    d_out_bias = jnp.sum(first_hidden_gradient, axis=0)
    d_gains = jnp.stack([first_gain_gradient, second_gain_gradient])
    d_shifts = jnp.stack([d_shift1, d_shift2])
    d_attn = contract_cols(dh1_low, wo_b).astype(bf16)
    delta = jnp.sum((d_attn.astype(f32) * attn.astype(f32)).reshape(rows, heads, HEAD), axis=-1).T
    d_query, d_kv_all = attend_back(
        query, kv, d_attn, lse.transpose(0, 2, 1), delta.reshape(heads // 2, 2, rows)
    )
    d_kv = lax.psum_scatter(d_kv_all, "blk", scatter_dimension=0, tiled=True).astype(f32)
    d_key = d_kv[:, :width]
    d_value = d_kv[:, width:]
    d_qv = jnp.stack([jnp.sum(d_query, axis=0), jnp.sum(d_value, axis=0)])
    d_qkv = jnp.concatenate([d_query, d_key, d_value], axis=1).astype(bf16)
    d_w_qkv = contract_rows(tokens, d_qkv)
    d_tokens = first_hidden_gradient + contract_cols(d_qkv, wq_b)
    grads = [d_qv, d_out_bias[None], d_gains, d_shifts, d_up_bias[None], d_down_bias[None]]
    row = jnp.concatenate([split_owner(v, n) for v in grads], axis=1)
    row = jnp.pad(row, ((0, 0), (0, SPARE * width - row.shape[1]))).reshape(n, SPARE, width)
    blocks = []
    for d_full, v in zip((d_w_qkv, d_w_out, d_w_up, d_w_down), large):
        d_low = d_full.astype(bf16).reshape((n,) + v.shape)
        blocks += [d_low[:, :, i : i + width] for i in range(0, v.shape[1], width)]
    packed = jnp.concatenate(blocks + [row.astype(bf16)], axis=1)
    packed = lax.psum_scatter(packed, ("dp", "blk"), scatter_dimension=0, tiled=True)[0]
    wholes, at = [], 0
    for v in large:
        high, columns = v.shape
        blocks = []
        for _ in range(columns // width):
            blocks.append(packed[at : at + high])
            at += high
        wholes.append(jnp.concatenate(blocks, axis=1).astype(f32))
    g_wqkv, g_wout, g_wup, g_wdown = wholes
    row, at, parts = packed[at:].reshape(-1).astype(f32), 0, []
    for size, v in zip(sizes, small):
        parts.append(row[at : at + size].reshape(v.shape))
        at += size
    g_qv, g_bout, g_gain, g_shift, g_bup, g_bdown = parts
    return (
        output,
        d_tokens,
        g_wqkv,
        g_qv,
        g_wout,
        g_bout,
        g_gain,
        g_shift,
        g_wup,
        g_bup,
        g_wdown,
        g_bdown,
    )


def on_device(
    tokens,
    w_qkv,
    qv_bias,
    w_out,
    out_bias,
    norm_gain,
    norm_bias,
    w_up,
    up_bias,
    w_down,
    down_bias,
    cotangent,
):
    f32 = jnp.float32
    bf16 = jnp.bfloat16
    rows, width = tokens.shape
    n = lax.axis_size("dp") * lax.axis_size("blk")
    own = out_bias.shape[0]
    span = up_bias.shape[0]
    depth = layout_of([w_qkv, w_out, w_up, w_down], own, span)
    if depth is None:
        return plain_on_device(
            tokens,
            w_qkv,
            qv_bias,
            w_out,
            out_bias,
            norm_gain,
            norm_bias,
            w_up,
            up_bias,
            w_down,
            down_bias,
            cotangent,
        )
    large = [w_out, w_up, w_down]
    narrow = jnp.concatenate([qv_bias, out_bias[None], norm_gain, norm_bias, down_bias[None]])
    flat = jnp.concatenate(
        [
            jnp.pad(narrow, ((0, 0), (0, 128 - own))),
            jnp.pad(up_bias[None], ((0, 7), (0, 128 - span))),
        ]
    )
    outs = forward_kernel(tokens, w_qkv, flat, large, depth)
    wo_full, wu_full, wd_full = [flat_rows(w) for w in outs[:3]]
    every, dense, kv, query, narrow_full, bu_full, attn, lse = outs[4:]
    output, dh1, d_attn, delta, lse, sums, d_up_bias, d_w_out, d_w_up, d_w_down = middle(
        tokens, attn, lse, cotangent, narrow_full, bu_full, wo_full, wu_full, wd_full
    )
    g_wout, g_wup, g_wdown, g_wqkv, row, token_sum, query_part = backward_kernel(
        query,
        kv,
        d_attn,
        lse,
        delta,
        every,
        dense,
        sums,
        d_up_bias,
        [d_w_out, d_w_up, d_w_down],
        large,
        depth,
    )
    d_tokens, g_wqkv, g_wout, g_wup, g_wdown, g_qv, g_gain, g_shift, g_bout, g_bdown, g_bup = finish(
        [g_wqkv, g_wout, g_wup, g_wdown], row, dh1, query_part, token_sum, own, span
    )
    g_bout, g_bdown, g_bup = g_bout[0], g_bdown[0], g_bup[0]
    return (
        output,
        d_tokens,
        g_wqkv,
        g_qv,
        g_wout,
        g_bout,
        g_gain,
        g_shift,
        g_wup,
        g_bup,
        g_wdown,
        g_bdown,
    )


def solution(mesh):
    return jax.shard_map(
        on_device,
        mesh=mesh,
        in_specs=(
            P(("dp", "blk"), None),
            P(("dp", "blk"), None),
            P(None, ("dp", "blk")),
            P(("dp", "blk"), None),
            P(("dp", "blk")),
            P(None, ("dp", "blk")),
            P(None, ("dp", "blk")),
            P(("dp", "blk"), None),
            P(("dp", "blk")),
            P(("dp", "blk"), None),
            P(("dp", "blk")),
            P(("dp", "blk"), None),
        ),
        out_specs=(
            P(("dp", "blk"), None),
            P(("dp", "blk"), None),
            P(("dp", "blk"), None),
            P(None, ("dp", "blk")),
            P(("dp", "blk"), None),
            P(("dp", "blk")),
            P(None, ("dp", "blk")),
            P(None, ("dp", "blk")),
            P(("dp", "blk"), None),
            P(("dp", "blk")),
            P(("dp", "blk"), None),
            P(("dp", "blk")),
        ),
        check_vma=False,
    )
```

```python
import functools
import itertools

import jax
import jax.numpy as jnp
import numpy as np
from jax import lax
from jax.experimental import pallas as pl
from jax.experimental.pallas import tpu as pltpu
from jax.sharding import PartitionSpec as P

HEAD = 64


EPS = 1e-05
SCALE = 0.125


def layernorm_forward(h, norm_gain_vector, norm_offset):
    row_average = jnp.mean(h, axis=-1, keepdims=True)
    centered_input = h - row_average
    var = jnp.mean(centered_input * centered_input, axis=-1, keepdims=True)
    inverse_deviation = lax.rsqrt(var + EPS)
    normalized_input = centered_input * inverse_deviation
    return (normalized_input * norm_gain_vector + norm_offset, normalized_input, inverse_deviation)


def layernorm_backward(incoming_gradient, normalized_input, inverse_deviation, norm_gain_vector):
    scaled_values = incoming_gradient * norm_gain_vector
    return inverse_deviation * (
        scaled_values
        - jnp.mean(scaled_values, axis=-1, keepdims=True)
        - normalized_input * jnp.mean(scaled_values * normalized_input, axis=-1, keepdims=True)
    )


def gelu_grad(up):
    cdf = 0.5 * (1.0 + jax.scipy.special.erf(up * 0.7071067811865476))
    return cdf + up * jnp.exp(-0.5 * up * up) * 0.3989422804014327


def contract_rows(left, right):
    return lax.dot_general(
        left, right, (((0,), (0,)), ((), ())), preferred_element_type=jnp.float32
    )


def contract_cols(left, right):
    return lax.dot_general(
        left, right, (((1,), (1,)), ((), ())), preferred_element_type=jnp.float32
    )


PAIR = 2 * HEAD


def attend_pair(width, q_ref, keys_of, attn_ref, lse_ref, i):
    at = pl.ds(pl.multiple_of(i * PAIR, PAIR), PAIR)
    q2 = q_ref[:, at]
    k2 = keys_of(at)
    v2 = keys_of(pl.ds(pl.multiple_of(width + i * PAIR, PAIR), PAIR))
    outs, logs = [], []
    for j in range(2):
        own = slice(j * HEAD, (j + 1) * HEAD)
        scores = contract_cols(q2[:, own], k2[:, own]) * SCALE
        peak = jnp.max(scores, axis=1, keepdims=True)
        weights = jnp.exp(scores - peak)
        total = jnp.sum(weights, axis=1, keepdims=True)
        part = jnp.dot(
            weights.astype(jnp.bfloat16), v2[:, own], preferred_element_type=jnp.float32
        )
        outs.append((part / total).astype(jnp.bfloat16))
        logs.append(peak + jnp.log(total))
    attn_ref[:, at] = jnp.concatenate(outs, axis=1)
    lse_ref[i] = jnp.concatenate(logs, axis=1)


def attend_back_pair(
    width, q_ref, keys_of, do_ref, lse_of, delta_of, dq_ref, put_keys, put_values, i
):
    at = pl.ds(pl.multiple_of(i * PAIR, PAIR), PAIR)
    val = pl.ds(pl.multiple_of(width + i * PAIR, PAIR), PAIR)
    q2 = q_ref[:, at]
    do2 = do_ref[:, at]
    k2 = keys_of(at)
    v2 = keys_of(val)
    dqs, dks, dvs = [], [], []
    for j in range(2):
        own = slice(j * HEAD, (j + 1) * HEAD)
        q_h, do_h, k_h, v_h = q2[:, own], do2[:, own], k2[:, own], v2[:, own]
        scores = contract_cols(k_h, q_h) * SCALE
        probs = jnp.exp(scores - lse_of(j))
        dprobs = contract_cols(v_h, do_h)
        dscores = (probs * (dprobs - delta_of(j))).astype(jnp.bfloat16)
        dqs.append(SCALE * contract_rows(dscores, k_h))
        dks.append(SCALE * jnp.dot(dscores, q_h, preferred_element_type=jnp.float32))
        dvs.append(jnp.dot(probs.astype(jnp.bfloat16), do_h, preferred_element_type=jnp.float32))
    dq_ref[:, at] = jnp.concatenate(dqs, axis=1)
    put_keys(at, jnp.concatenate(dks, axis=1))
    put_values(at, val, jnp.concatenate(dvs, axis=1))


def attend_kernel(width, q_ref, kv_ref, attn_ref, lse_ref):
    def pair(i, carry):
        attend_pair(width, q_ref, lambda at: kv_ref[:, at], attn_ref, lse_ref, i)
        return carry

    lax.fori_loop(0, width // PAIR, pair, 0)


def attend(query, kv):
    rows, width = query.shape
    vmem = pl.BlockSpec(memory_space=pltpu.VMEM)
    return pl.pallas_call(
        functools.partial(attend_kernel, width),
        out_shape=attend_shapes(rows, width),
        in_specs=[vmem] * 2,
        out_specs=(vmem, vmem),
        compiler_params=pltpu.CompilerParams(vmem_limit_bytes=60 << 20),
    )(query, kv)


def attend_shapes(rows, width):
    return (
        jax.ShapeDtypeStruct((rows, width), jnp.bfloat16),
        jax.ShapeDtypeStruct((width // PAIR, rows, 2), jnp.float32),
    )


def attend_back_kernel(width, q_ref, kv_ref, do_ref, lse_ref, delta_ref, dq_ref, dkv_ref):
    def put(at, value):
        dkv_ref[:, at] = value.astype(jnp.bfloat16)

    def pair(i, carry):
        attend_back_pair(
            width,
            q_ref,
            lambda at: kv_ref[:, at],
            do_ref,
            lambda k: lse_ref[i, k : k + 1],
            lambda k: delta_ref[i, k : k + 1],
            dq_ref,
            put,
            lambda at, val, value: put(val, value),
            i,
        )
        return carry

    lax.fori_loop(0, width // PAIR, pair, 0)


def attend_back(query, kv, d_attn, lse, delta):
    rows, width = query.shape
    vmem = pl.BlockSpec(memory_space=pltpu.VMEM)
    return pl.pallas_call(
        functools.partial(attend_back_kernel, width),
        out_shape=(
            jax.ShapeDtypeStruct((rows, width), jnp.float32),
            jax.ShapeDtypeStruct(kv.shape, jnp.bfloat16),
        ),
        in_specs=[vmem] * 5,
        out_specs=(vmem, vmem),
        compiler_params=pltpu.CompilerParams(vmem_limit_bytes=60 << 20),
    )(query, kv, d_attn, lse, delta)


def in_steps(pairs, steps, pair):
    bounds = [pairs * k // steps for k in range(steps + 1)]

    def step(low, high):
        def body(i, carry):
            pair(i)
            return carry

        lax.fori_loop(low, high, body, 0)

    return [functools.partial(step, lo, hi) for lo, hi in zip(bounds, bounds[1:])]


MESH = pl.DeviceIdType.MESH
CORES = 2


def tree_events(order, depth):
    spans = {"x": [0, 1], "y": [0, 1], "z": [0] + [s * k for k in range(1, depth) for s in (1, -1)]}
    sides = {"x": [("x", 1)], "y": [("y", 1)], "z": [("z", 1), ("z", -1)]}
    found = []
    for offsets in itertools.product(*(spans[d] for d in order)):
        moved = [i for i, o in enumerate(offsets) if o]
        last = moved[-1] if moved else -1
        parent, children = None, []
        if moved:
            toward = 1 if offsets[last] > 0 else -1
            parent = (order[last], toward)
            if order[last] == "z":
                children.append(("z", -toward))
        for d in order[last + 1 :]:
            children += sides[d]
        found.append((sum(abs(o) for o in offsets), dict(zip(order, offsets)), parent, children))
    return found


def here(depth):
    dp, blk = lax.axis_index("dp"), lax.axis_index("blk")
    return {"y": dp // CORES, "c": lax.rem(dp, CORES), "z": blk // 2, "x": lax.rem(blk, 2)}


def device_of(pos):
    return (pos["y"] * CORES + pos["c"], pos["z"] * 2 + pos["x"])


def beside(pos, side):
    d, step = side
    moved = dict(pos)
    moved[d] = pos[d] + step if d == "z" else 1 - pos[d]
    return moved


def exists(pos, side, depth):
    if side[0] != "z":
        return None
    return pos["z"] + 1 < depth if side[1] > 0 else pos["z"] >= 1


def source_of(pos, offsets):
    moved = dict(pos)
    for d, o in offsets.items():
        if o:
            moved[d] = pos[d] + o if d == "z" else 1 - pos[d]
    return moved


def in_line(pos, offsets, depth):
    o = offsets.get("z", 0)
    if o == 0:
        return None
    return pos["z"] + o < depth if o > 0 else pos["z"] >= -o


def when(cond, body):
    if cond is None:
        body()
    else:
        pl.when(cond)(body)


def greet(pos, sides, depth):
    barrier = pltpu.get_barrier_semaphore()
    for side in sides:
        when(
            exists(pos, side, depth),
            lambda side=side: pl.semaphore_signal(
                barrier, inc=1, device_id=device_of(beside(pos, side)), device_id_type=MESH
            ),
        )
    peers = sum(1 for d, _ in sides if d != "z")
    if any(d == "z" for d, _ in sides):
        up = jnp.where(pos["z"] + 1 < depth, 1, 0)
        peers = peers + up + jnp.where(pos["z"] >= 1, 1, 0)
    pl.semaphore_wait(barrier, peers)


def schedule(flows, depth, back=False):
    events = []
    for f, flow in enumerate(flows):
        tree = tree_events(flow["order"], depth)
        most = max(e[0] for e in tree)
        for hops, offsets, parent, children in tree:
            key = flow["when"][most - hops if back else hops]
            events.append((key, f, offsets, parent, children))
    events.sort(key=lambda e: (e[0], e[1]))
    return events


def group_of(offsets):
    return tuple(sorted((d, o) for d, o in offsets.items() if d != "z"))


def flat_sides(flows):
    axes = sorted({d for flow in flows for d in flow["order"]})
    sides = [s for d in axes for s in ([("z", 1), ("z", -1)] if d == "z" else [(d, 1)])]
    return sides + ([("c", 1)] if any(flow["cores"] for flow in flows) else [])


def block(ref, flow, src):
    lead = (src["y"], src["c"], src["z"], src["x"]) if flow["cores"] else (src["z"], src["x"])
    low, wide = flow["columns"]
    return ref.at[lead + (slice(None), pl.ds(low, wide))]


def column(ref, flow, src):
    lead = (src["y"], src["c"], slice(None), src["x"]) if flow["cores"] else (slice(None), src["x"])
    low, wide = flow["columns"]
    return ref.at[lead + (slice(None), pl.ds(low, wide))]


def gather_kernel(flows, depth, n_in, n_out, work, *refs):
    ins, outs = refs[:n_in], refs[n_in : n_in + n_out]
    recv, sent, core_recv, core_sent, local, extra = refs[n_in + n_out :]
    pos = here(depth)
    greet(pos, flat_sides(flows), depth)
    copies, waits, arrivals = {}, [], {}
    for f, flow in enumerate(flows):
        if not flow["made"]:
            low, wide = flow["in_columns"]
            own = ins[flow["in"]].at[:, pl.ds(low, wide)]
            copies[f] = pltpu.make_async_copy(own, block(outs[flow["out"]], flow, pos), local.at[f])
            copies[f].start()
    events = schedule(flows, depth)
    items = [(e[0], 0, e) for e in events]
    items += [(key, 1, step) for key, step in (work(pos, ins, outs, extra) if work else [])]
    items.sort(key=lambda item: item[0])
    last = {}
    for i, (_, kind, e) in enumerate(items):
        if kind == 0:
            last[(e[1], group_of(e[2]))] = i
    sites = 0
    for i, (_, kind, item) in enumerate(items):
        if kind == 1:
            needed, step = item
            for f in needed:
                if f in copies:
                    copies.pop(f).wait()
                for arrival in arrivals.pop(f, []):
                    arrival.wait()
            step()
            continue
        _, f, offsets, parent, children = item
        flow = flows[f]
        src = source_of(pos, offsets)
        out = outs[flow["out"]]
        low, wide = flow["in_columns"]
        target = block(out, flow, src)
        origin = target
        if parent is None and not flow["made"]:
            origin = ins[flow["in"]].at[:, pl.ds(low, wide)]
        mark = recv.at[f, src["y"] if "y" in flow["order"] else 0, src["z"], src["x"]]
        sends = []
        for side in children:
            sends.append(
                (
                    side,
                    functools.partial(
                        pltpu.make_async_remote_copy,
                        origin,
                        target,
                        sent.at[sites],
                        mark,
                        device_id=device_of(beside(pos, side)),
                        device_id_type=MESH,
                    ),
                )
            )
            sites += 1

        def arrive():
            if parent is not None:
                pltpu.make_async_copy(target, target, mark).wait()
            for side, send in sends:
                when(exists(pos, side, depth), lambda: send().start())

        def finish(sends=sends):
            for side, send in sends:
                when(exists(pos, side, depth), lambda: send().wait_send())

        cond = in_line(pos, offsets, depth)
        when(cond, arrive)
        if sends:
            waits.append((cond, finish))
        if flow["cores"] and last[(f, group_of(offsets))] == i:
            if f in copies and not any(o for d, o in offsets.items() if d != "z"):
                copies.pop(f).wait()
            other = beside(src, ("c", 1))
            whole = column(out, flow, src)
            core = pltpu.make_async_remote_copy(
                whole,
                whole,
                core_sent.at[f, src["y"], src["x"]],
                core_recv.at[f, src["y"], src["x"]],
                device_id=device_of(beside(pos, ("c", 1))),
                device_id_type=MESH,
            )
            core.start()
            landed = column(out, flow, other)
            arrivals.setdefault(f, []).append(
                pltpu.make_async_copy(landed, landed, core_recv.at[f, src["y"], src["x"]])
            )
            waits.append((None, core.wait_send))
    for copy in copies.values():
        copy.wait()
    for some in arrivals.values():
        for arrival in some:
            arrival.wait()
    for cond, finish in waits:
        when(cond, finish)


def count_sites(flows, depth):
    return sum(len(e[4]) for e in schedule(flows, depth))


def gather(flows, depth, inputs, out_shapes, spare, collective_id, work, in_vmem, out_vmem):
    hbm = pl.BlockSpec(memory_space=pl.ANY)
    vmem = pl.BlockSpec(memory_space=pltpu.VMEM)
    n = len(flows)
    kernel = functools.partial(
        gather_kernel, flows, depth, len(inputs), len(out_shapes) + len(spare), work
    )
    return pl.pallas_call(
        kernel,
        out_shape=tuple(out_shapes),
        in_specs=[vmem if i in in_vmem else hbm for i in range(len(inputs))],
        out_specs=tuple(vmem if i in out_vmem else hbm for i in range(len(out_shapes))),
        scratch_shapes=[pltpu.VMEM(v.shape, v.dtype) for v in spare]
        + [
            pltpu.SemaphoreType.DMA((n, 2, depth, 2)),
            pltpu.SemaphoreType.DMA((count_sites(flows, depth),)),
            pltpu.SemaphoreType.DMA((n, 2, 2)),
            pltpu.SemaphoreType.DMA((n, 2, 2)),
            pltpu.SemaphoreType.DMA((n,)),
            pltpu.SemaphoreType.DMA((3,)),
        ],
        compiler_params=pltpu.CompilerParams(
            collective_id=collective_id, has_side_effects=True, vmem_limit_bytes=62 << 20
        ),
    )(*inputs)


def slots_of(flow, d, depth):
    sizes = {"x": 2, "y": 2, "z": depth}
    before = flow["order"][: flow["order"].index(d)]
    return ([2] if d == "z" else []) + [sizes[k] for k in before] + ([depth] if d == "z" else [])


def slot(flow, d, src, side):
    before = flow["order"][: flow["order"].index(d)]
    return (
        ([0 if side > 0 else 1] if d == "z" else [])
        + [src[k] for k in before]
        + ([src["z"]] if d == "z" else [])
    )


def chunk_of(rows, columns):
    wide = 128
    while columns % (2 * wide) == 0 and rows * 2 * wide <= 24 * 1024:
        wide *= 2
    return wide


def scatter_kernel(flows, depth, n_in, n_out, n_made, work, *refs):
    ins, outs = refs[:n_in], refs[n_in : n_in + n_out]
    at = n_in + n_out
    made = refs[at : at + n_made]
    at += n_made
    mine, theirs, slots, marks = [], [], [], []
    for flow in flows:
        if flow["made"]:
            mine.append(made[flow["in"]])
        else:
            mine.append(refs[at])
            at += 1
        theirs.append(refs[at] if flow["cores"] else None)
        at += 1 if flow["cores"] else 0
        slots.append({})
        marks.append({})
        for d in flow["order"]:
            slots[-1][d], marks[-1][d] = refs[at], refs[at + 1]
            at += 2
    sent, core_recv, core_sent, local, extra = refs[at:]
    pos = here(depth)
    greet(pos, flat_sides(flows), depth)
    events = schedule(flows, depth, True)

    def lead(flow, src):
        if not flow["cores"]:
            return (src["z"], src["x"])
        return (src["y"],) + ((src["c"],) if flow["made"] else ()) + (src["z"], src["x"])

    def col(src):
        return (src["y"], slice(None), src["x"])

    def parts(f, own, cols):
        low = flows[f]["columns"][0] if flows[f]["made"] else 0
        return own + (slice(None), pl.ds(pl.multiple_of(low + cols.start, 128), cols.size))

    ready, waits, sites = {}, [], 0

    def begin(chosen):
        for _, f, offsets, parent, children in events:
            key = (f, group_of(offsets))
            if key in ready or f not in chosen:
                continue
            flow = flows[f]
            src = source_of(pos, {d: o for d, o in offsets.items() if d != "z"})
            y = src["y"] if flow["cores"] else 0
            whole = made[flow["in"]] if flow["made"] else ins[flow["in"]]
            loads = []
            if flow["cores"]:
                core = pltpu.make_async_remote_copy(
                    column(whole, flow, beside(src, ("c", 1))),
                    theirs[f].at[col(src)],
                    core_sent.at[f, y, src["x"]],
                    core_recv.at[f, y, src["x"]],
                    device_id=device_of(beside(pos, ("c", 1))),
                    device_id_type=MESH,
                )
                core.start()
                loads.append(core.wait_recv)
                waits.append((None, core.wait_send))
            if not flow["made"]:
                copy = pltpu.make_async_copy(
                    column(whole, flow, src), mine[f].at[col(src)], local.at[f, y, src["x"]]
                )
                copy.start()
                loads.append(copy.wait)
            ready[key] = loads

    begin([f for f, flow in enumerate(flows) if not flow["made"]])
    items = [(e[0], 0, e) for e in events]
    items += [(key, 1, step) for key, step in (work(pos, ins, outs, made, extra) if work else [])]
    items.sort(key=lambda item: item[0])
    for _, kind, item in items:
        if kind == 1:
            after, step = item
            step()
            begin(after)
            continue
        _, f, offsets, parent, children = item
        flow = flows[f]
        for load in ready.get((f, group_of(offsets)), []):
            load()
        ready[(f, group_of(offsets))] = []
        src = source_of(pos, offsets)
        own = lead(flow, src)
        send = None
        if parent is not None:
            d, toward = parent
            place = tuple(slot(flow, d, src, -toward))
            send = pltpu.make_async_remote_copy(
                mine[f].at[parts(f, own, pl.ds(0, flow["columns"][1]))],
                slots[f][d].at[place] if place else slots[f][d],
                sent.at[sites],
                marks[f][d].at[place if place else (0,)],
                device_id=device_of(beside(pos, parent)),
                device_id_type=MESH,
            )
            sites += 1

        def step():
            rows, columns = mine[f].shape[-2], flow["columns"][1]
            wide = chunk_of(rows, columns)
            terms = []
            for side in children:
                d = side[0]
                place = tuple(slot(flow, d, src, side[1]))
                buf = slots[f][d].at[place] if place else slots[f][d]
                there = exists(pos, side, depth)
                when(
                    there,
                    lambda: pltpu.make_async_copy(
                        buf, buf, marks[f][d].at[place if place else (0,)]
                    ).wait(),
                )
                terms.append((place, d, there))

            def total(cols):
                value = mine[f][parts(f, own, cols)].astype(jnp.float32)
                if flow["cores"]:
                    core = (src["y"], src["z"], src["x"], slice(None), cols)
                    value += theirs[f][core].astype(jnp.float32)
                return value

            def put(cols, value):
                if send is None:
                    low = flow["out_low"]
                    outs[flow["out"]][:, pl.ds(pl.multiple_of(low + cols.start, 128), wide)] = value
                else:
                    mine[f][parts(f, own, cols)] = value.astype(mine[f].dtype)

            def with_terms(chosen):
                def go():
                    def body(k, carry):
                        cols = pl.ds(pl.multiple_of(k * wide, wide), wide)
                        value = total(cols)
                        for place, d in chosen:
                            value += slots[f][d][place + (slice(None), cols)].astype(jnp.float32)
                        put(cols, value)
                        return carry

                    lax.fori_loop(0, columns // wide, body, 0, unroll=True)

                return go

            always = [(p, d) for p, d, there in terms if there is None]
            maybe = [(p, d, there) for p, d, there in terms if there is not None]
            if flow["cores"] or always or maybe:
                for picks in itertools.product((True, False), repeat=len(maybe)):
                    cond = None
                    for (p, d, there), pick in zip(maybe, picks):
                        test = there if pick else jnp.logical_not(there)
                        cond = test if cond is None else jnp.logical_and(cond, test)
                    chosen = always + [(p, d) for (p, d, _), pick in zip(maybe, picks) if pick]
                    if not chosen and not flow["cores"] and send is not None:
                        continue
                    when(cond, with_terms(chosen))
            if send is not None:
                send.start()

        cond = in_line(pos, offsets, depth)
        when(cond, step)
        if send is not None:
            waits.append((cond, send.wait_send))
    for cond, finish in waits:
        when(cond, finish)


def scatter(flows, depth, inputs, out_shapes, collective_id, work, made, in_vmem, spare):
    hbm = pl.BlockSpec(memory_space=pl.ANY)
    vmem = pl.BlockSpec(memory_space=pltpu.VMEM)
    n = len(flows)
    scratch = [pltpu.VMEM(m.shape, m.dtype) for m in made + spare]
    for flow in flows:
        source = made[flow["in"]] if flow["made"] else inputs[flow["in"]]
        rows, kind = source.shape[-2], source.dtype
        unit = (rows, flow["columns"][1])
        whole = ((2, depth, 2) if flow["cores"] else (depth, 2)) + unit
        if not flow["made"]:
            scratch.append(pltpu.VMEM(whole, kind))
        if flow["cores"]:
            scratch.append(pltpu.VMEM(whole, kind))
        for d in flow["order"]:
            places = tuple(slots_of(flow, d, depth))
            scratch.append(pltpu.VMEM(places + unit, kind))
            scratch.append(pltpu.SemaphoreType.DMA(places if places else (1,)))
    scratch += [
        pltpu.SemaphoreType.DMA((len(schedule(flows, depth)),)),
        pltpu.SemaphoreType.DMA((n, 2, 2)),
        pltpu.SemaphoreType.DMA((n, 2, 2)),
        pltpu.SemaphoreType.DMA((n, 2, 2)),
        pltpu.SemaphoreType.DMA((3,)),
    ]
    kernel = functools.partial(
        scatter_kernel, flows, depth, len(inputs), len(out_shapes), len(made + spare), work
    )
    return pl.pallas_call(
        kernel,
        out_shape=tuple(out_shapes),
        in_specs=[vmem if i in in_vmem else hbm for i in range(len(inputs))],
        out_specs=tuple([vmem] * len(out_shapes)),
        scratch_shapes=scratch,
        compiler_params=pltpu.CompilerParams(
            collective_id=collective_id, has_side_effects=True, vmem_limit_bytes=62 << 20
        ),
    )(*inputs)


ZXY, ZYX, XZY, YZX = ("z", "x", "y"), ("z", "y", "x"), ("x", "z", "y"), ("y", "z", "x")


def flow_of(order, source, which, low, wide, place, cores=True, made=False):
    return dict(
        order=order,
        cores=cores,
        columns=(low, wide),
        in_columns=(low, wide),
        out_low=low,
        made=made,
        out=which,
        when=place,
        **{"in": source},
    )


def layout_of(large, own, span):
    dp, blk = lax.axis_size("dp"), lax.axis_size("blk")
    fits = all(v.shape[0] % 8 == 0 and v.shape[1] % 128 == 0 for v in large)
    fits = fits and own <= 128 and span <= 128
    width, wide = large[1].shape[1], large[2].shape[1]
    fits = fits and wide % width == 0 and dp * blk % (wide // width) == 0
    if fits and dp == 2 * CORES and blk % 2 == 0 and 2 <= blk // 2 <= 4:
        return blk // 2
    return None


def flat_rows(whole):
    return whole.reshape(-1, whole.shape[-1])


def flat_rows(whole):
    return whole.reshape(-1, whole.shape[-1])


def forward_kernel(tokens, w_qkv, flat, large, depth):
    rows, width = tokens.shape
    n, high = 4 * CORES * depth, flat.shape[0]
    own, wide = width // n, large[1].shape[1]
    count, span = wide // width, wide // n
    bf16, f32 = jnp.bfloat16, jnp.float32
    column_of, lane_of = np.arange(width), np.arange(128)[:, None]
    lanes = np.stack([lane_of == column_of % k for k in (own, span)])
    places = [np.arange(k)[:, None, None] == column_of // (width // k) for k in (n, n // count)]

    def work(pos, ins, outs, extra):
        lanes_ref, place_ref, up_place_ref = ins[-3:]
        small, q_ref, narrow, up_bias, attn_ref, lse_ref, blocks, every, dense, kv_ref = (
            outs[3:4] + outs[7:]
        )
        saves = [
            pltpu.make_async_copy(held, kept, extra.at[k])
            for k, (held, kept) in enumerate(zip((every, dense, kv_ref), outs[4:7]))
        ]

        def unpack():
            for k in range(3):
                at = pl.ds(k * width, width)
                part = blocks[:, :, :, :, :, at].astype(f32).reshape(width, width)
                dense[:, at] = part.astype(bf16)
            saves[1].start()

        def project():
            rows_of = small[...].reshape(n * high, 128)
            spread = jnp.dot(rows_of, lanes_ref[0], preferred_element_type=f32)
            narrow[...] = jnp.sum(spread.reshape(n, high, width) * place_ref[...], axis=0)
            spread = jnp.dot(rows_of, lanes_ref[1], preferred_element_type=f32)
            spread = spread.reshape(count, n // count, high, width)
            for k in range(count):
                up_bias[k] = jnp.sum(spread[k] * up_place_ref[...], axis=0)
            query_bias, value_bias = narrow[0:1, :], narrow[1:2, :]
            mine = every[pos["z"], pos["x"]]
            query = jnp.dot(mine, dense[:, :width], preferred_element_type=f32)
            q_ref[...] = (query + query_bias).astype(bf16)
            later = jnp.concatenate([jnp.zeros_like(value_bias), value_bias], axis=1)

            def line(z, carry):
                some = every[z].reshape(2 * rows, width)
                part = jnp.dot(some, dense[:, width:], preferred_element_type=f32) + later
                kv_ref[z] = part.astype(bf16).reshape(2, rows, 2 * width)
                return carry

            lax.fori_loop(0, depth, line, 0)
            saves[0].start()
            saves[2].start()

        def saved():
            for save in saves:
                save.wait()

        def keys_of(at):
            return kv_ref[:, :, :, at].reshape(-1, PAIR)

        pair = functools.partial(attend_pair, width, q_ref, keys_of, attn_ref, lse_ref)
        steps = in_steps(width // PAIR, len(ATTEND), pair)
        found = [(UNPACK, ((0,), unpack)), (PROJECT, ((1, 2), project)), (99, ((), saved))]
        return found + [(key, ((), step)) for key, step in zip(ATTEND, steps)]

    shapes = whole_shapes(list(large) + [flat], depth) + [
        jax.ShapeDtypeStruct((depth, 2, rows, width), bf16),
        jax.ShapeDtypeStruct((width, 3 * width), bf16),
        jax.ShapeDtypeStruct((depth, 2, rows, 2 * width), bf16),
        jax.ShapeDtypeStruct((rows, width), bf16),
        jax.ShapeDtypeStruct((high, width), f32),
        jax.ShapeDtypeStruct((count, high, width), f32),
    ]
    shapes += list(attend_shapes(rows, width))
    inputs = [w_qkv, flat, tokens] + list(large)
    flows = [
        flow_of(GATHER_ORDERS[0], 0, len(shapes), 0, 3 * width, FIRST),
        flow_of(GATHER_ORDERS[1], 1, 3, 0, 128, FIRST),
        flow_of(("z", "x"), 2, len(shapes) + 1, 0, width, FIRST, cores=False),
    ]
    for i, (order, v) in enumerate(zip(GATHER_ORDERS[2:], large)):
        flows.append(flow_of(order, 3 + i, i, 0, v.shape[1], LATER))
    inputs += [jnp.asarray(lanes, bf16)]
    inputs += [jnp.asarray(np.broadcast_to(p, (len(p), high, width)), f32) for p in places]
    return gather(
        flows,
        depth,
        inputs,
        shapes,
        whole_shapes([w_qkv], depth) + shapes[4:7],
        1,
        work,
        in_vmem=range(len(inputs) - 3, len(inputs)),
        out_vmem=(3,) + tuple(range(7, len(shapes))),
    )


GATHER_ORDERS = (ZXY, ZYX, ZXY, XZY, YZX)
FIRST, LATER = (0, 1, 2, 3, 4, 5), (1.5, 2.5, 3.5, 4.5, 5.05, 6.0)
UNPACK, PROJECT, ATTEND = 5.1, 5.2, (6.2, 6.7, 7.7)
SCATTER_ORDERS = (ZXY, XZY, YZX, ZXY, ZYX)
BACK, EARLY = (0, 1.5, 2.5), (1.1, 2.1, 3.3, 4.3, 5.3, 6.3)
WEIGHTS, TOKENS, LAST = 2.6, 2.7, (3.0, 3.4, 4.4, 5.4, 6.4, 7.4)


def whole_shapes(large, depth):
    return [jax.ShapeDtypeStruct((2, CORES, depth, 2) + v.shape, v.dtype) for v in large]


def backward_kernel(query, kv, d_attn, lse, delta, every, dense, sums, d_up_bias, grads, large, depth):
    bf16, f32 = jnp.bfloat16, jnp.float32
    rows, width = query.shape
    n = 4 * CORES * depth
    own = width // n
    wide = d_up_bias.shape[1]
    count, span = wide // width, wide // n
    column_of = np.arange(width)
    line = np.arange(8 * n)[:, None] // 8
    places = [line == column_of // own, line % (n // count) == column_of // span]
    lanes = [column_of[:, None] % k == np.arange(128) for k in (own, span)]
    small = jax.ShapeDtypeStruct((2, CORES, depth, 2, 16, 128), f32)

    def work(pos, ins, outs, made, extra):
        q_ref, do_ref, lse_ref, delta_ref = ins[-10:-6]
        sums_ref, up_ref, place_ref, up_place_ref, lanes_ref, up_lanes_ref = ins[-6:]
        token_part, d_whole, small_made, dq_ref, dkv_ref, sum_ref, kv_ref, every_ref, w_ref = made
        loads = [
            pltpu.make_async_copy(kept, held, extra.at[k])
            for k, (kept, held) in enumerate(zip(ins[-13:-10], (kv_ref, every_ref, w_ref)))
        ]
        for load in loads:
            load.start()

        def keys_of(at):
            return kv_ref[:, :, :, at].reshape(-1, PAIR)

        def put_keys(at, value):
            dkv_ref[:, at] = value.astype(bf16)

        def put_values(at, val, value):
            sum_ref[:, at] = jnp.sum(value, axis=0, keepdims=True)
            dkv_ref[:, val] = value.astype(bf16)

        def pair(i):
            attend_back_pair(
                width,
                q_ref,
                keys_of,
                do_ref,
                lambda k: lse_ref[pl.ds(2 * i + k, 1), :],
                lambda k: delta_ref[pl.ds(2 * i + k, 1), :],
                dq_ref,
                put_keys,
                put_values,
                i,
            )

        def weights():
            loads[1].wait()
            whole = every_ref[...].reshape(-1, width)
            for k in range(3):
                if k == 0:
                    part = contract_rows(every_ref[pos["z"], pos["x"]], dq_ref[...].astype(bf16))
                else:
                    part = contract_rows(whole, dkv_ref[:, (k - 1) * width : k * width])
                part = part.reshape(2, CORES, depth, 2, own, width).astype(bf16)
                d_whole[:, :, :, :, :, k * width : (k + 1) * width] = part
            query_sum = jnp.sum(dq_ref[...], axis=0, keepdims=True)
            eight = jnp.concatenate([query_sum, sum_ref[...], sums_ref[2:8, :]], axis=0)
            whole = jnp.broadcast_to(eight[None], (n, 8, width)).reshape(8 * n, width)
            narrow = jnp.dot(
                whole * place_ref[...],
                lanes_ref[...],
                preferred_element_type=f32,
                precision=lax.Precision.HIGHEST,
            )
            spread = [
                jnp.broadcast_to(up_ref[:, k * width : (k + 1) * width], (8 * n // count, width))
                for k in range(count)
            ]
            up = jnp.dot(
                jnp.concatenate(spread, axis=0) * up_place_ref[...],
                up_lanes_ref[...],
                preferred_element_type=f32,
                precision=lax.Precision.HIGHEST,
            )
            lead = (2, CORES, depth, 2, 8, 128)
            small_made[:, :, :, :, 0:8, :] = narrow.reshape(lead)
            small_made[:, :, :, :, 8:16, :] = up.reshape(lead)

        def tokens_gradient():
            loads[2].wait()

            def line(z, carry):
                at = pl.ds(pl.multiple_of(z * 2 * rows, 2 * rows), 2 * rows)
                part = contract_cols(dkv_ref[at, :], w_ref[:, width:])
                token_part[z] = part.astype(bf16).reshape(2, rows, width)
                return carry

            lax.fori_loop(0, depth, line, 0)
            outs[-1][...] = contract_cols(dq_ref[...].astype(bf16), w_ref[:, :width])

        steps = in_steps(width // PAIR, len(BACK), pair)
        found = [(-1, ((), loads[0].wait))]
        found += [(key, ((), step)) for key, step in zip(BACK, steps)]
        return found + [(WEIGHTS, ((3, 4), weights)), (TOKENS, ((5,), tokens_gradient))]

    blocks = [g.reshape((2, CORES, depth, 2) + v.shape) for g, v in zip(grads, large)]
    made = [
        jax.ShapeDtypeStruct(every.shape, bf16),
        jax.ShapeDtypeStruct((2, CORES, depth, 2, own, 3 * width), bf16),
        jax.ShapeDtypeStruct(small.shape, f32),
    ]
    spare = [
        jax.ShapeDtypeStruct((rows, width), f32),
        jax.ShapeDtypeStruct((2 * depth * rows, 2 * width), bf16),
        jax.ShapeDtypeStruct((1, width), f32),
        kv,
        every,
        dense,
    ]
    flows = []
    for i, (order, v) in enumerate(zip(SCATTER_ORDERS, large)):
        flows.append(flow_of(order, i, i, 0, v.shape[1], EARLY))
    flows.append(flow_of(SCATTER_ORDERS[3], 1, 3, 0, 3 * width, LAST, made=True))
    flows.append(flow_of(SCATTER_ORDERS[4], 2, 4, 0, 128, LAST, made=True))
    flows.append(flow_of(("z", "x"), 0, 5, 0, width, LAST, cores=False, made=True))
    shapes = [jax.ShapeDtypeStruct(v.shape, f32) for v in large]
    shapes += [
        jax.ShapeDtypeStruct((own, 3 * width), f32),
        jax.ShapeDtypeStruct(small.shape[-2:], f32),
        jax.ShapeDtypeStruct((rows, width), f32),
        jax.ShapeDtypeStruct((rows, width), f32),
    ]
    inputs = blocks + [kv, every, dense, query, d_attn, lse, delta, sums, d_up_bias]
    inputs += [jnp.asarray(v, f32) for v in places + lanes]
    return scatter(
        flows, depth, inputs, shapes, 2, work, made, range(len(blocks) + 3, len(inputs)), spare
    )


def middle_kernel(chunk, *refs):
    bf16, f32 = jnp.bfloat16, jnp.float32
    tokens, attn, lse, cotangent, narrow, up_bias, head_of, wo_in, wu_in, wd_in = refs[:10]
    out, dh1_out, d_attn_out, delta_out, lse_out, sums, d_up_bias = refs[10:17]
    d_wo_out, d_wu_out, d_wd_out = refs[17:20]
    wo, wu, wd, d_wo, d_wu, d_wd, slope, act, arrived, left = refs[20:]
    count = wu.shape[0]

    def cut(c):
        return pl.ds(c * chunk, chunk)

    loads = [pltpu.make_async_copy(wo_in, wo, arrived.at[0])]
    for c in range(count):
        loads.append(pltpu.make_async_copy(wu_in.at[:, cut(c)], wu.at[c], arrived.at[1 + 2 * c]))
        loads.append(pltpu.make_async_copy(wd_in.at[cut(c), :], wd.at[c], arrived.at[2 + 2 * c]))
    for load in loads:
        load.start()

    def line(k):
        return narrow[k : k + 1, :]

    def total(value):
        return jnp.sum(value, axis=0, keepdims=True)

    logs = [lse[k] for k in range(lse.shape[0])]
    rows = tokens.shape[0]
    logs.append(jnp.zeros((rows, 128 - 2 * len(logs)), f32))
    lse_out[...] = jnp.concatenate(logs, axis=1).T[: lse_out.shape[0]]
    loads[0].wait()
    hidden = tokens[...].astype(f32) + line(2)
    hidden += jnp.dot(attn[...], wo[...], preferred_element_type=f32)
    y1, xhat1, rstd1 = layernorm_forward(hidden, line(3), line(5))
    y1_low = y1.astype(bf16)
    hidden = y1 + line(7)
    for c in range(count):
        loads[1 + 2 * c].wait()
        up = jnp.dot(y1_low, wu[c], preferred_element_type=f32) + up_bias[c, 8:9, :]
        cdf = 0.5 * (1.0 + lax.erf(up * 0.7071067811865476))
        slope[:, cut(c)] = cdf + up * jnp.exp(-0.5 * up * up) * 0.3989422804014327
        act[:, cut(c)] = (up * cdf).astype(bf16)
        loads[2 + 2 * c].wait()
        hidden += jnp.dot(act[:, cut(c)], wd[c], preferred_element_type=f32)
    y2, xhat2, rstd2 = layernorm_forward(hidden, line(4), line(6))
    out[...] = y2.astype(bf16)
    gradient = cotangent[...].astype(f32)
    dh2 = layernorm_backward(gradient, xhat2, rstd2, line(4))
    sums[0:2, :] = jnp.zeros((2, sums.shape[1]), f32)
    sums[4:5, :] = total(gradient * xhat2)
    sums[6:7, :] = total(gradient)
    sums[7:8, :] = total(dh2)
    dh2_low = dh2.astype(bf16)
    stores = []
    dy1 = dh2
    for c in range(count):
        d_wd[c] = contract_rows(act[:, cut(c)], dh2_low).astype(bf16)
        stores.append(pltpu.make_async_copy(d_wd.at[c], d_wd_out.at[cut(c), :], left.at[1 + 2 * c]))
        stores[-1].start()
        d_up_f = contract_cols(dh2_low, wd[c]) * slope[:, cut(c)]
        d_up_bias[:, cut(c)] = total(d_up_f)
        d_up = d_up_f.astype(bf16)
        d_wu[c] = contract_rows(y1_low, d_up).astype(bf16)
        stores.append(pltpu.make_async_copy(d_wu.at[c], d_wu_out.at[:, cut(c)], left.at[2 + 2 * c]))
        stores[-1].start()
        dy1 += contract_cols(d_up, wu[c])
    dh1 = layernorm_backward(dy1, xhat1, rstd1, line(3))
    sums[2:3, :] = total(dh1)
    sums[3:4, :] = total(dy1 * xhat1)
    sums[5:6, :] = total(dy1)
    dh1_out[...] = dh1
    dh1_low = dh1.astype(bf16)
    d_wo[...] = contract_rows(attn[...], dh1_low).astype(bf16)
    stores.append(pltpu.make_async_copy(d_wo, d_wo_out, left.at[0]))
    stores[-1].start()
    d_attn = contract_cols(dh1_low, wo[...]).astype(bf16)
    d_attn_out[...] = d_attn
    delta_out[...] = lax.dot_general(
        head_of[...],
        d_attn.astype(f32) * attn[...].astype(f32),
        (((1,), (1,)), ((), ())),
        preferred_element_type=f32,
        precision=lax.Precision.HIGHEST,
    )
    for store in stores:
        store.wait()


def middle(tokens, attn, lse, cotangent, narrow, up_bias, w_out, w_up, w_down):
    bf16, f32 = jnp.bfloat16, jnp.float32
    rows, width = tokens.shape
    wide = w_up.shape[1]
    chunk = width
    count = wide // chunk
    lines = -(-(width // HEAD) // 8) * 8
    head_of = np.arange(lines)[:, None] == np.arange(width) // HEAD
    vmem, hbm = pl.BlockSpec(memory_space=pltpu.VMEM), pl.BlockSpec(memory_space=pl.ANY)
    shapes = [
        ((rows, width), bf16),
        ((rows, width), f32),
        ((rows, width), bf16),
        ((lines, rows), f32),
        ((lines, rows), f32),
        ((8, width), f32),
        ((1, wide), f32),
        (w_out.shape, bf16),
        (w_up.shape, bf16),
        (w_down.shape, bf16),
    ]
    chunks = (count, width, chunk)
    return pl.pallas_call(
        functools.partial(middle_kernel, chunk),
        out_shape=tuple(jax.ShapeDtypeStruct(*v) for v in shapes),
        in_specs=[vmem] * 7 + [hbm] * 3,
        out_specs=tuple([vmem] * 7 + [hbm] * 3),
        scratch_shapes=[
            pltpu.VMEM(w_out.shape, bf16),
            pltpu.VMEM(chunks, bf16),
            pltpu.VMEM(chunks, bf16),
            pltpu.VMEM(w_out.shape, bf16),
            pltpu.VMEM(chunks, bf16),
            pltpu.VMEM(chunks, bf16),
            pltpu.VMEM((rows, wide), f32),
            pltpu.VMEM((rows, wide), bf16),
            pltpu.SemaphoreType.DMA((1 + 2 * count,)),
            pltpu.SemaphoreType.DMA((1 + 2 * count,)),
        ],
        compiler_params=pltpu.CompilerParams(vmem_limit_bytes=60 << 20),
        name="ffn",
    )(
        tokens, attn, lse, cotangent, narrow, up_bias, jnp.asarray(head_of, f32), w_out, w_up, w_down
    )


def finish_kernel(*refs):
    parts, row, dh1, query_part, token_sum = refs[:4], refs[4], refs[5], refs[6], refs[7]
    d_tokens, grads, pairs, singles, up = refs[8], refs[9:13], refs[13:16], refs[16:18], refs[18]
    d_tokens[...] = dh1[...] + query_part[...] + token_sum[...]
    for part, grad in zip(parts, grads):
        grad[...] = part[...]
    own = pairs[0].shape[1]
    for k, pair in zip((0, 3, 5), pairs):
        pair[...] = row[k : k + 2, :own]
    for k, single in zip((2, 7), singles):
        single[...] = row[k : k + 1, :own]
    up[...] = row[8:9, : up.shape[1]]


def finish(parts, row, dh1, query_part, token_sum, own, span):
    f32 = jnp.float32
    shapes = [dh1.shape] + [p.shape for p in parts] + [(2, own)] * 3 + [(1, own)] * 2 + [(1, span)]
    vmem = pl.BlockSpec(memory_space=pltpu.VMEM)
    return pl.pallas_call(
        finish_kernel,
        out_shape=tuple(jax.ShapeDtypeStruct(shape, f32) for shape in shapes),
        in_specs=[vmem] * 8,
        out_specs=tuple([vmem] * len(shapes)),
        name="finish",
    )(*parts, row, dh1, query_part, token_sum)


SPARE = 16


def split_owner(full, count):
    p = full.shape[0]
    return full.reshape(p, count, -1).transpose(1, 0, 2).reshape(count, -1)


def join_owner(parts, p):
    count = parts.shape[0]
    return parts.reshape(count, p, -1).transpose(1, 0, 2).reshape(p, -1)


def plain_on_device(
    tokens,
    w_qkv,
    qv_bias,
    w_out,
    out_bias,
    norm_gain,
    norm_bias,
    w_up,
    up_bias,
    w_down,
    down_bias,
    cotangent,
):
    f32 = jnp.float32
    bf16 = jnp.bfloat16
    rows, width = tokens.shape
    heads = width // HEAD
    n = lax.axis_size("dp") * lax.axis_size("blk")
    small = [qv_bias, out_bias, norm_gain, norm_bias, up_bias, down_bias]
    sizes = [v.size for v in small]
    flat = jnp.concatenate([v.reshape(-1) for v in small])
    flat = jnp.pad(flat, (0, SPARE * width - flat.size)).reshape(SPARE, width)
    large = [w_qkv, w_out, w_up, w_down]
    shard = jnp.concatenate(
        [v[:, i : i + width] for v in large for i in range(0, v.shape[1], width)] + [flat]
    )
    packed = lax.all_gather(shard, ("dp", "blk"), axis=0)
    wholes, at = [], 0
    for v in large:
        high, columns = v.shape
        blocks = []
        for _ in range(columns // width):
            blocks.append(packed[:, at : at + high].reshape(n * high, width))
            at += high
        wholes.append(jnp.concatenate(blocks, axis=1))
    wq_full, wo_full, wu_full, wd_full = wholes
    row_full = packed[:, at:].reshape(n, -1)
    parts, at = [], 0
    for size, v in zip(sizes, small):
        parts.append(join_owner(row_full[:, at : at + size], 2 if v.ndim == 2 else 1))
        at += size
    qvb_full, bo_full, gain_full, shift_full, bu_full, bd_full = parts
    bo_full, bu_full, bd_full = bo_full[0], bu_full[0], bd_full[0]
    norm_gain_pair = gain_full.astype(f32)
    norm_offset_pair = shift_full.astype(f32)
    qvb = qvb_full.astype(f32)
    bias_row = jnp.concatenate([qvb[0], jnp.zeros((width,), f32), qvb[1]])
    qkv = (jnp.dot(tokens, wq_full, preferred_element_type=f32) + bias_row).astype(bf16)
    query = qkv[:, :width]
    kv = lax.all_gather(qkv[:, width:], "blk", axis=0, tiled=True)
    attn, lse = attend(query, kv)
    first_hidden = (
        tokens.astype(f32)
        + jnp.dot(attn, wo_full, preferred_element_type=f32)
        + bo_full.astype(f32)
    )
    first_norm_output, first_normalized, first_inverse_deviation = layernorm_forward(
        first_hidden, norm_gain_pair[0], norm_offset_pair[0]
    )
    y1_low = first_norm_output.astype(bf16)
    up = jnp.dot(y1_low, wu_full, preferred_element_type=f32) + bu_full.astype(f32)
    act = jax.nn.gelu(up, approximate=False).astype(bf16)
    second_hidden = (
        first_norm_output + jnp.dot(act, wd_full, preferred_element_type=f32) + bd_full.astype(f32)
    )
    output_float, second_normalized, second_inverse_deviation = layernorm_forward(
        second_hidden, norm_gain_pair[1], norm_offset_pair[1]
    )
    output = output_float.astype(bf16)
    wq_b, wo_b, wu_b, wd_b = wq_full, wo_full, wu_full, wd_full
    gain_pair_block = norm_gain_pair
    incoming_gradient = cotangent.astype(f32)
    second_gain_gradient = jnp.sum(incoming_gradient * second_normalized, axis=0)
    d_shift2 = jnp.sum(incoming_gradient, axis=0)
    second_hidden_gradient = layernorm_backward(
        incoming_gradient, second_normalized, second_inverse_deviation, gain_pair_block[1]
    )
    dh2_low = second_hidden_gradient.astype(bf16)
    d_w_down = contract_rows(act, dh2_low)
    d_down_bias = jnp.sum(second_hidden_gradient, axis=0)
    d_up_f = contract_cols(dh2_low, wd_b) * gelu_grad(up)
    d_up_bias = jnp.sum(d_up_f, axis=0)
    d_up = d_up_f.astype(bf16)
    d_w_up = contract_rows(y1_low, d_up)
    first_output_gradient = second_hidden_gradient + contract_cols(d_up, wu_b)
    first_gain_gradient = jnp.sum(first_output_gradient * first_normalized, axis=0)
    d_shift1 = jnp.sum(first_output_gradient, axis=0)
    first_hidden_gradient = layernorm_backward(
        first_output_gradient, first_normalized, first_inverse_deviation, gain_pair_block[0]
    )
    dh1_low = first_hidden_gradient.astype(bf16)
    d_w_out = contract_rows(attn, dh1_low)
    d_out_bias = jnp.sum(first_hidden_gradient, axis=0)
    d_gains = jnp.stack([first_gain_gradient, second_gain_gradient])
    d_shifts = jnp.stack([d_shift1, d_shift2])
    d_attn = contract_cols(dh1_low, wo_b).astype(bf16)
    delta = jnp.sum((d_attn.astype(f32) * attn.astype(f32)).reshape(rows, heads, HEAD), axis=-1).T
    d_query, d_kv_all = attend_back(
        query, kv, d_attn, lse.transpose(0, 2, 1), delta.reshape(heads // 2, 2, rows)
    )
    d_kv = lax.psum_scatter(d_kv_all, "blk", scatter_dimension=0, tiled=True).astype(f32)
    d_key = d_kv[:, :width]
    d_value = d_kv[:, width:]
    d_qv = jnp.stack([jnp.sum(d_query, axis=0), jnp.sum(d_value, axis=0)])
    d_qkv = jnp.concatenate([d_query, d_key, d_value], axis=1).astype(bf16)
    d_w_qkv = contract_rows(tokens, d_qkv)
    d_tokens = first_hidden_gradient + contract_cols(d_qkv, wq_b)
    grads = [d_qv, d_out_bias[None], d_gains, d_shifts, d_up_bias[None], d_down_bias[None]]
    row = jnp.concatenate([split_owner(v, n) for v in grads], axis=1)
    row = jnp.pad(row, ((0, 0), (0, SPARE * width - row.shape[1]))).reshape(n, SPARE, width)
    blocks = []
    for d_full, v in zip((d_w_qkv, d_w_out, d_w_up, d_w_down), large):
        d_low = d_full.astype(bf16).reshape((n,) + v.shape)
        blocks += [d_low[:, :, i : i + width] for i in range(0, v.shape[1], width)]
    packed = jnp.concatenate(blocks + [row.astype(bf16)], axis=1)
    packed = lax.psum_scatter(packed, ("dp", "blk"), scatter_dimension=0, tiled=True)[0]
    wholes, at = [], 0
    for v in large:
        high, columns = v.shape
        blocks = []
        for _ in range(columns // width):
            blocks.append(packed[at : at + high])
            at += high
        wholes.append(jnp.concatenate(blocks, axis=1).astype(f32))
    g_wqkv, g_wout, g_wup, g_wdown = wholes
    row, at, parts = packed[at:].reshape(-1).astype(f32), 0, []
    for size, v in zip(sizes, small):
        parts.append(row[at : at + size].reshape(v.shape))
        at += size
    g_qv, g_bout, g_gain, g_shift, g_bup, g_bdown = parts
    return (
        output,
        d_tokens,
        g_wqkv,
        g_qv,
        g_wout,
        g_bout,
        g_gain,
        g_shift,
        g_wup,
        g_bup,
        g_wdown,
        g_bdown,
    )


def on_device(
    tokens,
    w_qkv,
    qv_bias,
    w_out,
    out_bias,
    norm_gain,
    norm_bias,
    w_up,
    up_bias,
    w_down,
    down_bias,
    cotangent,
):
    f32 = jnp.float32
    bf16 = jnp.bfloat16
    rows, width = tokens.shape
    n = lax.axis_size("dp") * lax.axis_size("blk")
    own = out_bias.shape[0]
    span = up_bias.shape[0]
    depth = layout_of([w_qkv, w_out, w_up, w_down], own, span)
    if depth is None:
        return plain_on_device(
            tokens,
            w_qkv,
            qv_bias,
            w_out,
            out_bias,
            norm_gain,
            norm_bias,
            w_up,
            up_bias,
            w_down,
            down_bias,
            cotangent,
        )
    large = [w_out, w_up, w_down]
    flat = jnp.zeros((16, 128), bf16)
    lines = [(0, qv_bias), (2, out_bias), (3, norm_gain), (5, norm_bias), (7, down_bias), (8, up_bias)]
    for row, v in lines:
        v = v.reshape(-1, v.shape[-1])
        flat += jnp.pad(v, ((row, 16 - row - v.shape[0]), (0, 128 - v.shape[1])))
    outs = forward_kernel(tokens, w_qkv, flat, large, depth)
    wo_full, wu_full, wd_full = [flat_rows(w) for w in outs[:3]]
    every, dense, kv, query, narrow_full, bu_full, attn, lse = outs[4:]
    output, dh1, d_attn, delta, lse, sums, d_up_bias, d_w_out, d_w_up, d_w_down = middle(
        tokens, attn, lse, cotangent, narrow_full, bu_full, wo_full, wu_full, wd_full
    )
    g_wout, g_wup, g_wdown, g_wqkv, row, token_sum, query_part = backward_kernel(
        query,
        kv,
        d_attn,
        lse,
        delta,
        every,
        dense,
        sums,
        d_up_bias,
        [d_w_out, d_w_up, d_w_down],
        large,
        depth,
    )
    d_tokens, g_wqkv, g_wout, g_wup, g_wdown, g_qv, g_gain, g_shift, g_bout, g_bdown, g_bup = finish(
        [g_wqkv, g_wout, g_wup, g_wdown], row, dh1, query_part, token_sum, own, span
    )
    g_bout, g_bdown, g_bup = g_bout[0], g_bdown[0], g_bup[0]
    return (
        output,
        d_tokens,
        g_wqkv,
        g_qv,
        g_wout,
        g_bout,
        g_gain,
        g_shift,
        g_wup,
        g_bup,
        g_wdown,
        g_bdown,
    )


def solution(mesh):
    return jax.shard_map(
        on_device,
        mesh=mesh,
        in_specs=(
            P(("dp", "blk"), None),
            P(("dp", "blk"), None),
            P(None, ("dp", "blk")),
            P(("dp", "blk"), None),
            P(("dp", "blk")),
            P(None, ("dp", "blk")),
            P(None, ("dp", "blk")),
            P(("dp", "blk"), None),
            P(("dp", "blk")),
            P(("dp", "blk"), None),
            P(("dp", "blk")),
            P(("dp", "blk"), None),
        ),
        out_specs=(
            P(("dp", "blk"), None),
            P(("dp", "blk"), None),
            P(("dp", "blk"), None),
            P(None, ("dp", "blk")),
            P(("dp", "blk"), None),
            P(("dp", "blk")),
            P(None, ("dp", "blk")),
            P(None, ("dp", "blk")),
            P(("dp", "blk"), None),
            P(("dp", "blk")),
            P(("dp", "blk"), None),
            P(("dp", "blk")),
        ),
        check_vma=False,
    )
```
